32 devices in a mesh: groups: 2 (over y), gx: 8 (over z, x), gy: 2 (over core).
Axes of the slice: x: 2, y: 2, z: 4, core: 2. Of those that a mesh axis runs over, the one named last changes fastest.
Arguments:
- voxels: bfloat16 [16, 128, 128, 64], P(('groups', 'gx'), 'gy'), parts along dimension 0, may hold values from -6 to 6
- occupancy: int32 [16, 128, 128], P(('groups', 'gx'), 'gy'), parts along dimension 0, may hold values 0 or 1
- row_weights: bfloat16 [8, 64], P('gx'), may hold values from -2 to 2
- column_weights: bfloat16 [128, 64], P('gy'), may hold values from -0.5 to 0.5
- depth_weights: bfloat16 [128, 64], replicated, may hold values from -0.5 to 0.5
- plane_kernels: bfloat16 [3, 2, 3, 3, 64, 64], replicated, may hold values from -0.25 to 0.25
- expand_weight: bfloat16 [64, 128], replicated, may hold values from -0.75 to 0.75
- shrink_weight: bfloat16 [128, 64], replicated, may hold values from -1 to 1
Outputs:
- updated: bfloat16 [16, 128, 128, 64], P(('groups', 'gx'), 'gy'), parts along dimension 0
The draws below stay inside these ranges and needn't reach their ends.
There are 2 independent parts, one for each index of `groups`. The reference program is written for one: setup_inputs(seed, part) draws one part's arguments, and reference() takes and returns one part's arrays. A program takes and returns all parts, laid end to end along the dimension named above; an argument that names none is the same for every part. Nothing has to cross between parts.
All inputs are finite; a program needn't handle non-finite values. No bound on the sum of `occupancy` on one device may be relied on, other than what follows from the above.
Results may differ from the reference program's by a relative error of at most 0.015.
Values may be sent and summed in bfloat16 or wider, within the bound.
A program may use at most 64 MiB of HBM per device.

```python
import jax
import jax.numpy as jnp
from jax import lax

C = 64
H = 128
Z = 128
X = 8
Y = 128


def set_ends(result, own_key, smallest, largest):
    longest = result.shape.index(max(result.shape))
    spots = []
    for shift in (0, 1):
        where = [jax.random.randint(jax.random.fold_in(own_key, axis), (), 0, length) for axis, length in enumerate(result.shape)]
        where[longest] = (where[longest] + shift) % result.shape[longest]
        spots.append(tuple(where))
    return result.at[spots[0]].set(smallest).at[spots[1]].set(largest)


def levels(stream_key, extent, shards, low, high):
    level = 1.0
    for position, blocks in shards:
        draws = jax.random.uniform(jax.random.fold_in(jax.random.fold_in(stream_key, 6), position), (blocks,), jnp.float32, low / len(shards), high / len(shards))
        level = level * jnp.repeat(jnp.exp(draws), extent[position] // blocks).reshape((-1,) + (1,) * (len(extent) - 1 - position))
    return level


def centred(key, shape, spread, limit, cuts=(), dtype=jnp.bfloat16):
    entries = jax.random.normal(key, shape, jnp.float32) * spread
    if len(cuts) > 0:
        entries = levels(key, shape, cuts, -0.22, 0.18) * entries
    return jnp.clip(entries, min=-limit, max=limit).astype(dtype)


def setup_inputs(seed: int = 0, part: int = 0) -> dict:
    streams_of = jax.random.split(jax.random.key(seed), 9)
    part_keys = jax.random.split(jax.random.fold_in(streams_of[8], part), 9)
    voxels = centred(part_keys[0], (X, Y, Z, C), 1.0, 6.0, ((0, 8), (1, 2)))
    occupancy = set_ends((jax.random.randint(part_keys[1], (X, Y, Z), 0, 2) < 1).astype(jnp.int32), jax.random.fold_in(part_keys[1], 1), 0, 1)
    row_weights = centred(streams_of[2], (X, C), X ** -0.5, 2.0, ((0, 8),))
    column_weights = centred(streams_of[3], (Y, C), Y ** -0.5, 0.5, ((0, 2),))
    depth_weights = centred(streams_of[4], (Z, C), Z ** -0.5, 0.5)
    plane_kernels = centred(streams_of[5], (3, 2, 3, 3, C, C), (9 * C) ** -0.5, 0.25)
    expand_weight = centred(streams_of[6], (C, H), C ** -0.5, 0.75)
    shrink_weight = centred(streams_of[7], (H, C), (H // 4) ** -0.5, 1.0)
    return {"voxels": voxels, "occupancy": occupancy, "row_weights": row_weights, "column_weights": column_weights, "depth_weights": depth_weights, "plane_kernels": plane_kernels, "expand_weight": expand_weight, "shrink_weight": shrink_weight}


product_scale = 8.0


def conv_same(plane, kernel):
    rows = plane.shape[0]
    cols = plane.shape[1]
    padded = jnp.pad(plane.astype(jnp.float32), ((1, 1), (1, 1), (0, 0)))
    total = jnp.zeros((rows, cols, kernel.shape[-1]), jnp.float32)
    for row_off in range(3):
        for col_off in range(3):
            window = padded[row_off:row_off + rows, col_off:col_off + cols]
            total = total + jnp.einsum("ijc,co->ijo", window, kernel[row_off, col_off].astype(jnp.float32))
    return total


def plane_block(plane, kernels):
    inner = jax.nn.silu(conv_same(plane, kernels[0])).astype(jnp.bfloat16)
    return conv_same(inner, kernels[1]).astype(jnp.bfloat16)


def reference(voxels, occupancy, row_weights, column_weights, depth_weights, plane_kernels, expand_weight, shrink_weight):
    features = voxels * occupancy.astype(jnp.bfloat16)[..., None]
    widened = features.astype(jnp.float32)
    xy_plane = jnp.einsum("xyzc,zc->xyc", widened, depth_weights.astype(jnp.float32)).astype(jnp.bfloat16)
    xz_plane = jnp.einsum("xyzc,yc->xzc", widened, column_weights.astype(jnp.float32)).astype(jnp.bfloat16)
    yz_plane = jnp.einsum("xyzc,xc->yzc", widened, row_weights.astype(jnp.float32)).astype(jnp.bfloat16)
    xy_out = plane_block(xy_plane, plane_kernels[0])
    xz_out = plane_block(xz_plane, plane_kernels[1])
    yz_out = plane_block(yz_plane, plane_kernels[2])
    expand_wide = expand_weight.astype(jnp.float32)
    shrink_wide = shrink_weight.astype(jnp.float32)

    def per_slice(items):
        feature_slice, xy_row, xz_row = items
        product = xy_row.astype(jnp.float32)[:, None, :] * xz_row.astype(jnp.float32)[None, :, :]
        product = product * yz_out.astype(jnp.float32)
        mixed = (product_scale * product).astype(jnp.bfloat16).astype(jnp.float32)
        hidden = jax.nn.silu(jnp.einsum("yzc,ch->yzh", mixed, expand_wide)).astype(jnp.bfloat16)
        branch = jnp.einsum("yzh,hc->yzc", hidden.astype(jnp.float32), shrink_wide)
        return (feature_slice.astype(jnp.float32) + branch).astype(jnp.bfloat16)

    return lax.map(per_slice, (features, xy_out, xz_out))
```

```python
import functools

import jax
import jax.numpy as jnp
from jax import lax
from jax.experimental import pallas as pl
from jax.experimental.pallas import tpu as pltpu
from jax.sharding import PartitionSpec as P

MESH = pl.DeviceIdType.MESH
reach = 2

product_scale = 8.0


def with_halo(cells, sides, width):
    for axis, dim in sides:
        count = lax.axis_size(axis)
        ends = count - 1
        head = lax.slice_in_dim(cells, 0, width, axis=dim)
        tail = lax.slice_in_dim(cells, cells.shape[dim] - width, cells.shape[dim], axis=dim)
        cells = jnp.concatenate(
            [
                lax.ppermute(tail, axis, [(i, (i + 1) % count) for i in range(ends)]),
                cells,
                lax.ppermute(head, axis, [((i + 1) % count, i) for i in range(ends)]),
            ],
            axis=dim,
        )
    return cells


def conv_valid(padded, kernel):
    rows = padded.shape[0] - 2
    cols = padded.shape[1] - 2
    total = jnp.zeros((rows, cols, kernel.shape[-1]), jnp.float32)
    for row_off in range(3):
        for col_off in range(3):
            window = padded[row_off : row_off + rows, col_off : col_off + cols]
            total = total + jnp.einsum(
                "ijc,co->ijo", window, kernel[row_off, col_off], preferred_element_type=jnp.float32
            )
    return total


def plane_block(plane, kernels, extend):
    inner = jax.nn.silu(conv_valid(extend(plane), kernels[0])).astype(jnp.bfloat16)
    return conv_valid(extend(inner), kernels[1]).astype(jnp.bfloat16)


def rim_xy(plane):
    return with_halo(plane, (("gx", 0), ("gy", 1)), 1)


def rim_xz(plane):
    padded = with_halo(plane, (("gx", 0),), 1)
    return jnp.pad(padded, ((0, 0), (1, 1), (0, 0)))


def rim_yz(plane):
    padded = with_halo(plane, (("gy", 0),), 1)
    return jnp.pad(padded, ((0, 0), (1, 1), (0, 0)))


def conv_row(window, weight):
    taps = jnp.dot(weight, window, preferred_element_type=jnp.float32)
    chans = taps.shape[0] // 3
    cols = taps.shape[1]
    lane = lax.broadcasted_iota(jnp.int32, (chans, cols), 1)
    left = pltpu.roll(taps[:chans], 1, 1)
    right = pltpu.roll(taps[2 * chans :], cols - 1, 1)
    left = jnp.where(lane == 0, 0.0, left)
    right = jnp.where(lane == cols - 1, 0.0, right)
    return taps[chans : 2 * chans] + left + right


def silu(v):
    half = 0.5 * v
    return half + half * jnp.tanh(half)


def identity(size):
    row = lax.broadcasted_iota(jnp.int32, (size, size), 0)
    col = lax.broadcasted_iota(jnp.int32, (size, size), 1)
    return jnp.where(row == col, 1.0, 0.0)


def flipped(x):
    eye = identity(x.shape[1]).astype(x.dtype)
    return lax.dot_general(eye, x, (((1,), (1,)), ((), ())), preferred_element_type=jnp.float32)


def column(x, at):
    lane = lax.broadcasted_iota(jnp.int32, x.shape, 1)
    return jnp.sum(jnp.where(lane == at, x, 0.0), axis=1, keepdims=True)


def pick(index, values):
    chosen = values[0]
    for i, value in enumerate(values):
        if i > 0 and value != values[0]:
            chosen = jnp.where(index == i, value, chosen)
    return chosen


def others(m, z):
    return [k for k in range(m) if k != z]


def joined(m, z, k):
    return z in (0, m - 1) and abs(k - z) == 2


def joins(m, z):
    found = []
    for end, step in ((0, 1), (m - 1, -1)):
        if z == end + step:
            found.append((end, z + step))
    return found


def sum_order(m, z):
    first = {k for _, k in joins(m, z)} | {k for k in others(m, z) if joined(m, z, k)}
    ks = sorted(others(m, z), key=lambda k: (k not in first, -abs(k - z)))
    rest = ks[1:]
    chunks = [(ks[0], 0), (ks[0], 1)] + [(k, 0) for k in rest] + [(k, 1) for k in rest] + [(z, 0), (z, 1)]
    return [2 * k + h for k, h in chunks]


def passed(m, z, k):
    return k in (0, m - 1) and abs(k - z) == 2


def give_order(m, z):
    return sorted(others(m, z), key=lambda k: -abs(k - z))


def take_order(m, z):
    direct = sorted([k for k in others(m, z) if not passed(m, k, z)], key=lambda k: (k in (0, m - 1), -abs(k - z)))
    late = [k for k in others(m, z) if passed(m, k, z)]
    ks = direct + late
    chunks = [(k, h) for k in ks[:2] for h in (1,)] + [(k, 0) for k in ks[:2]] + [(k, h) for k in ks[2:] for h in (1, 0)]
    return [2 * k + h for k, h in chunks]


def block_kernel(
    n, voxels_in, occupancy_in, row_weights_in, column_weights_in, depth_in, kernels_in, expand_in, shrink_in, updated,
    voxels, occupancy, row_weights, column_weights, depth_weights, plane_kernels, expand, shrink, load_s, fetch_s,
    part, rows_in, weights, wide, yz_out, row_sums, turned,
    pair_in, pair_sum, line_in, yz_sum, yz_plane, yz_inner,
    row_other, row_slots, row_plane, row_inner, outs,
    pair_s, pair_r, line_s, line_r, halo_s, halo_r, row_s, row_r, core_s, core_r, spread_s, spread_r, cross_s, cross_r, known,
):
    me = lax.axis_index("gx")
    g = lax.axis_index("gy")
    m = n // 2
    a = me // 2
    b = me % 2
    count, chans, cols = part.shape
    rows = count // n
    sub = 2 * reach
    bf = jnp.bfloat16
    f32 = jnp.float32
    partner = a * 2 + 1 - b

    def table(make):
        return [make(z) for z in range(m)]

    def feature_row(y):
        return voxels[y].astype(f32) * occupancy[pl.ds(y, 1), :].astype(f32)

    def piece(bb, aa):
        return bb * m + aa + bb * (m - 1 - 2 * aa)

    def owner(j):
        bb = j // m
        aa = j % m
        return (aa + bb * (m - 1 - 2 * aa)) * 2 + bb

    def offset(h, r):
        edge = r if r < reach else rows - sub + r
        if isinstance(h, int):
            return edge if h == 0 else reach + r
        return jnp.where(h == 0, edge, reach + r)

    def chunk(bb, q):
        return pl.ds(piece(bb, q // 2) * rows + (q % 2) * sub, sub)

    def remote(src, dst, send, recv, gx, gy=None):
        target = {"gx": gx} if gy is None else {"gx": gx, "gy": gy}
        return pltpu.make_async_remote_copy(
            src_ref=src, dst_ref=dst, send_sem=send, recv_sem=recv, device_id=target, device_id_type=MESH
        )

    place = g * n + piece(b, a)
    last = 2 * n - 1
    before = jnp.maximum(place - 1, 0)
    after = jnp.minimum(place + 1, last)

    barrier = pltpu.get_barrier_semaphore()

    def greet(gx, gy):
        pl.semaphore_signal(barrier, inc=1, device_id={"gx": gx, "gy": gy}, device_id_type=MESH)

    lower = a > 0
    upper = a < m - 1
    slant = jnp.where(b == 0, lower, upper)
    seam_low = place == n - 1
    seam_high = place == n
    greet(partner, g)
    greet(me, 1 - g)
    pl.when(lower)(lambda: greet(jnp.maximum(me - 2, 0), g))
    pl.when(upper)(lambda: greet(jnp.minimum(me + 2, n - 1), g))
    pl.when(slant)(lambda: greet(jnp.clip(me + 2 * b - 1, 0, n - 1), g))
    pl.when(seam_low)(lambda: greet(owner(0), 1 - g))
    pl.when(seam_high)(lambda: greet(owner(n - 1), 1 - g))
    greeters = (
        2 + lower.astype(jnp.int32) + upper.astype(jnp.int32) + slant.astype(jnp.int32)
        + seam_low.astype(jnp.int32) + seam_high.astype(jnp.int32)
    )

    order = table(lambda z: sum_order(m, z))
    turns = [pick(a, [o[i] for o in order]) for i in range(2 * m)]
    lanes = [pick(a, [sum_order(m, z)[i] // 2 for z in range(m)]) for i in (0, 2)]
    lanes += [pick(a, [sum_order(m, z)[2 + i] // 2 for z in range(m)]) for i in range(1, m - 2)]
    lanes = lanes + [a]

    small = [
        pltpu.make_async_copy(row_weights_in, row_weights, load_s.at[0]),
        pltpu.make_async_copy(occupancy_in, occupancy, load_s.at[1]),
    ]
    large = []
    for bb in (1 - b, b):
        for k in lanes:
            at = pl.ds(piece(bb, k) * rows, rows)
            large.append(pltpu.make_async_copy(voxels_in.at[at], voxels.at[at], load_s.at[2 + len(large)]))
    fetches = [
        pltpu.make_async_copy(kernels_in, plane_kernels, fetch_s.at[0]),
        pltpu.make_async_copy(column_weights_in, column_weights, fetch_s.at[1]),
        pltpu.make_async_copy(depth_in, depth_weights, fetch_s.at[2]),
        pltpu.make_async_copy(expand_in, expand, fetch_s.at[3]),
        pltpu.make_async_copy(shrink_in, shrink, fetch_s.at[4]),
    ]
    for copy in small + large + fetches:
        copy.start()

    for copy in small:
        copy.wait()
    rw = jnp.broadcast_to(row_weights[...].astype(f32), (chans, chans))
    rw = jnp.sum(rw * identity(chans), axis=1, keepdims=True)

    def yz_terms(j):
        for h in range(2):
            for r in range(sub):
                part[j * rows + h * sub + r] = (feature_row(j * rows + offset(h, r)) * rw).astype(bf)

    pair_copies = []
    for q in turns:
        pair_copies.append(remote(part.at[chunk(1 - b, q)], pair_in.at[q], pair_s.at[q], pair_r.at[q], partner))

    large[0].wait()
    yz_terms(piece(1 - b, lanes[0]))
    pl.semaphore_wait(barrier, greeters)
    pair_copies[0].start()
    pair_copies[1].start()
    for i in range(1, m - 1):
        large[i].wait()
        yz_terms(piece(1 - b, lanes[i]))
        pair_copies[1 + i].start()
    for i in range(1, m - 1):
        pair_copies[m - 1 + i].start()
    large[m - 1].wait()
    yz_terms(piece(1 - b, lanes[m - 1]))
    pair_copies[2 * m - 2].start()
    pair_copies[2 * m - 1].start()

    def tell(level, side):
        step = 2 if side == 0 else -2
        pl.semaphore_signal(
            known.at[level, side], inc=1, device_id={"gx": jnp.clip(me - step, 0, n - 1), "gy": g}, device_id_type=MESH
        )

    def heard(level, side):
        return (a + level <= m - 1) if side == 0 else (a - level >= 0)

    def tells(level, side):
        return (lower if side == 0 else upper) & heard(level - 1, side)

    def tell_level(level):
        for side in range(2):
            if level > 2:
                pl.when(heard(level - 1, side))(lambda: pl.semaphore_wait(known.at[level - 1, side], 1))
            if level < m:
                pl.when(tells(level, side))(lambda: tell(level, side))

    tell_level(2)

    for i in range(m):
        large[m + i].wait()
        yz_terms(piece(b, lanes[i]))

    for copy in fetches:
        copy.wait()
    turned[...] = flipped(column_weights[...])
    row_sums[...] = jnp.zeros(row_sums.shape, f32)
    lane = lax.broadcasted_iota(jnp.int32, (chans, cols), 1)

    group = 4
    share = count // (2 * m)

    def row_terms(first):
        depth = depth_weights[...].astype(f32)

        def some(step, carry):
            xy, xz = row_sums[0], row_sums[1]
            for k in range(group):
                y = first + step * group + k
                f = feature_row(y)
                xy = jnp.where(lane == g * count + y, jnp.sum(f * depth, axis=1, keepdims=True), xy)
                xz = xz + f * column(turned[...], y)
            row_sums[0] = xy
            row_sums[1] = xz
            return carry

        lax.fori_loop(0, share // group, some, 0)

    def flip_plane(p, layer):
        for off in range(3):
            taps = plane_kernels[p, layer, :, off].reshape(3 * chans, chans)
            weights[p, layer, off * chans : (off + 1) * chans, :] = flipped(taps).astype(bf)

    for level in range(3, m):
        tell_level(level)

    holds = table(lambda z: [k for _, k in joins(m, z)])
    held = pick(a, [ks[0] if ks else -1 for ks in holds])
    source = pick(a, [joins(m, z)[0][0] if joins(m, z) else -1 for z in range(m)])

    def line_target(i):
        k = turns[i] // 2
        gx = pick(a, [((z + (1 if order[z][i] // 2 > z else -1)) if joined(m, z, order[z][i] // 2) else order[z][i] // 2) for z in range(m)])
        slot = pick(a, [2 * (m if joined(m, z, order[z][i] // 2) else z) + order[z][i] % 2 for z in range(m)])
        return k, gx * 2 + b, slot

    line_copies = []
    for i in range(2 * m - 2):
        k, gx, slot = line_target(i)
        q = turns[i]
        line_copies.append(remote(pair_sum.at[q], line_in.at[slot], line_s.at[q], line_r.at[slot], gx))

    def reduce_pair(i):
        q = turns[i]
        pair_copies[i].wait_recv()
        mine = part[chunk(b, q)].astype(f32)
        pair_sum[q] = (mine + pair_in[q].astype(f32)).astype(bf)
        pl.when(q // 2 != held)(line_copies[i].start)

    def reduce_joined(h):
        @pl.when(held >= 0)
        def _():
            q = 2 * jnp.maximum(held, 0) + h
            slot = 2 * m + h
            remote(pair_sum.at[q], line_in.at[slot], line_s.at[q], line_r.at[slot], partner).wait_recv()
            pair_sum[q] = (pair_sum[q].astype(f32) + line_in[slot].astype(f32)).astype(bf)
            line_copies[h].start()

    def reduce_own(h):
        q = turns[2 * m - 2 + h]
        pair_copies[2 * m - 2 + h].wait_recv()
        yz_sum[h] = part[chunk(b, q)].astype(f32) + pair_in[q].astype(f32)

    def reduce_line(h):
        for i in range(m - 1):
            src = pick(a, [sorted(others(m, z), key=lambda s: (abs(s - z), s))[i] for z in range(m)])
            skip = pick(a, [int(joined(m, sorted(others(m, z), key=lambda s: (abs(s - z), s))[i], z)) for z in range(m)])

            @pl.when(skip == 0)
            def _():
                slot = 2 * src + h
                remote(pair_sum.at[slot], line_in.at[slot], line_s.at[slot], line_r.at[slot], partner).wait_recv()
                yz_sum[h] = yz_sum[h] + line_in[slot].astype(f32)

    row_terms(0)
    reduce_pair(0)
    row_terms(share)
    reduce_pair(1)
    tell_level(m)
    row_terms(2 * share)
    reduce_pair(2)
    wide[...] = flipped(expand[...]).astype(bf)
    flip_plane(2, 0)
    reduce_joined(0)
    for i in range(3, 2 * m - 2):
        row_terms(i * share)
        reduce_pair(i)
        if i == 3:
            flip_plane(2, 1)
            reduce_joined(1)
    for i in range(2 * m - 2, 2 * m):
        row_terms(i * share)
    rows_in[...] = row_sums[...].astype(bf)
    core = remote(rows_in.at[1 - g], row_other.at[...], core_s.at[0], core_r.at[0], me, 1 - g)
    core.start()
    for layer in range(2):
        flip_plane(g, layer)

    edge = reach * chans
    halo = [
        (place > 0, place < last, remote(
            yz_plane.at[pl.ds(edge, edge)], yz_plane.at[pl.ds(edge + rows * chans, edge)],
            halo_s.at[0], halo_r.at[0], owner(before % n), before // n,
        )),
        (place < last, place > 0, remote(
            yz_plane.at[pl.ds(rows * chans, edge)], yz_plane.at[pl.ds(0, edge)],
            halo_s.at[1], halo_r.at[1], owner(after % n), after // n,
        )),
    ]

    @pl.when(place == 0)
    def _():
        yz_plane[pl.ds(0, edge), :] = jnp.zeros((edge, cols), bf)

    @pl.when(place == last)
    def _():
        yz_plane[pl.ds(edge + rows * chans, edge), :] = jnp.zeros((edge, cols), bf)

    def settle(h):
        for r in range(sub):
            at = (reach + offset(h, r)) * chans
            yz_plane[at : at + chans, :] = yz_sum[h, r].astype(bf)

    reduce_own(0)
    core.wait_recv()
    mid = rows_in[g].astype(f32) + row_other[...].astype(f32)
    row_slots[reach] = mid.astype(bf)
    row_copies = []
    for dx in range(-reach, reach + 1):
        if dx != 0:
            slot = reach - dx
            copy = remote(
                row_slots.at[reach], row_slots.at[slot], row_s.at[slot], row_r.at[slot], jnp.clip(me + dx, 0, n - 1)
            )
            row_copies.append((dx, copy))
    reduce_line(0)
    settle(0)
    for sends, _, copy in halo:
        pl.when(sends)(copy.start)
    for dx, copy in row_copies:
        pl.when((me + dx >= 0) & (me + dx < n))(copy.start)
    reduce_own(1)
    reduce_line(1)
    settle(1)

    def inner_row(i, keep):
        inner = silu(conv_row(yz_plane[i * chans : (i + 3) * chans, :], weights[2, 0])) * keep
        yz_inner[i * chans : (i + 1) * chans, :] = inner.astype(bf)

    spread_copies = []
    own = piece(b, a)

    def give_chunk(h):
        for r in range(sub):
            at = offset(h, r) * chans
            done = conv_row(yz_inner[at : at + 3 * chans, :], weights[2, 1])
            yz_out[own * rows + h * sub + r] = done.astype(bf)
        q = 2 * a + h
        cross_copy(b, q).start()
        for i in range(m - 1):
            k = pick(a, [give_order(m, z)[i] for z in range(m)])
            skip = pick(a, [int(passed(m, z, give_order(m, z)[i])) for z in range(m)])
            at = chunk(b, q)
            copy = remote(yz_out.at[at], yz_out.at[at], spread_s.at[2 * i + h], spread_r.at[q], k * 2 + b)
            pl.when(skip == 0)(copy.start)
            spread_copies.append((skip == 0, copy))

    def cross_copy(bb, q):
        at = chunk(bb, q)
        return remote(yz_out.at[at], yz_out.at[at], cross_s.at[q], cross_r.at[q], partner)

    for i in range(reach, rows):
        inner_row(i, 1.0)
    give_chunk(1)
    for _, receives, copy in halo:
        pl.when(receives)(copy.wait_recv)
    for i in list(range(reach)) + list(range(rows, rows + 2)):
        keep = 1.0
        if i == 0:
            keep = (place > 0).astype(f32)
        if i == rows + 1:
            keep = (place < last).astype(f32)
        inner_row(i, keep)
    give_chunk(0)

    for dx, copy in row_copies:
        pl.when((me - dx >= 0) & (me - dx < n))(copy.wait_recv)
    for s in range(2 * reach + 1):
        at = me + s - reach
        inside = (at >= 0) & (at < n)
        here = pl.ds(s * chans, chans)

        @pl.when(inside)
        def _():
            row_plane[here, :] = row_slots[s]

        @pl.when(jnp.logical_not(inside))
        def _():
            row_plane[here, :] = jnp.zeros((chans, cols), bf)

    for s in range(3):
        at = me + s - 1
        keep = ((at >= 0) & (at < n)).astype(f32)
        inner = silu(conv_row(row_plane[s * chans : (s + 3) * chans, :], weights[g, 0]))
        row_inner[s * chans : (s + 1) * chans, :] = (inner * keep).astype(bf)
    outs[g] = conv_row(row_inner[...], weights[g, 1]).astype(bf)
    share_out = remote(outs.at[g], outs.at[g], core_s.at[1], core_r.at[1], me, 1 - g)
    share_out.start()
    remote(outs.at[1 - g], outs.at[1 - g], core_s.at[1], core_r.at[1], me, 1 - g).wait_recv()

    def finish(bb, q):
        j = piece(bb, q // 2)
        h = q % 2
        xy_out = outs[0].astype(f32)
        xz_out = outs[1].astype(f32)
        at = [(j * rows + h * sub + r, j * rows + offset(h, r)) for r in range(sub)]
        mixed = []
        for s, y in at:
            product = column(xy_out, g * count + y) * xz_out
            product = product * yz_out[s].astype(f32)
            mixed.append((product_scale * product).astype(bf))
        mixed = jnp.concatenate(mixed, axis=1)
        hidden = silu(jnp.dot(wide[...], mixed, preferred_element_type=f32)).astype(bf)
        branch = jnp.dot(shrink[...], hidden, preferred_element_type=f32)
        for k, (s, y) in enumerate(at):
            updated[y] = (feature_row(y) + branch[:, k * cols : (k + 1) * cols]).astype(bf)

    takes = [pick(a, [take_order(m, z)[i] for z in range(m)]) for i in range(2 * m - 2)]
    hands = table(lambda z: [k for k in others(m, z) if any(passed(m, k, t) and abs(z - t) == 1 for t in others(m, z))])
    handed = pick(a, [ks[0] if ks else -1 for ks in hands])
    onward = pick(a, [(0 if z == 1 else m - 1) if hands[z] else 0 for z in range(m)])

    def hand_copy(h):
        q = 2 * jnp.maximum(handed, 0) + h
        at = chunk(b, q)
        return remote(yz_out.at[at], yz_out.at[at], spread_s.at[2 * (m - 1) + h], spread_r.at[q], onward * 2 + b)

    def take(i):
        q = takes[i]
        at = chunk(b, q)
        remote(yz_out.at[at], yz_out.at[at], spread_s.at[0], spread_r.at[q], partner).wait_recv()
        cross_copy(b, q).start()
        for h in range(2):
            pl.when((handed >= 0) & (q == 2 * handed + h))(hand_copy(h).start)
        finish(b, q)

    crossed = [2 * a + 1, 2 * a] + takes

    def take_crossed(i):
        q = crossed[i]
        cross_copy(1 - b, q).wait_recv()
        finish(1 - b, q)

    finish(b, 2 * a + 1)
    finish(b, 2 * a)
    takes_done = 0
    crossed_done = 0
    for step in "tctcttctct" + "c" * 4:
        if step == "t":
            take(takes_done)
            takes_done += 1
        else:
            take_crossed(crossed_done)
            crossed_done += 1
    while takes_done < len(takes):
        take(takes_done)
        takes_done += 1
    while crossed_done < len(crossed):
        take_crossed(crossed_done)
        crossed_done += 1

    for copy in pair_copies:
        copy.wait_send()
    for copy in line_copies:
        copy.wait_send()
    for sends, _, copy in halo:
        pl.when(sends)(copy.wait_send)
    core.wait_send()
    share_out.wait_send()
    for dx, copy in row_copies:
        pl.when((me + dx >= 0) & (me + dx < n))(copy.wait_send)
    for sent, copy in spread_copies:
        pl.when(sent)(copy.wait_send)
    for h in range(2):
        pl.when(handed >= 0)(hand_copy(h).wait_send)
    for q in crossed:
        cross_copy(b, q).wait_send()


def fused(voxels, occupancy, row_weights, column_weights, depth_weights, plane_kernels, expand_weight, shrink_weight):
    n = lax.axis_size("gx")
    m = n // 2
    count, cols, chans = voxels.shape[1:]
    rows = count // n
    sub = 2 * reach
    sets, layers = plane_kernels.shape[:2]
    planes = 2
    span = 2 * reach + 1
    bf = jnp.bfloat16
    f32 = jnp.float32
    dma = pltpu.SemaphoreType.DMA
    operands = (
        voxels[0].transpose(0, 2, 1),
        occupancy[0],
        row_weights,
        column_weights,
        depth_weights.T,
        plane_kernels,
        expand_weight,
        shrink_weight.T,
    )
    updated = pl.pallas_call(
        functools.partial(block_kernel, n),
        out_shape=pltpu.VMEM((count, chans, cols), bf),
        in_specs=[pl.BlockSpec(memory_space=pl.ANY) for _ in operands],
        out_specs=pl.BlockSpec(memory_space=pltpu.VMEM),
        scratch_shapes=[pltpu.VMEM(x.shape, x.dtype) for x in operands]
        + [
            dma((2 + 2 * m,)),
            dma((5,)),
            pltpu.VMEM((count, chans, cols), bf),
            pltpu.VMEM((planes, chans, cols), bf),
            pltpu.VMEM((sets, layers, 3 * chans, 3 * chans), bf),
            pltpu.VMEM(expand_weight.shape[::-1], bf),
            pltpu.VMEM((count, chans, cols), bf),
            pltpu.VMEM((planes, chans, cols), f32),
            pltpu.VMEM((chans, count), f32),
            pltpu.VMEM((2 * m, sub, chans, cols), bf),
            pltpu.VMEM((2 * m, sub, chans, cols), bf),
            pltpu.VMEM((2 * m + 2, sub, chans, cols), bf),
            pltpu.VMEM((2, sub, chans, cols), f32),
            pltpu.VMEM(((rows + 4) * chans, cols), bf),
            pltpu.VMEM(((rows + 2) * chans, cols), bf),
            pltpu.VMEM((chans, cols), bf),
            pltpu.VMEM((span, chans, cols), bf),
            pltpu.VMEM((span * chans, cols), bf),
            pltpu.VMEM((3 * chans, cols), bf),
            pltpu.VMEM((planes, chans, cols), bf),
            dma((2 * m,)), dma((2 * m,)), dma((2 * m,)), dma((2 * m + 2,)), dma((2,)), dma((2,)),
            dma((span,)), dma((span,)), dma((2,)), dma((2,)),
            dma((2 * m,)), dma((2 * m,)), dma((2 * m,)), dma((2 * m,)),
            pltpu.SemaphoreType.REGULAR((m, 2)),
        ],
        compiler_params=pltpu.CompilerParams(collective_id=0, has_side_effects=True),
    )(*operands)
    return updated.transpose(0, 2, 1)[None]


def fits(voxels):
    n = lax.axis_size("gx")
    sides = lax.axis_size("gy")
    xs, ys, zs, _ = voxels.shape
    return xs == 1 and sides == 2 and n % 2 == 0 and n >= 8 and ys == n * 4 * reach and 2 * ys == zs


def plain_planes(features, row_weights, column_weights, depth_weights, plane_kernels):
    xy_plane = jnp.einsum(
        "xyzc,zc->xyc", features, depth_weights, preferred_element_type=jnp.float32
    ).astype(jnp.bfloat16)
    xz_part = jnp.einsum(
        "xyzc,yc->xzc", features, column_weights, preferred_element_type=jnp.float32
    )
    yz_part = jnp.einsum("xyzc,xc->yzc", features, row_weights, preferred_element_type=jnp.float32)
    xy_out = plane_block(xy_plane, plane_kernels[0], rim_xy)
    xz_plane = lax.psum(xz_part, "gy").astype(jnp.bfloat16)
    xz_out = plane_block(xz_plane, plane_kernels[1], rim_xz)
    yz_plane = lax.psum(yz_part, "gx").astype(jnp.bfloat16)
    yz_out = plane_block(yz_plane, plane_kernels[2], rim_yz)
    return xy_out, xz_out, yz_out


def shards(
    voxels,
    occupancy,
    row_weights,
    column_weights,
    depth_weights,
    plane_kernels,
    expand_weight,
    shrink_weight,
):
    if fits(voxels):
        return fused(
            voxels,
            occupancy,
            row_weights,
            column_weights,
            depth_weights,
            plane_kernels,
            expand_weight,
            shrink_weight,
        )
    features = voxels * occupancy.astype(jnp.bfloat16)[..., None]
    xy_out, xz_out, yz_out = plain_planes(features, row_weights, column_weights, depth_weights, plane_kernels)
    product = xy_out.astype(jnp.float32)[:, :, None, :] * xz_out.astype(jnp.float32)[:, None, :, :]
    product = product * yz_out.astype(jnp.float32)[None, :, :, :]
    mixed = (product_scale * product).astype(jnp.bfloat16)
    hidden = jax.nn.silu(
        jnp.einsum("xyzc,ch->xyzh", mixed, expand_weight, preferred_element_type=jnp.float32)
    ).astype(jnp.bfloat16)
    branch = jnp.einsum("xyzh,hc->xyzc", hidden, shrink_weight, preferred_element_type=jnp.float32)
    return (features.astype(jnp.float32) + branch).astype(jnp.bfloat16)


def solution(mesh):
    in_specs = (
        P(("groups", "gx"), "gy", None, None),
        P(("groups", "gx"), "gy", None),
        P("gx", None),
        P("gy", None),
        P(),
        P(),
        P(),
        P(),
    )
    out_specs = P(("groups", "gx"), "gy", None, None)
    return jax.shard_map(shards, mesh=mesh, in_specs=in_specs, out_specs=out_specs, check_vma=False)
```

```python
import functools

import jax
import jax.numpy as jnp
from jax import lax
from jax.experimental import pallas as pl
from jax.experimental.pallas import tpu as pltpu
from jax.sharding import PartitionSpec as P

MESH = pl.DeviceIdType.MESH
reach = 2

product_scale = 8.0


def with_halo(cells, sides, width):
    for axis, dim in sides:
        count = lax.axis_size(axis)
        ends = count - 1
        head = lax.slice_in_dim(cells, 0, width, axis=dim)
        tail = lax.slice_in_dim(cells, cells.shape[dim] - width, cells.shape[dim], axis=dim)
        cells = jnp.concatenate(
            [
                lax.ppermute(tail, axis, [(i, (i + 1) % count) for i in range(ends)]),
                cells,
                lax.ppermute(head, axis, [((i + 1) % count, i) for i in range(ends)]),
            ],
            axis=dim,
        )
    return cells


def conv_valid(padded, kernel):
    rows = padded.shape[0] - 2
    cols = padded.shape[1] - 2
    total = jnp.zeros((rows, cols, kernel.shape[-1]), jnp.float32)
    for row_off in range(3):
        for col_off in range(3):
            window = padded[row_off : row_off + rows, col_off : col_off + cols]
            total = total + jnp.einsum(
                "ijc,co->ijo", window, kernel[row_off, col_off], preferred_element_type=jnp.float32
            )
    return total


def plane_block(plane, kernels, extend):
    inner = jax.nn.silu(conv_valid(extend(plane), kernels[0])).astype(jnp.bfloat16)
    return conv_valid(extend(inner), kernels[1]).astype(jnp.bfloat16)


def rim_xy(plane):
    return with_halo(plane, (("gx", 0), ("gy", 1)), 1)


def rim_xz(plane):
    padded = with_halo(plane, (("gx", 0),), 1)
    return jnp.pad(padded, ((0, 0), (1, 1), (0, 0)))


def rim_yz(plane):
    padded = with_halo(plane, (("gy", 0),), 1)
    return jnp.pad(padded, ((0, 0), (1, 1), (0, 0)))


def conv_row(window, weight):
    taps = jnp.dot(weight, window, preferred_element_type=jnp.float32)
    chans = taps.shape[0] // 3
    cols = taps.shape[1]
    lane = lax.broadcasted_iota(jnp.int32, (chans, cols), 1)
    left = pltpu.roll(taps[:chans], 1, 1)
    right = pltpu.roll(taps[2 * chans :], cols - 1, 1)
    left = jnp.where(lane == 0, 0.0, left)
    right = jnp.where(lane == cols - 1, 0.0, right)
    return taps[chans : 2 * chans] + left + right


def silu(v):
    half = 0.5 * v
    return half + half * jnp.tanh(half)


def identity(size):
    row = lax.broadcasted_iota(jnp.int32, (size, size), 0)
    col = lax.broadcasted_iota(jnp.int32, (size, size), 1)
    return jnp.where(row == col, 1.0, 0.0)


def flipped(x):
    eye = identity(x.shape[1]).astype(x.dtype)
    return lax.dot_general(eye, x, (((1,), (1,)), ((), ())), preferred_element_type=jnp.float32)


def column(x, at):
    lane = lax.broadcasted_iota(jnp.int32, x.shape, 1)
    return jnp.sum(jnp.where(lane == at, x, 0.0), axis=1, keepdims=True)


def pick(index, values):
    chosen = values[0]
    for i, value in enumerate(values):
        if i > 0 and value != values[0]:
            chosen = jnp.where(index == i, value, chosen)
    return chosen


def others(m, z):
    return [k for k in range(m) if k != z]


def joined(m, z, k):
    return z in (0, m - 1) and abs(k - z) > 1


def joins(m, z):
    if z == 1:
        return [(0, k) for k in range(m - 1, 1, -1)]
    if z == m - 2:
        return [(m - 1, k) for k in range(m - 2)]
    return []


def sum_order(m, z):
    far = sorted(others(m, z), key=lambda k: -abs(k - z))
    held = [k for _, k in joins(m, z)]
    first = [k for k in far if k in held or joined(m, z, k)]
    rest = [k for k in far if k not in first]
    ks = [(k, c) for c in range(3) for k in first] + [(k, c) for c in range(3) for k in rest + [z]]
    ks = [kc for kc in ks if kc[0] != z] + [kc for kc in ks if kc[0] == z]
    return [4 * k + c for k, c in ks]


def passed(m, z, k):
    return k in (0, m - 1) and abs(k - z) == 2


def give_order(m, z):
    return sorted(others(m, z), key=lambda k: -abs(k - z))


def take_order(m, z):
    direct = sorted([k for k in others(m, z) if not passed(m, k, z)], key=lambda k: (k in (0, m - 1), -abs(k - z)))
    late = [k for k in others(m, z) if passed(m, k, z)]
    ks = direct + late
    chunks = [(k, h) for k in ks[:2] for h in (1,)] + [(k, 0) for k in ks[:2]] + [(k, h) for k in ks[2:] for h in (1, 0)]
    return [2 * k + h for k, h in chunks]


def block_kernel(
    n, voxels_in, occupancy_in, row_weights_in, column_weights_in, depth_in, kernels_in, expand_in, shrink_in, updated,
    voxels, occupancy, row_weights, column_weights, depth_weights, plane_kernels, expand, shrink, load_s, fetch_s,
    part, rows_in, weights, wide, yz_out, row_sums, turned,
    pair_in, pair_sum, line_in, slab_in, slab_sum, yz_sum, yz_plane, yz_inner,
    row_other, row_slots, row_plane, row_inner, outs,
    pair_s, pair_r, line_s, line_r, slab_s, slab_r, halo_s, halo_r, row_s, row_r, core_s, core_r, spread_s, spread_r, cross_s, cross_r, known,
):
    me = lax.axis_index("gx")
    g = lax.axis_index("gy")
    m = n // 2
    a = me // 2
    b = me % 2
    count, chans, cols = part.shape
    rows = count // n
    sub = 2 * reach
    bf = jnp.bfloat16
    f32 = jnp.float32
    partner = a * 2 + 1 - b

    def table(make):
        return [make(z) for z in range(m)]

    def feature_row(y):
        return voxels[y].astype(f32) * occupancy[pl.ds(y, 1), :].astype(f32)

    def piece(bb, aa):
        return bb * m + aa + bb * (m - 1 - 2 * aa)

    def owner(j):
        bb = j // m
        aa = j % m
        return (aa + bb * (m - 1 - 2 * aa)) * 2 + bb

    def offset(h, r):
        edge = r if r < reach else rows - sub + r
        if isinstance(h, int):
            return edge if h == 0 else reach + r
        return jnp.where(h == 0, edge, reach + r)

    def chunk(bb, q):
        return pl.ds(piece(bb, q // 2) * rows + (q % 2) * sub, sub)

    def slice_of(bb, q):
        return pl.ds(piece(bb, q // 4) * rows + (q % 4) * reach, reach)

    def remote(src, dst, send, recv, gx, gy=None):
        target = {"gx": gx} if gy is None else {"gx": gx, "gy": gy}
        return pltpu.make_async_remote_copy(
            src_ref=src, dst_ref=dst, send_sem=send, recv_sem=recv, device_id=target, device_id_type=MESH
        )

    place = g * n + piece(b, a)
    last = 2 * n - 1
    before = jnp.maximum(place - 1, 0)
    after = jnp.minimum(place + 1, last)

    barrier = pltpu.get_barrier_semaphore()

    def greet(gx, gy):
        pl.semaphore_signal(barrier, inc=1, device_id={"gx": gx, "gy": gy}, device_id_type=MESH)

    lower = a > 0
    upper = a < m - 1
    slant = jnp.where(b == 0, lower, upper)
    seam_low = place == n - 1
    seam_high = place == n
    greet(partner, g)
    greet(me, 1 - g)
    pl.when(lower)(lambda: greet(jnp.maximum(me - 2, 0), g))
    pl.when(upper)(lambda: greet(jnp.minimum(me + 2, n - 1), g))
    pl.when(slant)(lambda: greet(jnp.clip(me + 2 * b - 1, 0, n - 1), g))
    pl.when(seam_low)(lambda: greet(owner(0), 1 - g))
    pl.when(seam_high)(lambda: greet(owner(n - 1), 1 - g))
    greeters = (
        2 + lower.astype(jnp.int32) + upper.astype(jnp.int32) + slant.astype(jnp.int32)
        + seam_low.astype(jnp.int32) + seam_high.astype(jnp.int32)
    )

    order = table(lambda z: sum_order(m, z))
    steps = 3 * m
    turns = [pick(a, [o[i] for o in order]) for i in range(steps)]

    small = [
        pltpu.make_async_copy(row_weights_in, row_weights, load_s.at[0]),
        pltpu.make_async_copy(occupancy_in, occupancy, load_s.at[1]),
    ]
    large = []
    for j in range(n):
        at = pl.ds(j * rows, rows)
        large.append(pltpu.make_async_copy(voxels_in.at[at], voxels.at[at], load_s.at[2 + j]))
    fetches = [
        pltpu.make_async_copy(kernels_in, plane_kernels, fetch_s.at[0]),
        pltpu.make_async_copy(column_weights_in, column_weights, fetch_s.at[1]),
        pltpu.make_async_copy(depth_in, depth_weights, fetch_s.at[2]),
        pltpu.make_async_copy(expand_in, expand, fetch_s.at[3]),
        pltpu.make_async_copy(shrink_in, shrink, fetch_s.at[4]),
    ]
    for copy in small + large + fetches:
        copy.start()

    for copy in small:
        copy.wait()
    rw = jnp.broadcast_to(row_weights[...].astype(f32), (chans, chans))
    rw = jnp.sum(rw * identity(chans), axis=1, keepdims=True)

    def yz_terms(j):
        for h in range(2):
            for r in range(sub):
                part[j * rows + h * sub + r] = (feature_row(j * rows + offset(h, r)) * rw).astype(bf)

    pair_copies = []
    for q in turns:
        pair_copies.append(remote(part.at[slice_of(1 - b, q)], pair_in.at[q], pair_s.at[q], pair_r.at[q], partner))

    def yz_pieces(j, carry):
        yz_terms(j)
        return carry

    for copy in large:
        copy.wait()
    lax.fori_loop(0, n, yz_pieces, 0)

    slab_copies = []
    for dist in range(1, m):
        for side in (-1, 1):
            k = jnp.clip(a + side * dist, 0, m - 1)
            there = (a + side * dist >= 0) & (a + side * dist < m)
            for bb in range(2):
                at = 2 * (dist + (m - 1 if side > 0 else 0) - 1) + bb
                copy = remote(
                    part.at[slice_of(bb, 4 * k + 3)], slab_in.at[2 * a + bb], slab_s.at[at], slab_r.at[2 * a + bb], k * 2 + b
                )
                slab_copies.append((dist, there, copy))

    def start_slabs(dist):
        for d, there, copy in slab_copies:
            if d == dist:
                pl.when(there)(copy.start)

    pl.semaphore_wait(barrier, greeters)
    for copy in pair_copies:
        copy.start()
    start_slabs(1)

    def tell(level, side):
        step = 2 if side == 0 else -2
        pl.semaphore_signal(
            known.at[level, side], inc=1, device_id={"gx": jnp.clip(me - step, 0, n - 1), "gy": g}, device_id_type=MESH
        )

    def heard(level, side):
        return (a + level <= m - 1) if side == 0 else (a - level >= 0)

    def tells(level, side):
        return (lower if side == 0 else upper) & heard(level - 1, side)

    def tell_level(level):
        for side in range(2):
            if level > 2:
                pl.when(heard(level - 1, side))(lambda: pl.semaphore_wait(known.at[level - 1, side], 1))
            if level < m:
                pl.when(tells(level, side))(lambda: tell(level, side))

    tell_level(2)

    for copy in fetches:
        copy.wait()
    turned[...] = flipped(column_weights[...])
    row_sums[...] = jnp.zeros(row_sums.shape, f32)
    lane = lax.broadcasted_iota(jnp.int32, (chans, cols), 1)

    group = 4
    share = count // (2 * m)

    def row_terms(first):
        depth = depth_weights[...].astype(f32)

        def some(step, carry):
            xy, xz = row_sums[0], row_sums[1]
            for k in range(group):
                y = first + step * group + k
                f = feature_row(y)
                xy = jnp.where(lane == g * count + y, jnp.sum(f * depth, axis=1, keepdims=True), xy)
                xz = xz + f * column(turned[...], y)
            row_sums[0] = xy
            row_sums[1] = xz
            return carry

        lax.fori_loop(0, share // group, some, 0)

    def flip_plane(p, layer):
        for off in range(3):
            taps = plane_kernels[p, layer, :, off].reshape(3 * chans, chans)
            weights[p, layer, off * chans : (off + 1) * chans, :] = flipped(taps).astype(bf)

    holds = table(lambda z: [k for _, k in joins(m, z)])
    holding = (a == 1) | (a == m - 2)

    def line_copy(i):
        gx, slot = [], []
        for z in range(m):
            k, c = order[z][i] // 4, order[z][i] % 4
            if k == z:
                gx.append(z)
                slot.append(0)
            elif joined(m, z, k):
                via = z + (1 if k > z else -1)
                gx.append(via)
                slot.append(4 * m + 4 * holds[via].index(k) + c)
            else:
                gx.append(k)
                slot.append(4 * z + c)
        to = pick(a, slot)
        q = turns[i]
        return remote(pair_sum.at[q], line_in.at[to], line_s.at[q], line_r.at[to], pick(a, gx) * 2 + b)

    line_copies = [line_copy(i) for i in range(steps - 3)]
    held = [pick(a, [int(order[z][i] // 4 in holds[z]) for z in range(m)]) for i in range(steps - 3)]

    def reduce_pair(i):
        q = turns[i]
        pair_copies[i].wait_recv()
        mine = part[slice_of(b, q)].astype(f32)
        pair_sum[q] = (mine + pair_in[q].astype(f32)).astype(bf)
        pl.when(held[i] == 0)(line_copies[i].start)

    def reduce_joined(i):
        @pl.when(holding)
        def _():
            q = turns[i]
            slot = 4 * m + pick(a, [4 * (holds[z].index(order[z][i] // 4) if holds[z] else 0) + order[z][i] % 4 for z in range(m)])
            remote(pair_sum.at[q], line_in.at[slot], line_s.at[q], line_r.at[slot], partner).wait_recv()
            pair_sum[q] = (pair_sum[q].astype(f32) + line_in[slot].astype(f32)).astype(bf)
            line_copies[i].start()

    def reduce_own(c):
        pair_copies[steps - 3 + c].wait_recv()
        q = 4 * a + c
        yz_sum[c] = part[slice_of(b, q)].astype(f32) + pair_in[q].astype(f32)

    def reduce_line(c):
        for i in range(m - 1):
            sources = [sorted(others(m, z), key=lambda s: (abs(s - z), s))[i] for z in range(m)]
            src = pick(a, sources)
            skip = pick(a, [int(joined(m, s, z)) for z, s in enumerate(sources)])

            @pl.when(skip == 0)
            def _():
                slot = 4 * src + c
                remote(pair_sum.at[slot], line_in.at[slot], line_s.at[slot], line_r.at[slot], partner).wait_recv()
                yz_sum[c] = yz_sum[c] + line_in[slot].astype(f32)

    slab_cross = remote(slab_sum, pair_in.at[4 * a + 3], pair_s.at[4 * a + 3], pair_r.at[4 * a + 3], partner)

    def reduce_slab():
        q = 4 * a + 3
        total = [part[slice_of(bb, q)].astype(f32) for bb in (1 - b, b)]
        for i in range(m - 1):
            src = pick(a, [others(m, z)[i] for z in range(m)])
            for side, bb in enumerate((1 - b, b)):
                slot = 2 * src + bb
                remote(slab_in.at[slot], slab_in.at[slot], slab_s.at[slot], slab_r.at[slot], partner).wait_recv()
                total[side] = total[side] + slab_in[slot].astype(f32)
        slab_sum[...] = total[0].astype(bf)
        slab_cross.start()
        yz_sum[3] = total[1]

    def reduce_slab_own():
        slab_cross.wait_recv()
        yz_sum[3] = yz_sum[3] + pair_in[4 * a + 3].astype(f32)

    for i in range(m):
        row_terms(i * share)
    for level in range(3, m + 1):
        tell_level(level)
        start_slabs(level - 1)
    for i in range(m, 2 * m):
        row_terms(i * share)
    rows_in[...] = row_sums[...].astype(bf)
    core = remote(rows_in.at[1 - g], row_other.at[...], core_s.at[0], core_r.at[0], me, 1 - g)
    core.start()
    flip_plane(2, 0)
    flip_plane(2, 1)

    first = 5
    for i in range(first):
        reduce_pair(i)
    merges = 3 * (m - 2)
    slab_at = steps - 3 - 1
    done = 0
    for i in range(first, steps - 3):
        if done < merges:
            reduce_joined(done)
            done += 1
        reduce_pair(i)
    reduce_slab()
    core.wait_recv()
    mid = rows_in[g].astype(f32) + row_other[...].astype(f32)
    row_slots[reach] = mid.astype(bf)
    row_copies = []
    for dx in range(-reach, reach + 1):
        if dx != 0:
            slot = reach - dx
            copy = remote(
                row_slots.at[reach], row_slots.at[slot], row_s.at[slot], row_r.at[slot], jnp.clip(me + dx, 0, n - 1)
            )
            row_copies.append((dx, copy))
            pl.when((me + dx >= 0) & (me + dx < n))(copy.start)
    while done < merges:
        reduce_joined(done)
        done += 1
    for layer in range(2):
        flip_plane(g, layer)
    wide[...] = flipped(expand[...]).astype(bf)

    edge = reach * chans
    halo = [
        (place > 0, place < last, remote(
            yz_plane.at[pl.ds(edge, edge)], yz_plane.at[pl.ds(edge + rows * chans, edge)],
            halo_s.at[0], halo_r.at[0], owner(before % n), before // n,
        )),
        (place < last, place > 0, remote(
            yz_plane.at[pl.ds(rows * chans, edge)], yz_plane.at[pl.ds(0, edge)],
            halo_s.at[1], halo_r.at[1], owner(after % n), after // n,
        )),
    ]

    @pl.when(place == 0)
    def _():
        yz_plane[pl.ds(0, edge), :] = jnp.zeros((edge, cols), bf)

    @pl.when(place == last)
    def _():
        yz_plane[pl.ds(edge + rows * chans, edge), :] = jnp.zeros((edge, cols), bf)

    def settle(c):
        for i in range(reach):
            h, r = c // 2, (c % 2) * reach + i
            at = (reach + offset(h, r)) * chans
            yz_plane[at : at + chans, :] = yz_sum[c, i].astype(bf)

    for c in range(2):
        reduce_own(c)
    for c in range(2):
        reduce_line(c)
        settle(c)
    for sends, _, copy in halo:
        pl.when(sends)(copy.start)
    reduce_own(2)
    reduce_line(2)
    settle(2)
    reduce_slab_own()
    settle(3)

    def inner_row(i, keep):
        inner = silu(conv_row(yz_plane[i * chans : (i + 3) * chans, :], weights[2, 0])) * keep
        yz_inner[i * chans : (i + 1) * chans, :] = inner.astype(bf)

    spread_copies = []
    own = piece(b, a)

    def give_chunk(h):
        for r in range(sub):
            at = offset(h, r) * chans
            done = conv_row(yz_inner[at : at + 3 * chans, :], weights[2, 1])
            yz_out[own * rows + h * sub + r] = done.astype(bf)
        q = 2 * a + h
        cross_copy(b, q).start()
        for i in range(m - 1):
            k = pick(a, [give_order(m, z)[i] for z in range(m)])
            skip = pick(a, [int(passed(m, z, give_order(m, z)[i])) for z in range(m)])
            at = chunk(b, q)
            copy = remote(yz_out.at[at], yz_out.at[at], spread_s.at[2 * i + h], spread_r.at[q], k * 2 + b)
            pl.when(skip == 0)(copy.start)
            spread_copies.append((skip == 0, copy))

    def cross_copy(bb, q):
        at = chunk(bb, q)
        return remote(yz_out.at[at], yz_out.at[at], cross_s.at[q], cross_r.at[q], partner)

    for i in range(reach, rows):
        inner_row(i, 1.0)
    give_chunk(1)
    for _, receives, copy in halo:
        pl.when(receives)(copy.wait_recv)
    for i in list(range(reach)) + list(range(rows, rows + 2)):
        keep = 1.0
        if i == 0:
            keep = (place > 0).astype(f32)
        if i == rows + 1:
            keep = (place < last).astype(f32)
        inner_row(i, keep)
    give_chunk(0)

    for dx, copy in row_copies:
        pl.when((me - dx >= 0) & (me - dx < n))(copy.wait_recv)
    for s in range(2 * reach + 1):
        at = me + s - reach
        inside = (at >= 0) & (at < n)
        here = pl.ds(s * chans, chans)

        @pl.when(inside)
        def _():
            row_plane[here, :] = row_slots[s]

        @pl.when(jnp.logical_not(inside))
        def _():
            row_plane[here, :] = jnp.zeros((chans, cols), bf)

    for s in range(3):
        at = me + s - 1
        keep = ((at >= 0) & (at < n)).astype(f32)
        inner = silu(conv_row(row_plane[s * chans : (s + 3) * chans, :], weights[g, 0]))
        row_inner[s * chans : (s + 1) * chans, :] = (inner * keep).astype(bf)
    outs[g] = conv_row(row_inner[...], weights[g, 1]).astype(bf)
    share_out = remote(outs.at[g], outs.at[g], core_s.at[1], core_r.at[1], me, 1 - g)
    share_out.start()
    remote(outs.at[1 - g], outs.at[1 - g], core_s.at[1], core_r.at[1], me, 1 - g).wait_recv()

    def finish(bb, q):
        j = piece(bb, q // 2)
        h = q % 2
        xy_out = outs[0].astype(f32)
        xz_out = outs[1].astype(f32)
        at = [(j * rows + h * sub + r, j * rows + offset(h, r)) for r in range(sub)]
        mixed = []
        for s, y in at:
            product = column(xy_out, g * count + y) * xz_out
            product = product * yz_out[s].astype(f32)
            mixed.append((product_scale * product).astype(bf))
        mixed = jnp.concatenate(mixed, axis=1)
        hidden = silu(jnp.dot(wide[...], mixed, preferred_element_type=f32)).astype(bf)
        branch = jnp.dot(shrink[...], hidden, preferred_element_type=f32)
        for k, (s, y) in enumerate(at):
            updated[y] = (feature_row(y) + branch[:, k * cols : (k + 1) * cols]).astype(bf)

    takes = [pick(a, [take_order(m, z)[i] for z in range(m)]) for i in range(2 * m - 2)]
    hands = table(lambda z: [k for k in others(m, z) if any(passed(m, k, t) and abs(z - t) == 1 for t in others(m, z))])
    handed = pick(a, [ks[0] if ks else -1 for ks in hands])
    onward = pick(a, [(0 if z == 1 else m - 1) if hands[z] else 0 for z in range(m)])

    def hand_copy(h):
        q = 2 * jnp.maximum(handed, 0) + h
        at = chunk(b, q)
        return remote(yz_out.at[at], yz_out.at[at], spread_s.at[2 * (m - 1) + h], spread_r.at[q], onward * 2 + b)

    def take(i):
        q = takes[i]
        at = chunk(b, q)
        remote(yz_out.at[at], yz_out.at[at], spread_s.at[0], spread_r.at[q], partner).wait_recv()
        cross_copy(b, q).start()
        for h in range(2):
            pl.when((handed >= 0) & (q == 2 * handed + h))(hand_copy(h).start)
        finish(b, q)

    crossed = [2 * a + 1, 2 * a] + takes

    def take_crossed(i):
        q = crossed[i]
        cross_copy(1 - b, q).wait_recv()
        finish(1 - b, q)

    finish(b, 2 * a + 1)
    finish(b, 2 * a)
    takes_done = 0
    crossed_done = 0
    for step in "tctcttctct" + "c" * 4:
        if step == "t":
            take(takes_done)
            takes_done += 1
        else:
            take_crossed(crossed_done)
            crossed_done += 1
    while takes_done < len(takes):
        take(takes_done)
        takes_done += 1
    while crossed_done < len(crossed):
        take_crossed(crossed_done)
        crossed_done += 1

    for copy in pair_copies:
        copy.wait_send()
    slab_cross.wait_send()
    for copy in line_copies:
        copy.wait_send()
    for _, there, copy in slab_copies:
        pl.when(there)(copy.wait_send)
    for sends, _, copy in halo:
        pl.when(sends)(copy.wait_send)
    core.wait_send()
    share_out.wait_send()
    for dx, copy in row_copies:
        pl.when((me + dx >= 0) & (me + dx < n))(copy.wait_send)
    for sent, copy in spread_copies:
        pl.when(sent)(copy.wait_send)
    for h in range(2):
        pl.when(handed >= 0)(hand_copy(h).wait_send)
    for q in crossed:
        cross_copy(b, q).wait_send()


def fused(voxels, occupancy, row_weights, column_weights, depth_weights, plane_kernels, expand_weight, shrink_weight):
    n = lax.axis_size("gx")
    m = n // 2
    count, cols, chans = voxels.shape[1:]
    rows = count // n
    sub = 2 * reach
    sets, layers = plane_kernels.shape[:2]
    planes = 2
    span = 2 * reach + 1
    bf = jnp.bfloat16
    f32 = jnp.float32
    dma = pltpu.SemaphoreType.DMA
    operands = (
        voxels[0].transpose(0, 2, 1),
        occupancy[0],
        row_weights,
        column_weights,
        depth_weights.T,
        plane_kernels,
        expand_weight,
        shrink_weight.T,
    )
    updated = pl.pallas_call(
        functools.partial(block_kernel, n),
        out_shape=pltpu.VMEM((count, chans, cols), bf),
        in_specs=[pl.BlockSpec(memory_space=pl.ANY) for _ in operands],
        out_specs=pl.BlockSpec(memory_space=pltpu.VMEM),
        scratch_shapes=[pltpu.VMEM(x.shape, x.dtype) for x in operands]
        + [
            dma((2 + n,)),
            dma((5,)),
            pltpu.VMEM((count, chans, cols), bf),
            pltpu.VMEM((planes, chans, cols), bf),
            pltpu.VMEM((sets, layers, 3 * chans, 3 * chans), bf),
            pltpu.VMEM(expand_weight.shape[::-1], bf),
            pltpu.VMEM((count, chans, cols), bf),
            pltpu.VMEM((planes, chans, cols), f32),
            pltpu.VMEM((chans, count), f32),
            pltpu.VMEM((4 * m, reach, chans, cols), bf),
            pltpu.VMEM((4 * m, reach, chans, cols), bf),
            pltpu.VMEM((8 * m, reach, chans, cols), bf),
            pltpu.VMEM((2 * m, reach, chans, cols), bf),
            pltpu.VMEM((reach, chans, cols), bf),
            pltpu.VMEM((4, reach, chans, cols), f32),
            pltpu.VMEM(((rows + 4) * chans, cols), bf),
            pltpu.VMEM(((rows + 2) * chans, cols), bf),
            pltpu.VMEM((chans, cols), bf),
            pltpu.VMEM((span, chans, cols), bf),
            pltpu.VMEM((span * chans, cols), bf),
            pltpu.VMEM((3 * chans, cols), bf),
            pltpu.VMEM((planes, chans, cols), bf),
            dma((4 * m,)), dma((4 * m,)), dma((4 * m,)), dma((8 * m,)), dma((4 * m,)), dma((2 * m,)), dma((2,)), dma((2,)),
            dma((span,)), dma((span,)), dma((2,)), dma((2,)),
            dma((2 * m,)), dma((2 * m,)), dma((2 * m,)), dma((2 * m,)),
            pltpu.SemaphoreType.REGULAR((m, 2)),
        ],
        compiler_params=pltpu.CompilerParams(collective_id=0, has_side_effects=True),
    )(*operands)
    return updated.transpose(0, 2, 1)[None]


def fits(voxels):
    n = lax.axis_size("gx")
    sides = lax.axis_size("gy")
    xs, ys, zs, _ = voxels.shape
    return xs == 1 and sides == 2 and n % 2 == 0 and n >= 8 and ys == n * 4 * reach and 2 * ys == zs


def plain_planes(features, row_weights, column_weights, depth_weights, plane_kernels):
    xy_plane = jnp.einsum(
        "xyzc,zc->xyc", features, depth_weights, preferred_element_type=jnp.float32
    ).astype(jnp.bfloat16)
    xz_part = jnp.einsum(
        "xyzc,yc->xzc", features, column_weights, preferred_element_type=jnp.float32
    )
    yz_part = jnp.einsum("xyzc,xc->yzc", features, row_weights, preferred_element_type=jnp.float32)
    xy_out = plane_block(xy_plane, plane_kernels[0], rim_xy)
    xz_plane = lax.psum(xz_part, "gy").astype(jnp.bfloat16)
    xz_out = plane_block(xz_plane, plane_kernels[1], rim_xz)
    yz_plane = lax.psum(yz_part, "gx").astype(jnp.bfloat16)
    yz_out = plane_block(yz_plane, plane_kernels[2], rim_yz)
    return xy_out, xz_out, yz_out


def shards(
    voxels,
    occupancy,
    row_weights,
    column_weights,
    depth_weights,
    plane_kernels,
    expand_weight,
    shrink_weight,
):
    if fits(voxels):
        return fused(
            voxels,
            occupancy,
            row_weights,
            column_weights,
            depth_weights,
            plane_kernels,
            expand_weight,
            shrink_weight,
        )
    features = voxels * occupancy.astype(jnp.bfloat16)[..., None]
    xy_out, xz_out, yz_out = plain_planes(features, row_weights, column_weights, depth_weights, plane_kernels)
    product = xy_out.astype(jnp.float32)[:, :, None, :] * xz_out.astype(jnp.float32)[:, None, :, :]
    product = product * yz_out.astype(jnp.float32)[None, :, :, :]
    mixed = (product_scale * product).astype(jnp.bfloat16)
    hidden = jax.nn.silu(
        jnp.einsum("xyzc,ch->xyzh", mixed, expand_weight, preferred_element_type=jnp.float32)
    ).astype(jnp.bfloat16)
    branch = jnp.einsum("xyzh,hc->xyzc", hidden, shrink_weight, preferred_element_type=jnp.float32)
    return (features.astype(jnp.float32) + branch).astype(jnp.bfloat16)


def solution(mesh):
    in_specs = (
        P(("groups", "gx"), "gy", None, None),
        P(("groups", "gx"), "gy", None),
        P("gx", None),
        P("gy", None),
        P(),
        P(),
        P(),
        P(),
    )
    out_specs = P(("groups", "gx"), "gy", None, None)
    return jax.shard_map(shards, mesh=mesh, in_specs=in_specs, out_specs=out_specs, check_vma=False)
```

```python
import functools

import jax
import jax.numpy as jnp
from jax import lax
from jax.experimental import pallas as pl
from jax.experimental.pallas import tpu as pltpu
from jax.sharding import PartitionSpec as P

MESH = pl.DeviceIdType.MESH
reach = 2

product_scale = 8.0


def with_halo(cells, sides, width):
    for axis, dim in sides:
        count = lax.axis_size(axis)
        ends = count - 1
        head = lax.slice_in_dim(cells, 0, width, axis=dim)
        tail = lax.slice_in_dim(cells, cells.shape[dim] - width, cells.shape[dim], axis=dim)
        cells = jnp.concatenate(
            [
                lax.ppermute(tail, axis, [(i, (i + 1) % count) for i in range(ends)]),
                cells,
                lax.ppermute(head, axis, [((i + 1) % count, i) for i in range(ends)]),
            ],
            axis=dim,
        )
    return cells


def conv_valid(padded, kernel):
    rows = padded.shape[0] - 2
    cols = padded.shape[1] - 2
    total = jnp.zeros((rows, cols, kernel.shape[-1]), jnp.float32)
    for row_off in range(3):
        for col_off in range(3):
            window = padded[row_off : row_off + rows, col_off : col_off + cols]
            total = total + jnp.einsum(
                "ijc,co->ijo", window, kernel[row_off, col_off], preferred_element_type=jnp.float32
            )
    return total


def plane_block(plane, kernels, extend):
    inner = jax.nn.silu(conv_valid(extend(plane), kernels[0])).astype(jnp.bfloat16)
    return conv_valid(extend(inner), kernels[1]).astype(jnp.bfloat16)


def rim_xy(plane):
    return with_halo(plane, (("gx", 0), ("gy", 1)), 1)


def rim_xz(plane):
    padded = with_halo(plane, (("gx", 0),), 1)
    return jnp.pad(padded, ((0, 0), (1, 1), (0, 0)))


def rim_yz(plane):
    padded = with_halo(plane, (("gy", 0),), 1)
    return jnp.pad(padded, ((0, 0), (1, 1), (0, 0)))


def conv_row(window, weight):
    taps = jnp.dot(weight, window, preferred_element_type=jnp.float32)
    chans = taps.shape[0] // 3
    cols = taps.shape[1]
    lane = lax.broadcasted_iota(jnp.int32, (chans, cols), 1)
    left = pltpu.roll(taps[:chans], 1, 1)
    right = pltpu.roll(taps[2 * chans :], cols - 1, 1)
    left = jnp.where(lane == 0, 0.0, left)
    right = jnp.where(lane == cols - 1, 0.0, right)
    return taps[chans : 2 * chans] + left + right


def silu(v):
    half = 0.5 * v
    return half + half * jnp.tanh(half)


def identity(size):
    row = lax.broadcasted_iota(jnp.int32, (size, size), 0)
    col = lax.broadcasted_iota(jnp.int32, (size, size), 1)
    return jnp.where(row == col, 1.0, 0.0)


def flipped(x):
    eye = identity(x.shape[1]).astype(x.dtype)
    return lax.dot_general(eye, x, (((1,), (1,)), ((), ())), preferred_element_type=jnp.float32)


def column(x, at):
    lane = lax.broadcasted_iota(jnp.int32, x.shape, 1)
    return jnp.sum(jnp.where(lane == at, x, 0.0), axis=1, keepdims=True)


own_order = (2, 3, 1, 0)


def pick(index, values):
    chosen = values[0]
    for i, value in enumerate(values):
        if i > 0 and value != values[0]:
            chosen = jnp.where(index == i, value, chosen)
    return chosen


def others(m, z):
    return [k for k in range(m) if k != z]


def joined(m, z, k):
    return z in (0, m - 1) and abs(k - z) > 1


def joins(m, z):
    if z == 1:
        return [(0, k) for k in range(m - 1, 1, -1)]
    if z == m - 2:
        return [(m - 1, k) for k in range(m - 2)]
    return []


def sum_order(m, z):
    far = sorted(others(m, z), key=lambda k: -abs(k - z))
    held = [k for _, k in joins(m, z)]
    first = [k for k in far if k in held or joined(m, z, k)]
    rest = [k for k in far if k not in first]
    ks = [(k, c) for c in range(3) for k in first] + [(k, c) for c in range(3) for k in rest + [z]]
    ks = [kc for kc in ks if kc[0] != z] + [kc for kc in ks if kc[0] == z]
    return [4 * k + c for k, c in ks]


def passed(m, z, k):
    return k == m - 1 and z == m - 3


def give_order(m, z):
    return sorted(others(m, z), key=lambda k: k - z if k > z else k)


def take_order(m, z):
    ks = sorted(others(m, z), key=lambda k: (passed(m, k, z), abs(k - z)))
    return [4 * k + c for c in own_order for k in ks]


def block_kernel(
    n, voxels_in, occupancy_in, row_weights_in, column_weights_in, depth_in, kernels_in, expand_in, shrink_in, updated,
    voxels, occupancy, row_weights, column_weights, depth_weights, plane_kernels, expand, shrink, load_s, fetch_s,
    part, rows_in, weights, wide, yz_out, row_sums, turned,
    pair_in, pair_sum, line_in, slab_in, slab_sum, yz_sum, yz_plane, yz_inner,
    row_other, row_slots, row_plane, row_inner, outs,
    pair_s, pair_r, line_s, line_r, slab_s, slab_r, halo_s, halo_r, row_s, row_r, core_s, core_r, spread_s, spread_r, cross_s, cross_r, known,
):
    me = lax.axis_index("gx")
    g = lax.axis_index("gy")
    m = n // 2
    a = me // 2
    b = me % 2
    count, chans, cols = part.shape
    rows = count // n
    bf = jnp.bfloat16
    f32 = jnp.float32
    partner = a * 2 + 1 - b

    def table(make):
        return [make(z) for z in range(m)]

    def feature_row(y):
        return voxels[y].astype(f32) * occupancy[pl.ds(y, 1), :].astype(f32)

    def piece(bb, aa):
        return bb * m + aa + bb * (m - 1 - 2 * aa)

    def owner(j):
        bb = j // m
        aa = j % m
        return (aa + bb * (m - 1 - 2 * aa)) * 2 + bb

    def offset(c):
        starts = [0, rows - reach, reach, 2 * reach]
        return starts[c] if isinstance(c, int) else pick(c, starts)

    def slice_of(bb, q):
        return pl.ds(piece(bb, q // 4) * rows + (q % 4) * reach, reach)

    def remote(src, dst, send, recv, gx, gy=None):
        target = {"gx": gx} if gy is None else {"gx": gx, "gy": gy}
        return pltpu.make_async_remote_copy(
            src_ref=src, dst_ref=dst, send_sem=send, recv_sem=recv, device_id=target, device_id_type=MESH
        )

    place = g * n + piece(b, a)
    last = 2 * n - 1
    before = jnp.maximum(place - 1, 0)
    after = jnp.minimum(place + 1, last)

    barrier = pltpu.get_barrier_semaphore()

    def greet(gx, gy):
        pl.semaphore_signal(barrier, inc=1, device_id={"gx": gx, "gy": gy}, device_id_type=MESH)

    lower = a > 0
    upper = a < m - 1
    slant = jnp.where(b == 0, lower, upper)
    seam_low = place == n - 1
    seam_high = place == n
    greet(partner, g)
    greet(me, 1 - g)
    pl.when(lower)(lambda: greet(jnp.maximum(me - 2, 0), g))
    pl.when(upper)(lambda: greet(jnp.minimum(me + 2, n - 1), g))
    pl.when(slant)(lambda: greet(jnp.clip(me + 2 * b - 1, 0, n - 1), g))
    pl.when(seam_low)(lambda: greet(owner(0), 1 - g))
    pl.when(seam_high)(lambda: greet(owner(n - 1), 1 - g))
    greeters = (
        2 + lower.astype(jnp.int32) + upper.astype(jnp.int32) + slant.astype(jnp.int32)
        + seam_low.astype(jnp.int32) + seam_high.astype(jnp.int32)
    )

    order = table(lambda z: sum_order(m, z))
    steps = 3 * m
    turns = [pick(a, [o[i] for o in order]) for i in range(steps)]

    small = [
        pltpu.make_async_copy(row_weights_in, row_weights, load_s.at[0]),
        pltpu.make_async_copy(occupancy_in, occupancy, load_s.at[1]),
    ]
    large = []
    for bb in (1 - b, b):
        for k in range(m):
            at = pl.ds(piece(bb, k) * rows, rows)
            large.append(pltpu.make_async_copy(voxels_in.at[at], voxels.at[at], load_s.at[2 + len(large)]))
    fetches = [
        pltpu.make_async_copy(kernels_in, plane_kernels, fetch_s.at[0]),
        pltpu.make_async_copy(column_weights_in, column_weights, fetch_s.at[1]),
        pltpu.make_async_copy(depth_in, depth_weights, fetch_s.at[2]),
        pltpu.make_async_copy(expand_in, expand, fetch_s.at[3]),
        pltpu.make_async_copy(shrink_in, shrink, fetch_s.at[4]),
    ]
    for copy in small + large + fetches:
        copy.start()

    for copy in small:
        copy.wait()
    rw = jnp.broadcast_to(row_weights[...].astype(f32), (chans, chans))
    rw = jnp.sum(rw * identity(chans), axis=1, keepdims=True)

    def yz_terms(j):
        for c in range(4):
            for r in range(reach):
                part[j * rows + c * reach + r] = (feature_row(j * rows + offset(c) + r) * rw).astype(bf)

    pair_copies = []
    for q in turns:
        pair_copies.append(remote(part.at[slice_of(1 - b, q)], pair_in.at[q], pair_s.at[q], pair_r.at[q], partner))

    def yz_pieces(bb):
        def some(k, carry):
            yz_terms(piece(bb, k))
            return carry

        lax.fori_loop(0, m, some, 0)

    for copy in large[:m]:
        copy.wait()
    yz_pieces(1 - b)

    slab_copies = []
    for dist in range(1, m):
        for side in (-1, 1):
            k = jnp.clip(a + side * dist, 0, m - 1)
            there = (a + side * dist >= 0) & (a + side * dist < m)
            for bb in range(2):
                at = 2 * (dist + (m - 1 if side > 0 else 0) - 1) + bb
                copy = remote(
                    part.at[slice_of(bb, 4 * k + 3)], slab_in.at[2 * a + bb], slab_s.at[at], slab_r.at[2 * a + bb], k * 2 + b
                )
                slab_copies.append((dist, there, copy))

    def start_slabs(dist):
        for d, there, copy in slab_copies:
            if d == dist:
                pl.when(there)(copy.start)

    pl.semaphore_wait(barrier, greeters)
    for copy in pair_copies:
        copy.start()
    for copy in large[m:]:
        copy.wait()
    yz_pieces(b)
    start_slabs(1)

    def tell(level, side):
        step = 2 if side == 0 else -2
        pl.semaphore_signal(
            known.at[level, side], inc=1, device_id={"gx": jnp.clip(me - step, 0, n - 1), "gy": g}, device_id_type=MESH
        )

    def heard(level, side):
        return (a + level <= m - 1) if side == 0 else (a - level >= 0)

    def tells(level, side):
        return (lower if side == 0 else upper) & heard(level - 1, side)

    def tell_level(level):
        for side in range(2):
            if level > 2:
                pl.when(heard(level - 1, side))(lambda: pl.semaphore_wait(known.at[level - 1, side], 1))
            if level < m:
                pl.when(tells(level, side))(lambda: tell(level, side))

    tell_level(2)

    for copy in fetches:
        copy.wait()
    turned[...] = flipped(column_weights[...])
    row_sums[...] = jnp.zeros(row_sums.shape, f32)
    lane = lax.broadcasted_iota(jnp.int32, (chans, cols), 1)

    group = 4
    share = count // (2 * m)

    def row_terms(first):
        depth = depth_weights[...].astype(f32)

        def some(step, carry):
            xy, xz = row_sums[0], row_sums[1]
            for k in range(group):
                y = first + step * group + k
                f = feature_row(y)
                xy = jnp.where(lane == g * count + y, jnp.sum(f * depth, axis=1, keepdims=True), xy)
                xz = xz + f * column(turned[...], y)
            row_sums[0] = xy
            row_sums[1] = xz
            return carry

        lax.fori_loop(0, share // group, some, 0)

    def flip_plane(p, layer):
        for off in range(3):
            taps = plane_kernels[p, layer, :, off].reshape(3 * chans, chans)
            weights[p, layer, off * chans : (off + 1) * chans, :] = flipped(taps).astype(bf)

    holds = table(lambda z: [k for _, k in joins(m, z)])
    holding = (a == 1) | (a == m - 2)

    def line_copy(i):
        gx, slot = [], []
        for z in range(m):
            k, c = order[z][i] // 4, order[z][i] % 4
            if k == z:
                gx.append(z)
                slot.append(0)
            elif joined(m, z, k):
                via = z + (1 if k > z else -1)
                gx.append(via)
                slot.append(4 * m + 4 * holds[via].index(k) + c)
            else:
                gx.append(k)
                slot.append(4 * z + c)
        to = pick(a, slot)
        q = turns[i]
        return remote(pair_sum.at[q], line_in.at[to], line_s.at[q], line_r.at[to], pick(a, gx) * 2 + b)

    line_copies = [line_copy(i) for i in range(steps - 3)]
    held = [pick(a, [int(order[z][i] // 4 in holds[z]) for z in range(m)]) for i in range(steps - 3)]

    def reduce_pair(i):
        q = turns[i]
        pair_copies[i].wait_recv()
        mine = part[slice_of(b, q)].astype(f32)
        pair_sum[q] = (mine + pair_in[q].astype(f32)).astype(bf)
        pl.when(held[i] == 0)(line_copies[i].start)

    def reduce_joined(i):
        @pl.when(holding)
        def _():
            q = turns[i]
            slot = 4 * m + pick(a, [4 * (holds[z].index(order[z][i] // 4) if holds[z] else 0) + order[z][i] % 4 for z in range(m)])
            remote(pair_sum.at[q], line_in.at[slot], line_s.at[q], line_r.at[slot], partner).wait_recv()
            pair_sum[q] = (pair_sum[q].astype(f32) + line_in[slot].astype(f32)).astype(bf)
            line_copies[i].start()

    def reduce_own(c):
        pair_copies[steps - 3 + c].wait_recv()
        q = 4 * a + c
        yz_sum[c] = part[slice_of(b, q)].astype(f32) + pair_in[q].astype(f32)

    def reduce_line(c):
        for i in range(m - 1):
            sources = [sorted(others(m, z), key=lambda s: (abs(s - z), s))[i] for z in range(m)]
            src = pick(a, sources)
            skip = pick(a, [int(joined(m, s, z)) for z, s in enumerate(sources)])

            @pl.when(skip == 0)
            def _():
                slot = 4 * src + c
                remote(pair_sum.at[slot], line_in.at[slot], line_s.at[slot], line_r.at[slot], partner).wait_recv()
                yz_sum[c] = yz_sum[c] + line_in[slot].astype(f32)

    slab_cross = remote(slab_sum, pair_in.at[4 * a + 3], pair_s.at[4 * a + 3], pair_r.at[4 * a + 3], partner)

    def reduce_slab():
        q = 4 * a + 3
        total = [part[slice_of(bb, q)].astype(f32) for bb in (1 - b, b)]
        for i in range(m - 1):
            src = pick(a, [others(m, z)[i] for z in range(m)])
            for side, bb in enumerate((1 - b, b)):
                slot = 2 * src + bb
                remote(slab_in.at[slot], slab_in.at[slot], slab_s.at[slot], slab_r.at[slot], partner).wait_recv()
                total[side] = total[side] + slab_in[slot].astype(f32)
        slab_sum[...] = total[0].astype(bf)
        slab_cross.start()
        yz_sum[3] = total[1]

    def reduce_slab_own():
        slab_cross.wait_recv()
        yz_sum[3] = yz_sum[3] + pair_in[4 * a + 3].astype(f32)

    for i in range(m):
        row_terms(i * share)
    for level in range(3, m + 1):
        tell_level(level)
        start_slabs(level - 1)
    for i in range(m, 2 * m):
        row_terms(i * share)
    rows_in[...] = row_sums[...].astype(bf)
    core = remote(rows_in.at[1 - g], row_other.at[...], core_s.at[0], core_r.at[0], me, 1 - g)
    core.start()
    flip_plane(2, 0)
    flip_plane(2, 1)

    first = 5
    for i in range(first):
        reduce_pair(i)
    merges = 3 * (m - 2)
    slab_at = steps - 3 - 1
    done = 0
    for i in range(first, steps - 3):
        if done < merges:
            reduce_joined(done)
            done += 1
        reduce_pair(i)
    reduce_slab()
    core.wait_recv()
    mid = rows_in[g].astype(f32) + row_other[...].astype(f32)
    row_slots[reach] = mid.astype(bf)
    row_copies = []
    for dx in range(-reach, reach + 1):
        if dx != 0:
            slot = reach - dx
            copy = remote(
                row_slots.at[reach], row_slots.at[slot], row_s.at[slot], row_r.at[slot], jnp.clip(me + dx, 0, n - 1)
            )
            row_copies.append((dx, copy))
            pl.when((me + dx >= 0) & (me + dx < n))(copy.start)
    while done < merges:
        reduce_joined(done)
        done += 1
    for layer in range(2):
        flip_plane(g, layer)
    wide[...] = flipped(expand[...]).astype(bf)

    edge = reach * chans
    halo = [
        (place > 0, place < last, remote(
            yz_plane.at[pl.ds(edge, edge)], yz_plane.at[pl.ds(edge + rows * chans, edge)],
            halo_s.at[0], halo_r.at[0], owner(before % n), before // n,
        )),
        (place < last, place > 0, remote(
            yz_plane.at[pl.ds(rows * chans, edge)], yz_plane.at[pl.ds(0, edge)],
            halo_s.at[1], halo_r.at[1], owner(after % n), after // n,
        )),
    ]

    @pl.when(place == 0)
    def _():
        yz_plane[pl.ds(0, edge), :] = jnp.zeros((edge, cols), bf)

    @pl.when(place == last)
    def _():
        yz_plane[pl.ds(edge + rows * chans, edge), :] = jnp.zeros((edge, cols), bf)

    def settle(c):
        for r in range(reach):
            at = (reach + offset(c) + r) * chans
            yz_plane[at : at + chans, :] = yz_sum[c, r].astype(bf)

    def inner_row(i, keep):
        inner = silu(conv_row(yz_plane[i * chans : (i + 3) * chans, :], weights[2, 0])) * keep
        yz_inner[i * chans : (i + 1) * chans, :] = inner.astype(bf)

    for c in range(2):
        reduce_own(c)
    for c in range(2):
        reduce_line(c)
        settle(c)
        pl.when(halo[c][0])(halo[c][2].start)
    reduce_own(2)
    reduce_slab_own()
    settle(3)
    for i in range(rows - reach, rows):
        inner_row(i, 1.0)
    reduce_line(2)
    settle(2)

    spread_copies = []
    own = piece(b, a)

    def cross_copy(bb, q):
        at = slice_of(bb, q)
        return remote(yz_out.at[at], yz_out.at[at], cross_s.at[q], cross_r.at[q], partner)

    def give_chunk(c):
        for r in range(reach):
            at = (offset(c) + r) * chans
            done = conv_row(yz_inner[at : at + 3 * chans, :], weights[2, 1])
            yz_out[own * rows + c * reach + r] = done.astype(bf)
        q = 4 * a + c
        cross_copy(b, q).start()
        for i in range(m - 1):
            k = pick(a, [give_order(m, z)[i] for z in range(m)])
            skip = pick(a, [int(passed(m, z, give_order(m, z)[i])) for z in range(m)])
            at = slice_of(b, q)
            copy = remote(yz_out.at[at], yz_out.at[at], spread_s.at[4 * i + c], spread_r.at[q], k * 2 + b)
            pl.when(skip == 0)(copy.start)
            spread_copies.append((skip == 0, copy))

    for i in range(reach, rows - reach):
        inner_row(i, 1.0)
    give_chunk(2)
    give_chunk(3)
    pl.when(halo[0][1])(halo[0][2].wait_recv)
    inner_row(rows, 1.0)
    inner_row(rows + 1, (place < last).astype(f32))
    give_chunk(1)
    pl.when(halo[1][1])(halo[1][2].wait_recv)
    inner_row(0, (place > 0).astype(f32))
    inner_row(1, 1.0)
    give_chunk(0)

    for dx, copy in row_copies:
        pl.when((me - dx >= 0) & (me - dx < n))(copy.wait_recv)
    for s in range(2 * reach + 1):
        at = me + s - reach
        inside = (at >= 0) & (at < n)
        here = pl.ds(s * chans, chans)

        @pl.when(inside)
        def _():
            row_plane[here, :] = row_slots[s]

        @pl.when(jnp.logical_not(inside))
        def _():
            row_plane[here, :] = jnp.zeros((chans, cols), bf)

    for s in range(3):
        at = me + s - 1
        keep = ((at >= 0) & (at < n)).astype(f32)
        inner = silu(conv_row(row_plane[s * chans : (s + 3) * chans, :], weights[g, 0]))
        row_inner[s * chans : (s + 1) * chans, :] = (inner * keep).astype(bf)
    outs[g] = conv_row(row_inner[...], weights[g, 1]).astype(bf)
    share_out = remote(outs.at[g], outs.at[g], core_s.at[1], core_r.at[1], me, 1 - g)
    share_out.start()
    remote(outs.at[1 - g], outs.at[1 - g], core_s.at[1], core_r.at[1], me, 1 - g).wait_recv()

    def finish(bb, q):
        c = q % 4
        stored = piece(bb, q // 4) * rows + c * reach
        first = piece(bb, q // 4) * rows + offset(c)
        xy_out = outs[0].astype(f32)
        xz_out = outs[1].astype(f32)
        mixed = []
        for r in range(reach):
            product = column(xy_out, g * count + first + r) * xz_out
            product = product * yz_out[stored + r].astype(f32)
            mixed.append((product_scale * product).astype(bf))
        mixed = jnp.concatenate(mixed, axis=1)
        hidden = silu(jnp.dot(wide[...], mixed, preferred_element_type=f32)).astype(bf)
        branch = jnp.dot(shrink[...], hidden, preferred_element_type=f32)
        for r in range(reach):
            updated[first + r] = (feature_row(first + r) + branch[:, r * cols : (r + 1) * cols]).astype(bf)

    takes = [pick(a, [take_order(m, z)[i] for z in range(m)]) for i in range(4 * m - 4)]
    hands = a == m - 2
    handed = max(m - 3, 0)

    def hand_copy(q):
        at = slice_of(b, q)
        return remote(yz_out.at[at], yz_out.at[at], spread_s.at[4 * (m - 1) + q % 4], spread_r.at[q], (m - 1) * 2 + b)

    def take(i):
        q = takes[i]
        at = slice_of(b, q)
        remote(yz_out.at[at], yz_out.at[at], spread_s.at[0], spread_r.at[q], partner).wait_recv()
        cross_copy(b, q).start()
        pl.when(hands & (q // 4 == handed))(hand_copy(q).start)
        finish(b, q)

    crossed = [4 * a + c for c in own_order] + takes

    def take_crossed(i):
        q = crossed[i]
        cross_copy(1 - b, q).wait_recv()
        finish(1 - b, q)

    for c in own_order:
        finish(b, 4 * a + c)
    for i in range(len(crossed)):
        if i < len(takes):
            take(i)
        take_crossed(i)

    for copy in pair_copies:
        copy.wait_send()
    slab_cross.wait_send()
    for copy in line_copies:
        copy.wait_send()
    for _, there, copy in slab_copies:
        pl.when(there)(copy.wait_send)
    for sends, _, copy in halo:
        pl.when(sends)(copy.wait_send)
    core.wait_send()
    share_out.wait_send()
    for dx, copy in row_copies:
        pl.when((me + dx >= 0) & (me + dx < n))(copy.wait_send)
    for sent, copy in spread_copies:
        pl.when(sent)(copy.wait_send)
    for c in range(4):
        pl.when(hands)(hand_copy(4 * handed + c).wait_send)
    for q in crossed:
        cross_copy(b, q).wait_send()


def fused(voxels, occupancy, row_weights, column_weights, depth_weights, plane_kernels, expand_weight, shrink_weight):
    n = lax.axis_size("gx")
    m = n // 2
    count, cols, chans = voxels.shape[1:]
    rows = count // n
    sets, layers = plane_kernels.shape[:2]
    planes = 2
    span = 2 * reach + 1
    bf = jnp.bfloat16
    f32 = jnp.float32
    dma = pltpu.SemaphoreType.DMA
    operands = (
        voxels[0].transpose(0, 2, 1),
        occupancy[0],
        row_weights,
        column_weights,
        depth_weights.T,
        plane_kernels,
        expand_weight,
        shrink_weight.T,
    )
    updated = pl.pallas_call(
        functools.partial(block_kernel, n),
        out_shape=pltpu.VMEM((count, chans, cols), bf),
        in_specs=[pl.BlockSpec(memory_space=pl.ANY) for _ in operands],
        out_specs=pl.BlockSpec(memory_space=pltpu.VMEM),
        scratch_shapes=[pltpu.VMEM(x.shape, x.dtype) for x in operands]
        + [
            dma((2 + n,)),
            dma((5,)),
            pltpu.VMEM((count, chans, cols), bf),
            pltpu.VMEM((planes, chans, cols), bf),
            pltpu.VMEM((sets, layers, 3 * chans, 3 * chans), bf),
            pltpu.VMEM(expand_weight.shape[::-1], bf),
            pltpu.VMEM((count, chans, cols), bf),
            pltpu.VMEM((planes, chans, cols), f32),
            pltpu.VMEM((chans, count), f32),
            pltpu.VMEM((4 * m, reach, chans, cols), bf),
            pltpu.VMEM((4 * m, reach, chans, cols), bf),
            pltpu.VMEM((8 * m, reach, chans, cols), bf),
            pltpu.VMEM((2 * m, reach, chans, cols), bf),
            pltpu.VMEM((reach, chans, cols), bf),
            pltpu.VMEM((4, reach, chans, cols), f32),
            pltpu.VMEM(((rows + 4) * chans, cols), bf),
            pltpu.VMEM(((rows + 2) * chans, cols), bf),
            pltpu.VMEM((chans, cols), bf),
            pltpu.VMEM((span, chans, cols), bf),
            pltpu.VMEM((span * chans, cols), bf),
            pltpu.VMEM((3 * chans, cols), bf),
            pltpu.VMEM((planes, chans, cols), bf),
            dma((4 * m,)), dma((4 * m,)), dma((4 * m,)), dma((8 * m,)), dma((4 * m,)), dma((2 * m,)), dma((2,)), dma((2,)),
            dma((span,)), dma((span,)), dma((2,)), dma((2,)),
            dma((4 * m,)), dma((4 * m,)), dma((4 * m,)), dma((4 * m,)),
            pltpu.SemaphoreType.REGULAR((m, 2)),
        ],
        compiler_params=pltpu.CompilerParams(collective_id=0, has_side_effects=True),
    )(*operands)
    return updated.transpose(0, 2, 1)[None]


def fits(voxels):
    n = lax.axis_size("gx")
    sides = lax.axis_size("gy")
    xs, ys, zs, _ = voxels.shape
    return xs == 1 and sides == 2 and n % 2 == 0 and n >= 8 and ys == n * 4 * reach and 2 * ys == zs


def plain_planes(features, row_weights, column_weights, depth_weights, plane_kernels):
    xy_plane = jnp.einsum(
        "xyzc,zc->xyc", features, depth_weights, preferred_element_type=jnp.float32
    ).astype(jnp.bfloat16)
    xz_part = jnp.einsum(
        "xyzc,yc->xzc", features, column_weights, preferred_element_type=jnp.float32
    )
    yz_part = jnp.einsum("xyzc,xc->yzc", features, row_weights, preferred_element_type=jnp.float32)
    xy_out = plane_block(xy_plane, plane_kernels[0], rim_xy)
    xz_plane = lax.psum(xz_part, "gy").astype(jnp.bfloat16)
    xz_out = plane_block(xz_plane, plane_kernels[1], rim_xz)
    yz_plane = lax.psum(yz_part, "gx").astype(jnp.bfloat16)
    yz_out = plane_block(yz_plane, plane_kernels[2], rim_yz)
    return xy_out, xz_out, yz_out


def shards(
    voxels,
    occupancy,
    row_weights,
    column_weights,
    depth_weights,
    plane_kernels,
    expand_weight,
    shrink_weight,
):
    if fits(voxels):
        return fused(
            voxels,
            occupancy,
            row_weights,
            column_weights,
            depth_weights,
            plane_kernels,
            expand_weight,
            shrink_weight,
        )
    features = voxels * occupancy.astype(jnp.bfloat16)[..., None]
    xy_out, xz_out, yz_out = plain_planes(features, row_weights, column_weights, depth_weights, plane_kernels)
    product = xy_out.astype(jnp.float32)[:, :, None, :] * xz_out.astype(jnp.float32)[:, None, :, :]
    product = product * yz_out.astype(jnp.float32)[None, :, :, :]
    mixed = (product_scale * product).astype(jnp.bfloat16)
    hidden = jax.nn.silu(
        jnp.einsum("xyzc,ch->xyzh", mixed, expand_weight, preferred_element_type=jnp.float32)
    ).astype(jnp.bfloat16)
    branch = jnp.einsum("xyzh,hc->xyzc", hidden, shrink_weight, preferred_element_type=jnp.float32)
    return (features.astype(jnp.float32) + branch).astype(jnp.bfloat16)


def solution(mesh):
    in_specs = (
        P(("groups", "gx"), "gy", None, None),
        P(("groups", "gx"), "gy", None),
        P("gx", None),
        P("gy", None),
        P(),
        P(),
        P(),
        P(),
    )
    out_specs = P(("groups", "gx"), "gy", None, None)
    return jax.shard_map(shards, mesh=mesh, in_specs=in_specs, out_specs=out_specs, check_vma=False)
```

```python
import functools

import jax
import jax.numpy as jnp
from jax import lax
from jax.experimental import pallas as pl
from jax.experimental.pallas import tpu as pltpu
from jax.sharding import PartitionSpec as P

MESH = pl.DeviceIdType.MESH
reach = 2

product_scale = 8.0


def with_halo(cells, sides, width):
    for axis, dim in sides:
        count = lax.axis_size(axis)
        ends = count - 1
        head = lax.slice_in_dim(cells, 0, width, axis=dim)
        tail = lax.slice_in_dim(cells, cells.shape[dim] - width, cells.shape[dim], axis=dim)
        cells = jnp.concatenate(
            [
                lax.ppermute(tail, axis, [(i, (i + 1) % count) for i in range(ends)]),
                cells,
                lax.ppermute(head, axis, [((i + 1) % count, i) for i in range(ends)]),
            ],
            axis=dim,
        )
    return cells


def conv_valid(padded, kernel):
    rows = padded.shape[0] - 2
    cols = padded.shape[1] - 2
    total = jnp.zeros((rows, cols, kernel.shape[-1]), jnp.float32)
    for row_off in range(3):
        for col_off in range(3):
            window = padded[row_off : row_off + rows, col_off : col_off + cols]
            total = total + jnp.einsum(
                "ijc,co->ijo", window, kernel[row_off, col_off], preferred_element_type=jnp.float32
            )
    return total


def plane_block(plane, kernels, extend):
    inner = jax.nn.silu(conv_valid(extend(plane), kernels[0])).astype(jnp.bfloat16)
    return conv_valid(extend(inner), kernels[1]).astype(jnp.bfloat16)


def rim_xy(plane):
    return with_halo(plane, (("gx", 0), ("gy", 1)), 1)


def rim_xz(plane):
    padded = with_halo(plane, (("gx", 0),), 1)
    return jnp.pad(padded, ((0, 0), (1, 1), (0, 0)))


def rim_yz(plane):
    padded = with_halo(plane, (("gy", 0),), 1)
    return jnp.pad(padded, ((0, 0), (1, 1), (0, 0)))


def conv_row(window, weight):
    taps = jnp.dot(weight, window, preferred_element_type=jnp.float32)
    chans = taps.shape[0] // 3
    cols = taps.shape[1]
    lane = lax.broadcasted_iota(jnp.int32, (chans, cols), 1)
    left = pltpu.roll(taps[:chans], 1, 1)
    right = pltpu.roll(taps[2 * chans :], cols - 1, 1)
    left = jnp.where(lane == 0, 0.0, left)
    right = jnp.where(lane == cols - 1, 0.0, right)
    return taps[chans : 2 * chans] + left + right


def silu(v):
    half = 0.5 * v
    return half + half * jnp.tanh(half)


def identity(size):
    row = lax.broadcasted_iota(jnp.int32, (size, size), 0)
    col = lax.broadcasted_iota(jnp.int32, (size, size), 1)
    return jnp.where(row == col, 1.0, 0.0)


def flipped(x):
    eye = identity(x.shape[1]).astype(x.dtype)
    return lax.dot_general(eye, x, (((1,), (1,)), ((), ())), preferred_element_type=jnp.float32)


def column(x, at):
    lane = lax.broadcasted_iota(jnp.int32, x.shape, 1)
    return jnp.sum(jnp.where(lane == at, x, 0.0), axis=1, keepdims=True)


halves = ((2, 3), (1, 0))
own_order = halves[0] + halves[1]


def pick(index, values):
    chosen = values[0]
    for i, value in enumerate(values):
        if i > 0 and value != values[0]:
            chosen = jnp.where(index == i, value, chosen)
    return chosen


def others(m, z):
    return [k for k in range(m) if k != z]


def joined(m, z, k):
    return z in (0, m - 1) and abs(k - z) > 1


def joins(m, z):
    if z == 1:
        return [(0, k) for k in range(m - 1, 1, -1)]
    if z == m - 2:
        return [(m - 1, k) for k in range(m - 2)]
    return []


def sum_order(m, z):
    far = sorted(others(m, z), key=lambda k: -abs(k - z))
    held = [k for _, k in joins(m, z)]
    first = [k for k in far if k in held or joined(m, z, k)]
    rest = [k for k in far if k not in first]
    ks = [(k, c) for c in range(3) for k in first] + [(k, c) for c in range(3) for k in rest + [z]]
    ks = [kc for kc in ks if kc[0] != z] + [kc for kc in ks if kc[0] == z]
    return [4 * k + c for k, c in ks]


def passed(m, z, k):
    return k == m - 1 and z == m - 3


def give_order(m, z):
    return sorted(others(m, z), key=lambda k: k - z if k > z else k)


def take_order(m, z):
    def rank(k):
        return passed(m, k, z), z if k > z else z - k - 1, abs(k - z) > 1, -k

    ks = sorted(others(m, z), key=rank)
    return [4 * k + c for half in halves for k in ks for c in half]


def block_kernel(
    n, voxels_in, occupancy_in, row_weights_in, column_weights_in, depth_in, kernels_in, expand_in, shrink_in, updated,
    voxels, occupancy, row_weights, column_weights, depth_weights, plane_kernels, expand, shrink, load_s, fetch_s,
    part, rows_in, weights, wide, yz_out, row_sums, turned,
    pair_in, pair_sum, line_in, slab_in, slab_sum, yz_sum, yz_plane, yz_inner,
    row_other, row_slots, row_plane, row_inner, outs,
    pair_s, pair_r, line_s, line_r, slab_s, slab_r, halo_s, halo_r, row_s, row_r, core_s, core_r, spread_s, spread_r, cross_s, cross_r, known,
):
    me = lax.axis_index("gx")
    g = lax.axis_index("gy")
    m = n // 2
    a = me // 2
    b = me % 2
    count, chans, cols = part.shape
    rows = count // n
    bf = jnp.bfloat16
    f32 = jnp.float32
    partner = a * 2 + 1 - b

    def table(make):
        return [make(z) for z in range(m)]

    def feature_row(y):
        return voxels[y].astype(f32) * occupancy[pl.ds(y, 1), :].astype(f32)

    def piece(bb, aa):
        return bb * m + aa + bb * (m - 1 - 2 * aa)

    def owner(j):
        bb = j // m
        aa = j % m
        return (aa + bb * (m - 1 - 2 * aa)) * 2 + bb

    def offset(c):
        starts = [0, rows - reach, reach, 2 * reach]
        return starts[c] if isinstance(c, int) else pick(c, starts)

    def slice_of(bb, q):
        return pl.ds(piece(bb, q // 4) * rows + (q % 4) * reach, reach)

    def remote(src, dst, send, recv, gx, gy=None):
        target = {"gx": gx} if gy is None else {"gx": gx, "gy": gy}
        return pltpu.make_async_remote_copy(
            src_ref=src, dst_ref=dst, send_sem=send, recv_sem=recv, device_id=target, device_id_type=MESH
        )

    place = g * n + piece(b, a)
    last = 2 * n - 1
    before = jnp.maximum(place - 1, 0)
    after = jnp.minimum(place + 1, last)

    barrier = pltpu.get_barrier_semaphore()

    def greet(gx, gy):
        pl.semaphore_signal(barrier, inc=1, device_id={"gx": gx, "gy": gy}, device_id_type=MESH)

    lower = a > 0
    upper = a < m - 1
    slant = jnp.where(b == 0, lower, upper)
    seam_low = place == n - 1
    seam_high = place == n
    greet(partner, g)
    greet(me, 1 - g)
    pl.when(lower)(lambda: greet(jnp.maximum(me - 2, 0), g))
    pl.when(upper)(lambda: greet(jnp.minimum(me + 2, n - 1), g))
    pl.when(slant)(lambda: greet(jnp.clip(me + 2 * b - 1, 0, n - 1), g))
    pl.when(seam_low)(lambda: greet(owner(0), 1 - g))
    pl.when(seam_high)(lambda: greet(owner(n - 1), 1 - g))
    greeters = (
        2 + lower.astype(jnp.int32) + upper.astype(jnp.int32) + slant.astype(jnp.int32)
        + seam_low.astype(jnp.int32) + seam_high.astype(jnp.int32)
    )

    order = table(lambda z: sum_order(m, z))
    steps = 3 * m
    turns = [pick(a, [o[i] for o in order]) for i in range(steps)]

    small = [
        pltpu.make_async_copy(row_weights_in, row_weights, load_s.at[0]),
        pltpu.make_async_copy(occupancy_in, occupancy, load_s.at[1]),
    ]
    large = []
    for bb in (1 - b, b):
        for k in range(m):
            at = pl.ds(piece(bb, k) * rows, rows)
            large.append(pltpu.make_async_copy(voxels_in.at[at], voxels.at[at], load_s.at[2 + len(large)]))
    fetches = [
        pltpu.make_async_copy(kernels_in, plane_kernels, fetch_s.at[0]),
        pltpu.make_async_copy(column_weights_in, column_weights, fetch_s.at[1]),
        pltpu.make_async_copy(depth_in, depth_weights, fetch_s.at[2]),
        pltpu.make_async_copy(expand_in, expand, fetch_s.at[3]),
        pltpu.make_async_copy(shrink_in, shrink, fetch_s.at[4]),
    ]
    for copy in small + large + fetches:
        copy.start()

    for copy in small:
        copy.wait()
    rw = jnp.broadcast_to(row_weights[...].astype(f32), (chans, chans))
    rw = jnp.sum(rw * identity(chans), axis=1, keepdims=True)

    def yz_terms(j):
        for c in range(4):
            for r in range(reach):
                part[j * rows + c * reach + r] = (feature_row(j * rows + offset(c) + r) * rw).astype(bf)

    pair_copies = []
    for q in turns:
        pair_copies.append(remote(part.at[slice_of(1 - b, q)], pair_in.at[q], pair_s.at[0], pair_r.at[q], partner))

    def yz_pieces(bb):
        def some(k, carry):
            yz_terms(piece(bb, k))
            return carry

        lax.fori_loop(0, m, some, 0)

    for copy in large[:m]:
        copy.wait()
    yz_pieces(1 - b)

    def sent(buffer, size, sem, recv):
        return remote(buffer.at[pl.ds(0, size)], buffer.at[pl.ds(0, size)], sem.at[0], recv.at[0], partner)

    pair_all = sent(part, steps * reach, pair_s, pair_r)
    line_all = sent(pair_sum, steps - 3, line_s, line_r)
    slab_all = sent(part, 2 * (m - 1) * reach, slab_s, slab_r)
    cross_all = sent(yz_out, 4 * m * reach, cross_s, cross_r)
    slab_copies = []
    for dist in range(1, m):
        for side in (-1, 1):
            k = jnp.clip(a + side * dist, 0, m - 1)
            there = (a + side * dist >= 0) & (a + side * dist < m)
            for bb in range(2):
                copy = remote(
                    part.at[slice_of(bb, 4 * k + 3)], slab_in.at[2 * a + bb], slab_s.at[0], slab_r.at[2 * a + bb], k * 2 + b
                )
                slab_copies.append((dist, there, copy))

    def start_slabs(dist):
        for d, there, copy in slab_copies:
            if d == dist:
                pl.when(there)(copy.start)

    pl.semaphore_wait(barrier, greeters)
    for copy in pair_copies:
        copy.start()
    for copy in large[m:]:
        copy.wait()
    yz_pieces(b)
    start_slabs(1)

    def tell(level, side):
        step = 2 if side == 0 else -2
        pl.semaphore_signal(
            known.at[level, side], inc=1, device_id={"gx": jnp.clip(me - step, 0, n - 1), "gy": g}, device_id_type=MESH
        )

    def heard(level, side):
        return (a + level <= m - 1) if side == 0 else (a - level >= 0)

    def tells(level, side):
        return (lower if side == 0 else upper) & heard(level - 1, side)

    def tell_level(level):
        for side in range(2):
            if level > 2:
                pl.when(heard(level - 1, side))(lambda: pl.semaphore_wait(known.at[level - 1, side], 1))
            if level < m:
                pl.when(tells(level, side))(lambda: tell(level, side))

    tell_level(2)
    for level in range(3, m):
        tell_level(level)
        start_slabs(level - 1)

    for copy in fetches:
        copy.wait()
    turned[...] = flipped(column_weights[...])
    row_sums[...] = jnp.zeros(row_sums.shape, f32)
    lane = lax.broadcasted_iota(jnp.int32, (chans, cols), 1)

    group = 4
    share = count // (2 * m)

    def row_terms(first):
        depth = depth_weights[...].astype(f32)

        def some(step, carry):
            xy, xz = row_sums[0], row_sums[1]
            for k in range(group):
                y = first + step * group + k
                f = feature_row(y)
                xy = jnp.where(lane == g * count + y, jnp.sum(f * depth, axis=1, keepdims=True), xy)
                xz = xz + f * column(turned[...], y)
            row_sums[0] = xy
            row_sums[1] = xz
            return carry

        lax.fori_loop(0, share // group, some, 0)

    def flip_plane(p, layer):
        for off in range(3):
            taps = plane_kernels[p, layer, :, off].reshape(3 * chans, chans)
            weights[p, layer, off * chans : (off + 1) * chans, :] = flipped(taps).astype(bf)

    holds = table(lambda z: [k for _, k in joins(m, z)])
    holding = (a == 1) | (a == m - 2)

    def line_copy(i):
        gx, slot = [], []
        for z in range(m):
            k, c = order[z][i] // 4, order[z][i] % 4
            if k == z:
                gx.append(z)
                slot.append(0)
            elif joined(m, z, k):
                via = z + (1 if k > z else -1)
                gx.append(via)
                slot.append(4 * m + 4 * holds[via].index(k) + c)
            else:
                gx.append(k)
                slot.append(4 * z + c)
        to = pick(a, slot)
        q = turns[i]
        return remote(pair_sum.at[q], line_in.at[to], line_s.at[0], line_r.at[to], pick(a, gx) * 2 + b)

    line_copies = [line_copy(i) for i in range(steps - 3)]
    held = [pick(a, [int(order[z][i] // 4 in holds[z]) for z in range(m)]) for i in range(steps - 3)]

    def reduce_pair(i):
        q = turns[i]
        pair_copies[i].wait_recv()
        mine = part[slice_of(b, q)].astype(f32)
        pair_sum[q] = (mine + pair_in[q].astype(f32)).astype(bf)
        pl.when(held[i] == 0)(line_copies[i].start)

    def reduce_joined(i):
        @pl.when(holding)
        def _():
            q = turns[i]
            slot = 4 * m + pick(a, [4 * (holds[z].index(order[z][i] // 4) if holds[z] else 0) + order[z][i] % 4 for z in range(m)])
            remote(pair_sum.at[q], line_in.at[slot], line_s.at[0], line_r.at[slot], partner).wait_recv()
            pair_sum[q] = (pair_sum[q].astype(f32) + line_in[slot].astype(f32)).astype(bf)
            line_copies[i].start()

    def reduce_own(c):
        pair_copies[steps - 3 + c].wait_recv()
        q = 4 * a + c
        yz_sum[c] = part[slice_of(b, q)].astype(f32) + pair_in[q].astype(f32)

    def reduce_line(c):
        for i in range(m - 1):
            sources = [sorted(others(m, z), key=lambda s: (abs(s - z), s))[i] for z in range(m)]
            src = pick(a, sources)
            skip = pick(a, [int(joined(m, s, z)) for z, s in enumerate(sources)])

            @pl.when(skip == 0)
            def _():
                slot = 4 * src + c
                remote(pair_sum.at[slot], line_in.at[slot], line_s.at[0], line_r.at[slot], partner).wait_recv()
                yz_sum[c] = yz_sum[c] + line_in[slot].astype(f32)

    slab_cross = remote(slab_sum, pair_in.at[4 * a + 3], pair_s.at[1], pair_r.at[4 * a + 3], partner)

    def reduce_slab():
        q = 4 * a + 3
        total = [part[slice_of(bb, q)].astype(f32) for bb in (1 - b, b)]
        for i in range(m - 1):
            src = pick(a, [others(m, z)[i] for z in range(m)])
            for side, bb in enumerate((1 - b, b)):
                slot = 2 * src + bb
                remote(slab_in.at[slot], slab_in.at[slot], slab_s.at[0], slab_r.at[slot], partner).wait_recv()
                total[side] = total[side] + slab_in[slot].astype(f32)
        slab_sum[...] = total[0].astype(bf)
        slab_cross.start()
        yz_sum[3] = total[1]

    def reduce_slab_own():
        slab_cross.wait_recv()
        yz_sum[3] = yz_sum[3] + pair_in[4 * a + 3].astype(f32)

    for i in range(2):
        row_terms(i * share)
    tell_level(m)
    start_slabs(m - 1)
    for i in range(2, 2 * m):
        row_terms(i * share)
    rows_in[...] = row_sums[...].astype(bf)
    core = remote(rows_in.at[1 - g], row_other.at[...], core_s.at[0], core_r.at[0], me, 1 - g)
    core.start()
    flip_plane(2, 0)
    flip_plane(2, 1)

    first = 5
    for i in range(first):
        reduce_pair(i)
    merges = 3 * (m - 2)
    slab_at = steps - 3 - 1
    done = 0
    for i in range(first, steps - 3):
        if done < merges:
            reduce_joined(done)
            done += 1
        reduce_pair(i)
    reduce_slab()
    core.wait_recv()
    mid = rows_in[g].astype(f32) + row_other[...].astype(f32)
    row_slots[reach] = mid.astype(bf)
    row_copies = []
    for dx in range(-reach, reach + 1):
        if dx != 0:
            slot = reach - dx
            copy = remote(
                row_slots.at[reach], row_slots.at[slot], row_s.at[slot], row_r.at[slot], jnp.clip(me + dx, 0, n - 1)
            )
            row_copies.append((dx, copy))
            pl.when((me + dx >= 0) & (me + dx < n))(copy.start)
    while done < merges:
        reduce_joined(done)
        done += 1
    for layer in range(2):
        flip_plane(g, layer)
    wide[...] = flipped(expand[...]).astype(bf)

    edge = reach * chans
    halo = [
        (place > 0, place < last, remote(
            yz_plane.at[pl.ds(edge, edge)], yz_plane.at[pl.ds(edge + rows * chans, edge)],
            halo_s.at[0], halo_r.at[0], owner(before % n), before // n,
        )),
        (place < last, place > 0, remote(
            yz_plane.at[pl.ds(rows * chans, edge)], yz_plane.at[pl.ds(0, edge)],
            halo_s.at[1], halo_r.at[1], owner(after % n), after // n,
        )),
    ]

    @pl.when(place == 0)
    def _():
        yz_plane[pl.ds(0, edge), :] = jnp.zeros((edge, cols), bf)

    @pl.when(place == last)
    def _():
        yz_plane[pl.ds(edge + rows * chans, edge), :] = jnp.zeros((edge, cols), bf)

    def settle(c):
        for r in range(reach):
            at = (reach + offset(c) + r) * chans
            yz_plane[at : at + chans, :] = yz_sum[c, r].astype(bf)

    def inner_row(i, keep):
        inner = silu(conv_row(yz_plane[i * chans : (i + 3) * chans, :], weights[2, 0])) * keep
        yz_inner[i * chans : (i + 1) * chans, :] = inner.astype(bf)

    for c in range(2):
        reduce_own(c)
    for c in range(2):
        reduce_line(c)
        settle(c)
        pl.when(halo[c][0])(halo[c][2].start)
    reduce_own(2)
    reduce_slab_own()
    settle(3)
    for i in range(rows - reach, rows):
        inner_row(i, 1.0)
    reduce_line(2)
    settle(2)

    spread_copies = []
    own = piece(b, a)

    def cross_copy(bb, q):
        at = slice_of(bb, q)
        return remote(yz_out.at[at], yz_out.at[at], cross_s.at[0], cross_r.at[q], partner)

    def give_half(half):
        for c in half:
            for r in range(reach):
                at = (offset(c) + r) * chans
                done = conv_row(yz_inner[at : at + 3 * chans, :], weights[2, 1])
                yz_out[own * rows + c * reach + r] = done.astype(bf)
        for c in half:
            cross_copy(b, 4 * a + c).start()
        for i in range(m - 1):
            k = pick(a, [give_order(m, z)[i] for z in range(m)])
            skip = pick(a, [int(passed(m, z, give_order(m, z)[i])) for z in range(m)])
            for c in half:
                q = 4 * a + c
                at = slice_of(b, q)
                copy = remote(yz_out.at[at], yz_out.at[at], spread_s.at[4 * i + c], spread_r.at[q], k * 2 + b)
                pl.when(skip == 0)(copy.start)
                spread_copies.append((skip == 0, copy))

    for i in range(reach, rows - reach):
        inner_row(i, 1.0)
    give_half(halves[0])
    for dx, copy in row_copies:
        pl.when((me - dx >= 0) & (me - dx < n))(copy.wait_recv)
    for s in range(2 * reach + 1):
        at = me + s - reach
        inside = (at >= 0) & (at < n)
        here = pl.ds(s * chans, chans)

        @pl.when(inside)
        def _():
            row_plane[here, :] = row_slots[s]

        @pl.when(jnp.logical_not(inside))
        def _():
            row_plane[here, :] = jnp.zeros((chans, cols), bf)

    for s in range(3):
        at = me + s - 1
        keep = ((at >= 0) & (at < n)).astype(f32)
        inner = silu(conv_row(row_plane[s * chans : (s + 3) * chans, :], weights[g, 0]))
        row_inner[s * chans : (s + 1) * chans, :] = (inner * keep).astype(bf)
    outs[g] = conv_row(row_inner[...], weights[g, 1]).astype(bf)
    share_out = remote(outs.at[g], outs.at[g], core_s.at[1], core_r.at[1], me, 1 - g)
    share_out.start()
    for _, receives, copy in halo:
        pl.when(receives)(copy.wait_recv)
    inner_row(rows, 1.0)
    inner_row(rows + 1, (place < last).astype(f32))
    inner_row(0, (place > 0).astype(f32))
    inner_row(1, 1.0)
    give_half(halves[1])
    remote(outs.at[1 - g], outs.at[1 - g], core_s.at[1], core_r.at[1], me, 1 - g).wait_recv()

    def finish(*chunks):
        xy_out = outs[0].astype(f32)
        xz_out = outs[1].astype(f32)
        at = []
        for bb, q in chunks:
            c = q % 4
            stored = piece(bb, q // 4) * rows + c * reach
            first = piece(bb, q // 4) * rows + offset(c)
            at += [(stored + r, first + r) for r in range(reach)]
        mixed = []
        for s, y in at:
            product = column(xy_out, g * count + y) * xz_out
            product = product * yz_out[s].astype(f32)
            mixed.append((product_scale * product).astype(bf))
        mixed = jnp.concatenate(mixed, axis=1)
        hidden = silu(jnp.dot(wide[...], mixed, preferred_element_type=f32)).astype(bf)
        branch = jnp.dot(shrink[...], hidden, preferred_element_type=f32)
        for k, (s, y) in enumerate(at):
            updated[y] = (feature_row(y) + branch[:, k * cols : (k + 1) * cols]).astype(bf)

    takes = [pick(a, [take_order(m, z)[i] for z in range(m)]) for i in range(4 * m - 4)]
    hands = a == m - 2
    handed = max(m - 3, 0)

    def hand_copy(q):
        at = slice_of(b, q)
        return remote(yz_out.at[at], yz_out.at[at], spread_s.at[4 * (m - 1) + q % 4], spread_r.at[q], (m - 1) * 2 + b)

    def take(i):
        q = takes[i]
        at = slice_of(b, q)
        remote(yz_out.at[at], yz_out.at[at], spread_s.at[0], spread_r.at[q], partner).wait_recv()
        cross_copy(b, q).start()
        pl.when(hands & (q // 4 == handed))(hand_copy(q).start)
        return b, q

    crossed = [4 * a + c for c in own_order] + takes

    def take_crossed(i):
        q = crossed[i]
        cross_copy(1 - b, q).wait_recv()
        return 1 - b, q

    finish(*[(b, 4 * a + c) for c in own_order])

    def drain():
        pair_all.wait_send()
        slab_cross.wait_send()
        line_all.wait_send()
        slab_all.wait_send()
        for sends, _, copy in halo:
            pl.when(sends)(copy.wait_send)
        core.wait_send()
        share_out.wait_send()
        for dx, copy in row_copies:
            pl.when((me + dx >= 0) & (me + dx < n))(copy.wait_send)

    pair = 2
    for i in range(0, len(crossed), pair):
        ready = [take(j) for j in range(i, i + pair) if j < len(takes)]
        finish(*ready, *[take_crossed(j) for j in range(i, i + pair)])
        if i == 2 * pair:
            drain()
        if i == len(crossed) - 2 * pair:
            for given, copy in spread_copies:
                pl.when(given)(copy.wait_send)
            for c in range(4):
                pl.when(hands)(hand_copy(4 * handed + c).wait_send)

    cross_all.wait_send()


def fused(voxels, occupancy, row_weights, column_weights, depth_weights, plane_kernels, expand_weight, shrink_weight):
    n = lax.axis_size("gx")
    m = n // 2
    count, cols, chans = voxels.shape[1:]
    rows = count // n
    sets, layers = plane_kernels.shape[:2]
    planes = 2
    span = 2 * reach + 1
    bf = jnp.bfloat16
    f32 = jnp.float32
    dma = pltpu.SemaphoreType.DMA
    operands = (
        voxels[0].transpose(0, 2, 1),
        occupancy[0],
        row_weights,
        column_weights,
        depth_weights.T,
        plane_kernels,
        expand_weight,
        shrink_weight.T,
    )
    updated = pl.pallas_call(
        functools.partial(block_kernel, n),
        out_shape=pltpu.VMEM((count, chans, cols), bf),
        in_specs=[pl.BlockSpec(memory_space=pl.ANY) for _ in operands],
        out_specs=pl.BlockSpec(memory_space=pltpu.VMEM),
        scratch_shapes=[pltpu.VMEM(x.shape, x.dtype) for x in operands]
        + [
            dma((2 + n,)),
            dma((5,)),
            pltpu.VMEM((count, chans, cols), bf),
            pltpu.VMEM((planes, chans, cols), bf),
            pltpu.VMEM((sets, layers, 3 * chans, 3 * chans), bf),
            pltpu.VMEM(expand_weight.shape[::-1], bf),
            pltpu.VMEM((count, chans, cols), bf),
            pltpu.VMEM((planes, chans, cols), f32),
            pltpu.VMEM((chans, count), f32),
            pltpu.VMEM((4 * m, reach, chans, cols), bf),
            pltpu.VMEM((4 * m, reach, chans, cols), bf),
            pltpu.VMEM((8 * m, reach, chans, cols), bf),
            pltpu.VMEM((2 * m, reach, chans, cols), bf),
            pltpu.VMEM((reach, chans, cols), bf),
            pltpu.VMEM((4, reach, chans, cols), f32),
            pltpu.VMEM(((rows + 4) * chans, cols), bf),
            pltpu.VMEM(((rows + 2) * chans, cols), bf),
            pltpu.VMEM((chans, cols), bf),
            pltpu.VMEM((span, chans, cols), bf),
            pltpu.VMEM((span * chans, cols), bf),
            pltpu.VMEM((3 * chans, cols), bf),
            pltpu.VMEM((planes, chans, cols), bf),
            dma((2,)), dma((4 * m,)), dma((1,)), dma((8 * m,)), dma((1,)), dma((2 * m,)), dma((2,)), dma((2,)),
            dma((span,)), dma((span,)), dma((2,)), dma((2,)),
            dma((4 * m,)), dma((4 * m,)), dma((1,)), dma((4 * m,)),
            pltpu.SemaphoreType.REGULAR((m, 2)),
        ],
        compiler_params=pltpu.CompilerParams(collective_id=0, has_side_effects=True),
    )(*operands)
    return updated.transpose(0, 2, 1)[None]


def fits(voxels):
    n = lax.axis_size("gx")
    sides = lax.axis_size("gy")
    xs, ys, zs, _ = voxels.shape
    return xs == 1 and sides == 2 and n % 2 == 0 and n >= 8 and ys == n * 4 * reach and 2 * ys == zs


def plain_planes(features, row_weights, column_weights, depth_weights, plane_kernels):
    xy_plane = jnp.einsum(
        "xyzc,zc->xyc", features, depth_weights, preferred_element_type=jnp.float32
    ).astype(jnp.bfloat16)
    xz_part = jnp.einsum(
        "xyzc,yc->xzc", features, column_weights, preferred_element_type=jnp.float32
    )
    yz_part = jnp.einsum("xyzc,xc->yzc", features, row_weights, preferred_element_type=jnp.float32)
    xy_out = plane_block(xy_plane, plane_kernels[0], rim_xy)
    xz_plane = lax.psum(xz_part, "gy").astype(jnp.bfloat16)
    xz_out = plane_block(xz_plane, plane_kernels[1], rim_xz)
    yz_plane = lax.psum(yz_part, "gx").astype(jnp.bfloat16)
    yz_out = plane_block(yz_plane, plane_kernels[2], rim_yz)
    return xy_out, xz_out, yz_out


def shards(
    voxels,
    occupancy,
    row_weights,
    column_weights,
    depth_weights,
    plane_kernels,
    expand_weight,
    shrink_weight,
):
    if fits(voxels):
        return fused(
            voxels,
            occupancy,
            row_weights,
            column_weights,
            depth_weights,
            plane_kernels,
            expand_weight,
            shrink_weight,
        )
    features = voxels * occupancy.astype(jnp.bfloat16)[..., None]
    xy_out, xz_out, yz_out = plain_planes(features, row_weights, column_weights, depth_weights, plane_kernels)
    product = xy_out.astype(jnp.float32)[:, :, None, :] * xz_out.astype(jnp.float32)[:, None, :, :]
    product = product * yz_out.astype(jnp.float32)[None, :, :, :]
    mixed = (product_scale * product).astype(jnp.bfloat16)
    hidden = jax.nn.silu(
        jnp.einsum("xyzc,ch->xyzh", mixed, expand_weight, preferred_element_type=jnp.float32)
    ).astype(jnp.bfloat16)
    branch = jnp.einsum("xyzh,hc->xyzc", hidden, shrink_weight, preferred_element_type=jnp.float32)
    return (features.astype(jnp.float32) + branch).astype(jnp.bfloat16)


def solution(mesh):
    in_specs = (
        P(("groups", "gx"), "gy", None, None),
        P(("groups", "gx"), "gy", None),
        P("gx", None),
        P("gy", None),
        P(),
        P(),
        P(),
        P(),
    )
    out_specs = P(("groups", "gx"), "gy", None, None)
    return jax.shard_map(shards, mesh=mesh, in_specs=in_specs, out_specs=out_specs, check_vma=False)
```

```python
import functools

import jax
import jax.numpy as jnp
from jax import lax
from jax.experimental import pallas as pl
from jax.experimental.pallas import tpu as pltpu
from jax.sharding import PartitionSpec as P

MESH = pl.DeviceIdType.MESH
reach = 2

product_scale = 8.0


def with_halo(cells, sides, width):
    for axis, dim in sides:
        count = lax.axis_size(axis)
        ends = count - 1
        head = lax.slice_in_dim(cells, 0, width, axis=dim)
        tail = lax.slice_in_dim(cells, cells.shape[dim] - width, cells.shape[dim], axis=dim)
        cells = jnp.concatenate(
            [
                lax.ppermute(tail, axis, [(i, (i + 1) % count) for i in range(ends)]),
                cells,
                lax.ppermute(head, axis, [((i + 1) % count, i) for i in range(ends)]),
            ],
            axis=dim,
        )
    return cells


def conv_valid(padded, kernel):
    rows = padded.shape[0] - 2
    cols = padded.shape[1] - 2
    total = jnp.zeros((rows, cols, kernel.shape[-1]), jnp.float32)
    for row_off in range(3):
        for col_off in range(3):
            window = padded[row_off : row_off + rows, col_off : col_off + cols]
            total = total + jnp.einsum(
                "ijc,co->ijo", window, kernel[row_off, col_off], preferred_element_type=jnp.float32
            )
    return total


def plane_block(plane, kernels, extend):
    inner = jax.nn.silu(conv_valid(extend(plane), kernels[0])).astype(jnp.bfloat16)
    return conv_valid(extend(inner), kernels[1]).astype(jnp.bfloat16)


def rim_xy(plane):
    return with_halo(plane, (("gx", 0), ("gy", 1)), 1)


def rim_xz(plane):
    padded = with_halo(plane, (("gx", 0),), 1)
    return jnp.pad(padded, ((0, 0), (1, 1), (0, 0)))


def rim_yz(plane):
    padded = with_halo(plane, (("gy", 0),), 1)
    return jnp.pad(padded, ((0, 0), (1, 1), (0, 0)))


def conv_row(window, weight):
    taps = jnp.dot(weight, window, preferred_element_type=jnp.float32)
    chans = taps.shape[0] // 3
    cols = taps.shape[1]
    lane = lax.broadcasted_iota(jnp.int32, (chans, cols), 1)
    left = pltpu.roll(taps[:chans], 1, 1)
    right = pltpu.roll(taps[2 * chans :], cols - 1, 1)
    left = jnp.where(lane == 0, 0.0, left)
    right = jnp.where(lane == cols - 1, 0.0, right)
    return taps[chans : 2 * chans] + left + right


def silu(v):
    half = 0.5 * v
    return half + half * jnp.tanh(half)


def identity(size):
    row = lax.broadcasted_iota(jnp.int32, (size, size), 0)
    col = lax.broadcasted_iota(jnp.int32, (size, size), 1)
    return jnp.where(row == col, 1.0, 0.0)


def flipped(x):
    eye = identity(x.shape[1]).astype(x.dtype)
    return lax.dot_general(eye, x, (((1,), (1,)), ((), ())), preferred_element_type=jnp.float32)


def column(x, at):
    lane = lax.broadcasted_iota(jnp.int32, x.shape, 1)
    return jnp.sum(jnp.where(lane == at, x, 0.0), axis=1, keepdims=True)


halves = ((2, 3), (1, 0))
own_order = halves[0] + halves[1]


def pick(index, values):
    chosen = values[0]
    for i, value in enumerate(values):
        if i > 0 and value != values[0]:
            chosen = jnp.where(index == i, value, chosen)
    return chosen


def others(m, z):
    return [k for k in range(m) if k != z]


def joined(m, z, k):
    return z in (0, m - 1) and abs(k - z) > 1


def joins(m, z):
    if z == 1:
        return [(0, k) for k in range(m - 1, 1, -1)]
    if z == m - 2:
        return [(m - 1, k) for k in range(m - 2)]
    return []


def sum_order(m, z):
    far = sorted(others(m, z), key=lambda k: -abs(k - z))
    held = [k for _, k in joins(m, z)]
    first = [k for k in far if k in held or joined(m, z, k)]
    rest = [k for k in far if k not in first]
    ks = [(k, c) for c in range(3) for k in first] + [(k, c) for c in range(3) for k in rest + [z]]
    ks = [kc for kc in ks if kc[0] != z] + [kc for kc in ks if kc[0] == z]
    return [4 * k + c for k, c in ks]


def passed(m, z, k):
    return k == m - 1 and z == m - 3


def deferred(m, z, k):
    return (z == m - 1 and k == m - 2) or (z == m - 2 and k == m - 3)


def give_order(m, z):
    return sorted(others(m, z), key=lambda k: k - z if k > z else k)


def take_order(m, z):
    def rank(k):
        return z if k > z else z - k - 1, abs(k - z) > 1 and k < z, -k

    ks = sorted([k for k in others(m, z) if not passed(m, k, z) and not deferred(m, k, z)], key=rank)
    late = [k for k in others(m, z) if passed(m, k, z) or deferred(m, k, z)]
    return [4 * k + c for group in (ks, late) for half in halves for k in group for c in half]


def block_kernel(
    n, voxels_in, occupancy_in, row_weights_in, column_weights_in, depth_in, kernels_in, expand_in, shrink_in, updated,
    voxels, occupancy, row_weights, column_weights, depth_weights, plane_kernels, expand, shrink, load_s, fetch_s,
    part, rows_in, weights, wide, yz_out, row_sums, turned,
    pair_in, pair_sum, line_in, slab_in, slab_sum, yz_sum, yz_plane, yz_inner,
    row_other, row_slots, row_plane, row_inner, outs,
    pair_s, pair_r, line_s, line_r, slab_s, slab_r, halo_s, halo_r, row_s, row_r, core_s, core_r, spread_s, spread_r, cross_s, cross_r, known,
):
    me = lax.axis_index("gx")
    g = lax.axis_index("gy")
    m = n // 2
    a = me // 2
    b = me % 2
    count, chans, cols = part.shape
    rows = count // n
    bf = jnp.bfloat16
    f32 = jnp.float32
    partner = a * 2 + 1 - b

    def table(make):
        return [make(z) for z in range(m)]

    def feature_row(y):
        return voxels[y].astype(f32) * occupancy[pl.ds(y, 1), :].astype(f32)

    def piece(bb, aa):
        return bb * m + aa + bb * (m - 1 - 2 * aa)

    def owner(j):
        bb = j // m
        aa = j % m
        return (aa + bb * (m - 1 - 2 * aa)) * 2 + bb

    def offset(c):
        starts = [0, rows - reach, reach, 2 * reach]
        return starts[c] if isinstance(c, int) else pick(c, starts)

    def slice_of(bb, q):
        return pl.ds(piece(bb, q // 4) * rows + (q % 4) * reach, reach)

    def remote(src, dst, send, recv, gx, gy=None):
        target = {"gx": gx} if gy is None else {"gx": gx, "gy": gy}
        return pltpu.make_async_remote_copy(
            src_ref=src, dst_ref=dst, send_sem=send, recv_sem=recv, device_id=target, device_id_type=MESH
        )

    place = g * n + piece(b, a)
    last = 2 * n - 1
    before = jnp.maximum(place - 1, 0)
    after = jnp.minimum(place + 1, last)

    barrier = pltpu.get_barrier_semaphore()

    def greet(gx, gy):
        pl.semaphore_signal(barrier, inc=1, device_id={"gx": gx, "gy": gy}, device_id_type=MESH)

    lower = a > 0
    upper = a < m - 1
    slant = jnp.where(b == 0, lower, upper)
    seam_low = place == n - 1
    seam_high = place == n
    greet(partner, g)
    greet(me, 1 - g)
    pl.when(lower)(lambda: greet(jnp.maximum(me - 2, 0), g))
    pl.when(upper)(lambda: greet(jnp.minimum(me + 2, n - 1), g))
    pl.when(slant)(lambda: greet(jnp.clip(me + 2 * b - 1, 0, n - 1), g))
    pl.when(seam_low)(lambda: greet(owner(0), 1 - g))
    pl.when(seam_high)(lambda: greet(owner(n - 1), 1 - g))
    greeters = (
        2 + lower.astype(jnp.int32) + upper.astype(jnp.int32) + slant.astype(jnp.int32)
        + seam_low.astype(jnp.int32) + seam_high.astype(jnp.int32)
    )

    order = table(lambda z: sum_order(m, z))
    steps = 3 * m
    turns = [pick(a, [o[i] for o in order]) for i in range(steps)]

    small = [
        pltpu.make_async_copy(row_weights_in, row_weights, load_s.at[0]),
        pltpu.make_async_copy(occupancy_in, occupancy, load_s.at[1]),
    ]
    large = []
    for bb in (1 - b, b):
        for k in range(m):
            at = pl.ds(piece(bb, k) * rows, rows)
            large.append(pltpu.make_async_copy(voxels_in.at[at], voxels.at[at], load_s.at[2 + len(large)]))
    fetches = [
        pltpu.make_async_copy(kernels_in, plane_kernels, fetch_s.at[0]),
        pltpu.make_async_copy(column_weights_in, column_weights, fetch_s.at[1]),
        pltpu.make_async_copy(depth_in, depth_weights, fetch_s.at[2]),
        pltpu.make_async_copy(expand_in, expand, fetch_s.at[3]),
        pltpu.make_async_copy(shrink_in, shrink, fetch_s.at[4]),
    ]
    for copy in small + large + fetches:
        copy.start()

    for copy in small:
        copy.wait()
    rw = jnp.broadcast_to(row_weights[...].astype(f32), (chans, chans))
    rw = jnp.sum(rw * identity(chans), axis=1, keepdims=True)

    def yz_terms(j):
        for c in range(4):
            for r in range(reach):
                part[j * rows + c * reach + r] = (feature_row(j * rows + offset(c) + r) * rw).astype(bf)

    pair_copies = []
    for q in turns:
        pair_copies.append(remote(part.at[slice_of(1 - b, q)], pair_in.at[q], pair_s.at[0], pair_r.at[q], partner))

    def yz_pieces(bb):
        def some(k, carry):
            yz_terms(piece(bb, k))
            return carry

        lax.fori_loop(0, m, some, 0)

    for copy in large[:m]:
        copy.wait()
    yz_pieces(1 - b)

    def sent(buffer, size, sem, recv):
        return remote(buffer.at[pl.ds(0, size)], buffer.at[pl.ds(0, size)], sem.at[0], recv.at[0], partner)

    pair_all = sent(part, steps * reach, pair_s, pair_r)
    line_all = sent(pair_sum, steps - 3, line_s, line_r)
    slab_all = sent(part, 2 * (m - 1) * reach, slab_s, slab_r)
    cross_all = sent(yz_out, 4 * m * reach, cross_s, cross_r)
    slab_copies = []
    for dist in range(1, m):
        for side in (-1, 1):
            k = jnp.clip(a + side * dist, 0, m - 1)
            there = (a + side * dist >= 0) & (a + side * dist < m)
            for bb in range(2):
                copy = remote(
                    part.at[slice_of(bb, 4 * k + 3)], slab_in.at[2 * a + bb], slab_s.at[0], slab_r.at[2 * a + bb], k * 2 + b
                )
                slab_copies.append((dist, there, copy))

    def start_slabs(dist):
        for d, there, copy in slab_copies:
            if d == dist:
                pl.when(there)(copy.start)

    pl.semaphore_wait(barrier, greeters)
    for copy in pair_copies:
        copy.start()
    for copy in large[m:]:
        copy.wait()
    yz_pieces(b)
    start_slabs(1)

    def tell(level, side):
        step = 2 if side == 0 else -2
        pl.semaphore_signal(
            known.at[level, side], inc=1, device_id={"gx": jnp.clip(me - step, 0, n - 1), "gy": g}, device_id_type=MESH
        )

    def heard(level, side):
        return (a + level <= m - 1) if side == 0 else (a - level >= 0)

    def tells(level, side):
        return (lower if side == 0 else upper) & heard(level - 1, side)

    def tell_level(level):
        for side in range(2):
            if level > 2:
                pl.when(heard(level - 1, side))(lambda: pl.semaphore_wait(known.at[level - 1, side], 1))
            if level < m:
                pl.when(tells(level, side))(lambda: tell(level, side))

    tell_level(2)
    for level in range(3, m):
        tell_level(level)
        start_slabs(level - 1)

    for copy in fetches:
        copy.wait()
    turned[...] = flipped(column_weights[...])
    row_sums[...] = jnp.zeros(row_sums.shape, f32)
    lane = lax.broadcasted_iota(jnp.int32, (chans, cols), 1)

    group = 4
    share = count // (2 * m)

    def row_terms(first):
        depth = depth_weights[...].astype(f32)

        def some(step, carry):
            xy, xz = row_sums[0], row_sums[1]
            for k in range(group):
                y = first + step * group + k
                f = feature_row(y)
                xy = jnp.where(lane == g * count + y, jnp.sum(f * depth, axis=1, keepdims=True), xy)
                xz = xz + f * column(turned[...], y)
            row_sums[0] = xy
            row_sums[1] = xz
            return carry

        lax.fori_loop(0, share // group, some, 0)

    def flip_plane(p, layer):
        for off in range(3):
            taps = plane_kernels[p, layer, :, off].reshape(3 * chans, chans)
            weights[p, layer, off * chans : (off + 1) * chans, :] = flipped(taps).astype(bf)

    holds = table(lambda z: [k for _, k in joins(m, z)])
    holding = (a == 1) | (a == m - 2)

    def line_copy(i):
        gx, slot = [], []
        for z in range(m):
            k, c = order[z][i] // 4, order[z][i] % 4
            if k == z:
                gx.append(z)
                slot.append(0)
            elif joined(m, z, k):
                via = z + (1 if k > z else -1)
                gx.append(via)
                slot.append(4 * m + 4 * holds[via].index(k) + c)
            else:
                gx.append(k)
                slot.append(4 * z + c)
        to = pick(a, slot)
        q = turns[i]
        return remote(pair_sum.at[q], line_in.at[to], line_s.at[0], line_r.at[to], pick(a, gx) * 2 + b)

    line_copies = [line_copy(i) for i in range(steps - 3)]
    held = [pick(a, [int(order[z][i] // 4 in holds[z]) for z in range(m)]) for i in range(steps - 3)]

    def reduce_pair(i):
        q = turns[i]
        pair_copies[i].wait_recv()
        mine = part[slice_of(b, q)].astype(f32)
        pair_sum[q] = (mine + pair_in[q].astype(f32)).astype(bf)
        pl.when(held[i] == 0)(line_copies[i].start)

    def reduce_joined(i):
        @pl.when(holding)
        def _():
            q = turns[i]
            slot = 4 * m + pick(a, [4 * (holds[z].index(order[z][i] // 4) if holds[z] else 0) + order[z][i] % 4 for z in range(m)])
            remote(pair_sum.at[q], line_in.at[slot], line_s.at[0], line_r.at[slot], partner).wait_recv()
            pair_sum[q] = (pair_sum[q].astype(f32) + line_in[slot].astype(f32)).astype(bf)
            line_copies[i].start()

    def reduce_own(c):
        pair_copies[steps - 3 + c].wait_recv()
        q = 4 * a + c
        yz_sum[c] = part[slice_of(b, q)].astype(f32) + pair_in[q].astype(f32)

    def reduce_line(c):
        for i in range(m - 1):
            sources = [sorted(others(m, z), key=lambda s: (abs(s - z), s))[i] for z in range(m)]
            src = pick(a, sources)
            skip = pick(a, [int(joined(m, s, z)) for z, s in enumerate(sources)])

            @pl.when(skip == 0)
            def _():
                slot = 4 * src + c
                remote(pair_sum.at[slot], line_in.at[slot], line_s.at[0], line_r.at[slot], partner).wait_recv()
                yz_sum[c] = yz_sum[c] + line_in[slot].astype(f32)

    slab_cross = remote(slab_sum, pair_in.at[4 * a + 3], pair_s.at[1], pair_r.at[4 * a + 3], partner)

    def reduce_slab():
        q = 4 * a + 3
        total = [part[slice_of(bb, q)].astype(f32) for bb in (1 - b, b)]
        for i in range(m - 1):
            src = pick(a, [others(m, z)[i] for z in range(m)])
            for side, bb in enumerate((1 - b, b)):
                slot = 2 * src + bb
                remote(slab_in.at[slot], slab_in.at[slot], slab_s.at[0], slab_r.at[slot], partner).wait_recv()
                total[side] = total[side] + slab_in[slot].astype(f32)
        slab_sum[...] = total[0].astype(bf)
        slab_cross.start()
        yz_sum[3] = total[1]

    def reduce_slab_own():
        slab_cross.wait_recv()
        yz_sum[3] = yz_sum[3] + pair_in[4 * a + 3].astype(f32)

    for i in range(2):
        row_terms(i * share)
    tell_level(m)
    start_slabs(m - 1)
    for i in range(2, 2 * m):
        row_terms(i * share)
    rows_in[...] = row_sums[...].astype(bf)
    core = remote(rows_in.at[1 - g], row_other.at[...], core_s.at[0], core_r.at[0], me, 1 - g)
    core.start()
    flip_plane(2, 0)
    flip_plane(2, 1)

    first = 5
    for i in range(first):
        reduce_pair(i)
    merges = 3 * (m - 2)
    slab_at = steps - 3 - 1
    done = 0
    for i in range(first, steps - 3):
        if done < merges:
            reduce_joined(done)
            done += 1
        reduce_pair(i)
    reduce_slab()
    core.wait_recv()
    mid = rows_in[g].astype(f32) + row_other[...].astype(f32)
    row_slots[reach] = mid.astype(bf)
    row_copies = []
    for dx in range(-reach, reach + 1):
        if dx != 0:
            slot = reach - dx
            copy = remote(
                row_slots.at[reach], row_slots.at[slot], row_s.at[slot], row_r.at[slot], jnp.clip(me + dx, 0, n - 1)
            )
            row_copies.append((dx, copy))
            pl.when((me + dx >= 0) & (me + dx < n))(copy.start)
    while done < merges:
        reduce_joined(done)
        done += 1
    for layer in range(2):
        flip_plane(g, layer)
    wide[...] = flipped(expand[...]).astype(bf)

    edge = reach * chans
    halo = [
        (place > 0, place < last, remote(
            yz_plane.at[pl.ds(edge, edge)], yz_plane.at[pl.ds(edge + rows * chans, edge)],
            halo_s.at[0], halo_r.at[0], owner(before % n), before // n,
        )),
        (place < last, place > 0, remote(
            yz_plane.at[pl.ds(rows * chans, edge)], yz_plane.at[pl.ds(0, edge)],
            halo_s.at[1], halo_r.at[1], owner(after % n), after // n,
        )),
    ]

    @pl.when(place == 0)
    def _():
        yz_plane[pl.ds(0, edge), :] = jnp.zeros((edge, cols), bf)

    @pl.when(place == last)
    def _():
        yz_plane[pl.ds(edge + rows * chans, edge), :] = jnp.zeros((edge, cols), bf)

    def settle(c):
        for r in range(reach):
            at = (reach + offset(c) + r) * chans
            yz_plane[at : at + chans, :] = yz_sum[c, r].astype(bf)

    def inner_row(i, keep):
        inner = silu(conv_row(yz_plane[i * chans : (i + 3) * chans, :], weights[2, 0])) * keep
        yz_inner[i * chans : (i + 1) * chans, :] = inner.astype(bf)

    for c in range(2):
        reduce_own(c)
    for c in range(2):
        reduce_line(c)
        settle(c)
        pl.when(halo[c][0])(halo[c][2].start)
    reduce_own(2)
    reduce_slab_own()
    settle(3)
    for i in range(rows - reach, rows):
        inner_row(i, 1.0)
    reduce_line(2)
    settle(2)

    spread_copies = []
    own = piece(b, a)

    def cross_copy(bb, q):
        at = slice_of(bb, q)
        return remote(yz_out.at[at], yz_out.at[at], cross_s.at[0], cross_r.at[q], partner)

    def give_half(half):
        for c in half:
            for r in range(reach):
                at = (offset(c) + r) * chans
                done = conv_row(yz_inner[at : at + 3 * chans, :], weights[2, 1])
                yz_out[own * rows + c * reach + r] = done.astype(bf)
        for c in half:
            cross_copy(b, 4 * a + c).start()
        later = table(lambda z: [deferred(m, z, k) for k in give_order(m, z)])
        for turn, i, part_of in [(0, i, half) for i in range(1)] + [(1, i, halves[0]) for i in range(m - 1)] + [(2, i, half) for i in range(1, m - 1)]:
            first_half = half is halves[0]
            if turn == 1 and (first_half or not any(x[i] for x in later)):
                continue
            k = pick(a, [give_order(m, z)[i] for z in range(m)])
            go = [not passed(m, z, give_order(m, z)[i]) for z in range(m)]
            if turn == 1:
                go = [x and later[z][i] for z, x in enumerate(go)]
            elif first_half:
                go = [x and not later[z][i] for z, x in enumerate(go)]
            going = pick(a, [int(x) for x in go])
            for c in part_of:
                q = 4 * a + c
                at = slice_of(b, q)
                copy = remote(yz_out.at[at], yz_out.at[at], spread_s.at[4 * i + c], spread_r.at[q], k * 2 + b)
                pl.when(going == 1)(copy.start)
                spread_copies.append((going == 1, copy))

    for i in range(reach, rows - reach):
        inner_row(i, 1.0)
    give_half(halves[0])
    for dx, copy in row_copies:
        pl.when((me - dx >= 0) & (me - dx < n))(copy.wait_recv)
    for s in range(2 * reach + 1):
        at = me + s - reach
        inside = (at >= 0) & (at < n)
        here = pl.ds(s * chans, chans)

        @pl.when(inside)
        def _():
            row_plane[here, :] = row_slots[s]

        @pl.when(jnp.logical_not(inside))
        def _():
            row_plane[here, :] = jnp.zeros((chans, cols), bf)

    for s in range(3):
        at = me + s - 1
        keep = ((at >= 0) & (at < n)).astype(f32)
        inner = silu(conv_row(row_plane[s * chans : (s + 3) * chans, :], weights[g, 0]))
        row_inner[s * chans : (s + 1) * chans, :] = (inner * keep).astype(bf)
    outs[g] = conv_row(row_inner[...], weights[g, 1]).astype(bf)
    share_out = remote(outs.at[g], outs.at[g], core_s.at[1], core_r.at[1], me, 1 - g)
    share_out.start()
    for _, receives, copy in halo:
        pl.when(receives)(copy.wait_recv)
    inner_row(rows, 1.0)
    inner_row(rows + 1, (place < last).astype(f32))
    inner_row(0, (place > 0).astype(f32))
    inner_row(1, 1.0)
    give_half(halves[1])
    remote(outs.at[1 - g], outs.at[1 - g], core_s.at[1], core_r.at[1], me, 1 - g).wait_recv()

    def finish(*chunks):
        xy_out = outs[0].astype(f32)
        xz_out = outs[1].astype(f32)
        at = []
        for bb, q in chunks:
            c = q % 4
            stored = piece(bb, q // 4) * rows + c * reach
            first = piece(bb, q // 4) * rows + offset(c)
            at += [(stored + r, first + r) for r in range(reach)]
        mixed = []
        for s, y in at:
            product = column(xy_out, g * count + y) * xz_out
            product = product * yz_out[s].astype(f32)
            mixed.append((product_scale * product).astype(bf))
        mixed = jnp.concatenate(mixed, axis=1)
        hidden = silu(jnp.dot(wide[...], mixed, preferred_element_type=f32)).astype(bf)
        branch = jnp.dot(shrink[...], hidden, preferred_element_type=f32)
        for k, (s, y) in enumerate(at):
            updated[y] = (feature_row(y) + branch[:, k * cols : (k + 1) * cols]).astype(bf)

    takes = [pick(a, [take_order(m, z)[i] for z in range(m)]) for i in range(4 * m - 4)]
    hands = a == m - 2
    handed = max(m - 3, 0)

    def hand_copy(q):
        at = slice_of(b, q)
        return remote(yz_out.at[at], yz_out.at[at], spread_s.at[4 * (m - 1) + q % 4], spread_r.at[q], (m - 1) * 2 + b)

    def take(i):
        q = takes[i]
        at = slice_of(b, q)
        remote(yz_out.at[at], yz_out.at[at], spread_s.at[0], spread_r.at[q], partner).wait_recv()
        cross_copy(b, q).start()
        pl.when(hands & (q // 4 == handed))(hand_copy(q).start)
        return b, q

    crossed = [4 * a + c for c in own_order] + takes

    def take_crossed(i):
        q = crossed[i]
        cross_copy(1 - b, q).wait_recv()
        return 1 - b, q

    finish(*[(b, 4 * a + c) for c in own_order])

    def drain():
        pair_all.wait_send()
        slab_cross.wait_send()
        line_all.wait_send()
        slab_all.wait_send()
        for sends, _, copy in halo:
            pl.when(sends)(copy.wait_send)
        core.wait_send()
        share_out.wait_send()
        for dx, copy in row_copies:
            pl.when((me + dx >= 0) & (me + dx < n))(copy.wait_send)

    pair = 2
    lag = 2
    for i in range(0, len(takes), pair):
        ready = [take(j) for j in range(i, i + pair)]
        ready += [take_crossed(j) for j in range(i - lag * pair, i - lag * pair + pair) if j >= 0]
        finish(*ready)
        if i == 2 * pair:
            drain()
    at = len(takes) - lag * pair
    for size in (4, 2, 2):
        size = min(size, len(crossed) - at)
        if size > 0:
            finish(*[take_crossed(at + j) for j in range(size)])
            at += size
        if at == len(crossed) - 2:
            for given, copy in spread_copies:
                pl.when(given)(copy.wait_send)
            for c in range(4):
                pl.when(hands)(hand_copy(4 * handed + c).wait_send)
    while at < len(crossed):
        finish(take_crossed(at))
        at += 1
    cross_all.wait_send()


def fused(voxels, occupancy, row_weights, column_weights, depth_weights, plane_kernels, expand_weight, shrink_weight):
    n = lax.axis_size("gx")
    m = n // 2
    count, cols, chans = voxels.shape[1:]
    rows = count // n
    sets, layers = plane_kernels.shape[:2]
    planes = 2
    span = 2 * reach + 1
    bf = jnp.bfloat16
    f32 = jnp.float32
    dma = pltpu.SemaphoreType.DMA
    operands = (
        voxels[0].transpose(0, 2, 1),
        occupancy[0],
        row_weights,
        column_weights,
        depth_weights.T,
        plane_kernels,
        expand_weight,
        shrink_weight.T,
    )
    updated = pl.pallas_call(
        functools.partial(block_kernel, n),
        out_shape=pltpu.VMEM((count, chans, cols), bf),
        in_specs=[pl.BlockSpec(memory_space=pl.ANY) for _ in operands],
        out_specs=pl.BlockSpec(memory_space=pltpu.VMEM),
        scratch_shapes=[pltpu.VMEM(x.shape, x.dtype) for x in operands]
        + [
            dma((2 + n,)),
            dma((5,)),
            pltpu.VMEM((count, chans, cols), bf),
            pltpu.VMEM((planes, chans, cols), bf),
            pltpu.VMEM((sets, layers, 3 * chans, 3 * chans), bf),
            pltpu.VMEM(expand_weight.shape[::-1], bf),
            pltpu.VMEM((count, chans, cols), bf),
            pltpu.VMEM((planes, chans, cols), f32),
            pltpu.VMEM((chans, count), f32),
            pltpu.VMEM((4 * m, reach, chans, cols), bf),
            pltpu.VMEM((4 * m, reach, chans, cols), bf),
            pltpu.VMEM((8 * m, reach, chans, cols), bf),
            pltpu.VMEM((2 * m, reach, chans, cols), bf),
            pltpu.VMEM((reach, chans, cols), bf),
            pltpu.VMEM((4, reach, chans, cols), f32),
            pltpu.VMEM(((rows + 4) * chans, cols), bf),
            pltpu.VMEM(((rows + 2) * chans, cols), bf),
            pltpu.VMEM((chans, cols), bf),
            pltpu.VMEM((span, chans, cols), bf),
            pltpu.VMEM((span * chans, cols), bf),
            pltpu.VMEM((3 * chans, cols), bf),
            pltpu.VMEM((planes, chans, cols), bf),
            dma((2,)), dma((4 * m,)), dma((1,)), dma((8 * m,)), dma((1,)), dma((2 * m,)), dma((2,)), dma((2,)),
            dma((span,)), dma((span,)), dma((2,)), dma((2,)),
            dma((4 * m,)), dma((4 * m,)), dma((1,)), dma((4 * m,)),
            pltpu.SemaphoreType.REGULAR((m, 2)),
        ],
        compiler_params=pltpu.CompilerParams(collective_id=0, has_side_effects=True),
    )(*operands)
    return updated.transpose(0, 2, 1)[None]


def fits(voxels):
    n = lax.axis_size("gx")
    sides = lax.axis_size("gy")
    xs, ys, zs, _ = voxels.shape
    return xs == 1 and sides == 2 and n % 2 == 0 and n >= 8 and ys == n * 4 * reach and 2 * ys == zs


def plain_planes(features, row_weights, column_weights, depth_weights, plane_kernels):
    xy_plane = jnp.einsum(
        "xyzc,zc->xyc", features, depth_weights, preferred_element_type=jnp.float32
    ).astype(jnp.bfloat16)
    xz_part = jnp.einsum(
        "xyzc,yc->xzc", features, column_weights, preferred_element_type=jnp.float32
    )
    yz_part = jnp.einsum("xyzc,xc->yzc", features, row_weights, preferred_element_type=jnp.float32)
    xy_out = plane_block(xy_plane, plane_kernels[0], rim_xy)
    xz_plane = lax.psum(xz_part, "gy").astype(jnp.bfloat16)
    xz_out = plane_block(xz_plane, plane_kernels[1], rim_xz)
    yz_plane = lax.psum(yz_part, "gx").astype(jnp.bfloat16)
    yz_out = plane_block(yz_plane, plane_kernels[2], rim_yz)
    return xy_out, xz_out, yz_out


def shards(
    voxels,
    occupancy,
    row_weights,
    column_weights,
    depth_weights,
    plane_kernels,
    expand_weight,
    shrink_weight,
):
    if fits(voxels):
        return fused(
            voxels,
            occupancy,
            row_weights,
            column_weights,
            depth_weights,
            plane_kernels,
            expand_weight,
            shrink_weight,
        )
    features = voxels * occupancy.astype(jnp.bfloat16)[..., None]
    xy_out, xz_out, yz_out = plain_planes(features, row_weights, column_weights, depth_weights, plane_kernels)
    product = xy_out.astype(jnp.float32)[:, :, None, :] * xz_out.astype(jnp.float32)[:, None, :, :]
    product = product * yz_out.astype(jnp.float32)[None, :, :, :]
    mixed = (product_scale * product).astype(jnp.bfloat16)
    hidden = jax.nn.silu(
        jnp.einsum("xyzc,ch->xyzh", mixed, expand_weight, preferred_element_type=jnp.float32)
    ).astype(jnp.bfloat16)
    branch = jnp.einsum("xyzh,hc->xyzc", hidden, shrink_weight, preferred_element_type=jnp.float32)
    return (features.astype(jnp.float32) + branch).astype(jnp.bfloat16)


def solution(mesh):
    in_specs = (
        P(("groups", "gx"), "gy", None, None),
        P(("groups", "gx"), "gy", None),
        P("gx", None),
        P("gy", None),
        P(),
        P(),
        P(),
        P(),
    )
    out_specs = P(("groups", "gx"), "gy", None, None)
    return jax.shard_map(shards, mesh=mesh, in_specs=in_specs, out_specs=out_specs, check_vma=False)
```

```python
import functools

import jax
import jax.numpy as jnp
from jax import lax
from jax.experimental import pallas as pl
from jax.experimental.pallas import tpu as pltpu
from jax.sharding import PartitionSpec as P

MESH = pl.DeviceIdType.MESH
reach = 2

product_scale = 8.0


def with_halo(cells, sides, width):
    for axis, dim in sides:
        count = lax.axis_size(axis)
        ends = count - 1
        head = lax.slice_in_dim(cells, 0, width, axis=dim)
        tail = lax.slice_in_dim(cells, cells.shape[dim] - width, cells.shape[dim], axis=dim)
        cells = jnp.concatenate(
            [
                lax.ppermute(tail, axis, [(i, (i + 1) % count) for i in range(ends)]),
                cells,
                lax.ppermute(head, axis, [((i + 1) % count, i) for i in range(ends)]),
            ],
            axis=dim,
        )
    return cells


def conv_valid(padded, kernel):
    rows = padded.shape[0] - 2
    cols = padded.shape[1] - 2
    total = jnp.zeros((rows, cols, kernel.shape[-1]), jnp.float32)
    for row_off in range(3):
        for col_off in range(3):
            window = padded[row_off : row_off + rows, col_off : col_off + cols]
            total = total + jnp.einsum(
                "ijc,co->ijo", window, kernel[row_off, col_off], preferred_element_type=jnp.float32
            )
    return total


def plane_block(plane, kernels, extend):
    inner = jax.nn.silu(conv_valid(extend(plane), kernels[0])).astype(jnp.bfloat16)
    return conv_valid(extend(inner), kernels[1]).astype(jnp.bfloat16)


def rim_xy(plane):
    return with_halo(plane, (("gx", 0), ("gy", 1)), 1)


def rim_xz(plane):
    padded = with_halo(plane, (("gx", 0),), 1)
    return jnp.pad(padded, ((0, 0), (1, 1), (0, 0)))


def rim_yz(plane):
    padded = with_halo(plane, (("gy", 0),), 1)
    return jnp.pad(padded, ((0, 0), (1, 1), (0, 0)))


def conv_row(window, weight):
    taps = jnp.dot(weight, window, preferred_element_type=jnp.float32)
    chans = taps.shape[0] // 3
    cols = taps.shape[1]
    lane = lax.broadcasted_iota(jnp.int32, (chans, cols), 1)
    left = pltpu.roll(taps[:chans], 1, 1)
    right = pltpu.roll(taps[2 * chans :], cols - 1, 1)
    left = jnp.where(lane == 0, 0.0, left)
    right = jnp.where(lane == cols - 1, 0.0, right)
    return taps[chans : 2 * chans] + left + right


def silu(v):
    half = 0.5 * v
    return half + half * jnp.tanh(half)


def identity(size):
    row = lax.broadcasted_iota(jnp.int32, (size, size), 0)
    col = lax.broadcasted_iota(jnp.int32, (size, size), 1)
    return jnp.where(row == col, 1.0, 0.0)


def flipped(x):
    eye = identity(x.shape[1]).astype(x.dtype)
    return lax.dot_general(eye, x, (((1,), (1,)), ((), ())), preferred_element_type=jnp.float32)


def column(x, at):
    lane = lax.broadcasted_iota(jnp.int32, x.shape, 1)
    return jnp.sum(jnp.where(lane == at, x, 0.0), axis=1, keepdims=True)


halves = ((2, 3), (1, 0))
own_order = halves[0] + halves[1]


def pick(index, values):
    chosen = values[0]
    for i, value in enumerate(values):
        if i > 0 and value != values[0]:
            chosen = jnp.where(index == i, value, chosen)
    return chosen


def others(m, z):
    return [k for k in range(m) if k != z]


def joined(m, z, k):
    return z in (0, m - 1) and abs(k - z) > 1


def joins(m, z):
    if z == 1:
        return [(0, k) for k in range(m - 1, 1, -1)]
    if z == m - 2:
        return [(m - 1, k) for k in range(m - 2)]
    return []


def sum_order(m, z):
    far = sorted(others(m, z), key=lambda k: -abs(k - z))
    held = [k for _, k in joins(m, z)]
    first = [k for k in far if k in held or joined(m, z, k)]
    rest = [k for k in far if k not in first]
    ks = [(k, c) for c in range(3) for k in first] + [(k, c) for c in range(3) for k in rest + [z]]
    ks = [kc for kc in ks if kc[0] != z] + [kc for kc in ks if kc[0] == z]
    return [4 * k + c for k, c in ks]


def passed(m, z, k):
    return k == m - 1 and z == m - 3


def deferred(m, z, k):
    return (z == m - 1 and k == m - 2) or (z == m - 2 and k == m - 3)


def give_order(m, z):
    return sorted(others(m, z), key=lambda k: k - z if k > z else k)


def take_order(m, z):
    def rank(k):
        return z if k > z else z - k - 1, abs(k - z) > 1 and k < z, -k

    ks = sorted([k for k in others(m, z) if not passed(m, k, z) and not deferred(m, k, z)], key=rank)
    if m == 4 and z == 0:
        return [14, 15, 10, 11, 6, 7, 13, 5, 12, 4, 9, 8]
    if m == 4 and z == 1 and []:
        return []
    late = [k for k in others(m, z) if passed(m, k, z) or deferred(m, k, z)]
    return [4 * k + c for group in (ks, late) for half in halves for k in group for c in half]


def diverted(z, q):
    return z == 0 and q in [4 + c for c in halves[0]]


def cross_order(m, z):
    chunks = [4 * z + c for c in own_order] + take_order(m, z)
    late = [q for q in chunks if diverted(z, q)]
    chunks = [q for q in chunks if q not in late]
    if late:
        chunks[-2:-2] = late
    return chunks


def block_kernel(
    n, voxels_in, occupancy_in, row_weights_in, column_weights_in, depth_in, kernels_in, expand_in, shrink_in, updated,
    voxels, occupancy, row_weights, column_weights, depth_weights, plane_kernels, expand, shrink, load_s, fetch_s,
    part, rows_in, weights, wide, yz_out, row_sums, turned,
    pair_in, pair_sum, line_in, slab_in, slab_sum, yz_sum, yz_plane, yz_inner,
    row_other, row_slots, row_plane, row_inner, outs,
    pair_s, pair_r, line_s, line_r, slab_s, slab_r, halo_s, halo_r, row_s, row_r, core_s, core_r, spread_s, spread_r, cross_s, cross_r, divert_s, known,
):
    me = lax.axis_index("gx")
    g = lax.axis_index("gy")
    m = n // 2
    a = me // 2
    b = me % 2
    count, chans, cols = part.shape
    rows = count // n
    bf = jnp.bfloat16
    f32 = jnp.float32
    partner = a * 2 + 1 - b

    def table(make):
        return [make(z) for z in range(m)]

    def feature_row(y):
        return voxels[y].astype(f32) * occupancy[pl.ds(y, 1), :].astype(f32)

    def piece(bb, aa):
        return bb * m + aa + bb * (m - 1 - 2 * aa)

    def owner(j):
        bb = j // m
        aa = j % m
        return (aa + bb * (m - 1 - 2 * aa)) * 2 + bb

    def offset(c):
        starts = [0, rows - reach, reach, 2 * reach]
        return starts[c] if isinstance(c, int) else pick(c, starts)

    def slice_of(bb, q):
        return pl.ds(piece(bb, q // 4) * rows + (q % 4) * reach, reach)

    def remote(src, dst, send, recv, gx, gy=None):
        target = {"gx": gx} if gy is None else {"gx": gx, "gy": gy}
        return pltpu.make_async_remote_copy(
            src_ref=src, dst_ref=dst, send_sem=send, recv_sem=recv, device_id=target, device_id_type=MESH
        )

    place = g * n + piece(b, a)
    last = 2 * n - 1
    before = jnp.maximum(place - 1, 0)
    after = jnp.minimum(place + 1, last)

    barrier = pltpu.get_barrier_semaphore()

    def greet(gx, gy):
        pl.semaphore_signal(barrier, inc=1, device_id={"gx": gx, "gy": gy}, device_id_type=MESH)

    lower = a > 0
    upper = a < m - 1
    slant = jnp.where(b == 0, lower, upper)
    seam_low = place == n - 1
    seam_high = place == n
    greet(partner, g)
    greet(me, 1 - g)
    pl.when(lower)(lambda: greet(jnp.maximum(me - 2, 0), g))
    pl.when(upper)(lambda: greet(jnp.minimum(me + 2, n - 1), g))
    pl.when(slant)(lambda: greet(jnp.clip(me + 2 * b - 1, 0, n - 1), g))
    pl.when(seam_low)(lambda: greet(owner(0), 1 - g))
    pl.when(seam_high)(lambda: greet(owner(n - 1), 1 - g))
    greeters = (
        2 + lower.astype(jnp.int32) + upper.astype(jnp.int32) + slant.astype(jnp.int32)
        + seam_low.astype(jnp.int32) + seam_high.astype(jnp.int32)
    )

    order = table(lambda z: sum_order(m, z))
    steps = 3 * m
    turns = [pick(a, [o[i] for o in order]) for i in range(steps)]

    small = [
        pltpu.make_async_copy(row_weights_in, row_weights, load_s.at[0]),
        pltpu.make_async_copy(occupancy_in, occupancy, load_s.at[1]),
    ]
    large = []
    for bb in (1 - b, b):
        for k in range(m):
            at = pl.ds(piece(bb, k) * rows, rows)
            large.append(pltpu.make_async_copy(voxels_in.at[at], voxels.at[at], load_s.at[2 + len(large) // m]))
    fetches = [
        pltpu.make_async_copy(kernels_in, plane_kernels, fetch_s.at[0]),
        pltpu.make_async_copy(column_weights_in, column_weights, fetch_s.at[1]),
        pltpu.make_async_copy(depth_in, depth_weights, fetch_s.at[2]),
        pltpu.make_async_copy(expand_in, expand, fetch_s.at[3]),
        pltpu.make_async_copy(shrink_in, shrink, fetch_s.at[4]),
    ]
    for copy in small + large + fetches:
        copy.start()

    for copy in small:
        copy.wait()
    rw = jnp.broadcast_to(row_weights[...].astype(f32), (chans, chans))
    rw = jnp.sum(rw * identity(chans), axis=1, keepdims=True)

    def yz_terms(j):
        for c in range(4):
            for r in range(reach):
                part[j * rows + c * reach + r] = (feature_row(j * rows + offset(c) + r) * rw).astype(bf)

    pair_copies = []
    for i, q in enumerate(turns):
        pair_copies.append(remote(part.at[slice_of(1 - b, q)], pair_in.at[q], pair_s.at[0], pair_r.at[i], partner))

    def yz_pieces(bb):
        def some(k, carry):
            yz_terms(piece(bb, k))
            return carry

        lax.fori_loop(0, m, some, 0)

    def loaded(which):
        at = pl.ds(0, m * rows)
        pltpu.make_async_copy(voxels_in.at[at], voxels.at[at], load_s.at[2 + which]).wait()

    loaded(0)
    yz_pieces(1 - b)

    def sent(buffer, size, sem, recv):
        return remote(buffer.at[pl.ds(0, size)], buffer.at[pl.ds(0, size)], sem.at[0], recv.at[0], partner)

    pair_all = sent(part, steps * reach, pair_s, pair_r)
    line_all = sent(pair_sum, steps - 3, line_s, line_r)
    slab_all = sent(part, 2 * (m - 1) * reach, slab_s, slab_r)
    cross_all = sent(yz_out, 4 * m * reach, cross_s, cross_r)
    slab_copies = []
    for dist in range(1, m):
        for side in (-1, 1):
            k = jnp.clip(a + side * dist, 0, m - 1)
            there = (a + side * dist >= 0) & (a + side * dist < m)
            for bb in range(2):
                copy = remote(
                    part.at[slice_of(bb, 4 * k + 3)], slab_in.at[2 * a + bb], slab_s.at[0], slab_r.at[0], k * 2 + b
                )
                slab_copies.append((dist, there, copy))

    def start_slabs(dist):
        for d, there, copy in slab_copies:
            if d == dist:
                pl.when(there)(copy.start)

    pl.semaphore_wait(barrier, greeters)
    for copy in pair_copies:
        copy.start()
    loaded(1)
    yz_pieces(b)
    start_slabs(1)

    def tell(level, side):
        step = 2 if side == 0 else -2
        pl.semaphore_signal(
            known.at[level - 2, side], inc=1, device_id={"gx": jnp.clip(me - step, 0, n - 1), "gy": g}, device_id_type=MESH
        )

    def heard(level, side):
        return (a + level <= m - 1) if side == 0 else (a - level >= 0)

    def tells(level, side):
        return (lower if side == 0 else upper) & heard(level - 1, side)

    def tell_level(level):
        for side in range(2):
            if level > 2:
                pl.when(heard(level - 1, side))(lambda: pl.semaphore_wait(known.at[level - 3, side], 1))
            if level < m:
                pl.when(tells(level, side))(lambda: tell(level, side))

    tell_level(2)
    for level in range(3, m):
        tell_level(level)
        start_slabs(level - 1)

    for copy in fetches:
        copy.wait()
    turned[...] = flipped(column_weights[...])
    row_sums[...] = jnp.zeros(row_sums.shape, f32)
    lane = lax.broadcasted_iota(jnp.int32, (chans, cols), 1)

    group = 4
    share = count // (2 * m)

    def row_terms(first):
        depth = depth_weights[...].astype(f32)

        def some(step, carry):
            xy, xz = row_sums[0], row_sums[1]
            for k in range(group):
                y = first + step * group + k
                f = feature_row(y)
                xy = jnp.where(lane == g * count + y, jnp.sum(f * depth, axis=1, keepdims=True), xy)
                xz = xz + f * column(turned[...], y)
            row_sums[0] = xy
            row_sums[1] = xz
            return carry

        lax.fori_loop(0, share // group, some, 0)

    def flip_plane(p, layer):
        for off in range(3):
            taps = plane_kernels[p, layer, :, off].reshape(3 * chans, chans)
            weights[p, layer, off * chans : (off + 1) * chans, :] = flipped(taps).astype(bf)

    holds = table(lambda z: [k for _, k in joins(m, z)])
    holding = (a == 1) | (a == m - 2)

    def line_copy(i):
        gx, slot = [], []
        for z in range(m):
            k, c = order[z][i] // 4, order[z][i] % 4
            if k == z:
                gx.append(z)
                slot.append(0)
            elif joined(m, z, k):
                via = z + (1 if k > z else -1)
                gx.append(via)
                slot.append(3 * m + 3 * holds[via].index(k) + c)
            else:
                gx.append(k)
                slot.append(3 * z + c)
        to = pick(a, slot)
        q = turns[i]
        return remote(pair_sum.at[q], line_in.at[to], line_s.at[0], line_r.at[to], pick(a, gx) * 2 + b)

    line_copies = [line_copy(i) for i in range(steps - 3)]
    held = [pick(a, [int(order[z][i] // 4 in holds[z]) for z in range(m)]) for i in range(steps - 3)]

    def reduce_pair(i):
        q = turns[i]
        pair_copies[i].wait_recv()
        mine = part[slice_of(b, q)].astype(f32)
        pair_sum[q] = (mine + pair_in[q].astype(f32)).astype(bf)
        pl.when(held[i] == 0)(line_copies[i].start)

    def reduce_joined(i):
        @pl.when(holding)
        def _():
            q = turns[i]
            slot = 3 * m + pick(a, [3 * (holds[z].index(order[z][i] // 4) if holds[z] else 0) + order[z][i] % 4 for z in range(m)])
            remote(pair_sum.at[q], line_in.at[slot], line_s.at[0], line_r.at[slot], partner).wait_recv()
            pair_sum[q] = (pair_sum[q].astype(f32) + line_in[slot].astype(f32)).astype(bf)
            line_copies[i].start()

    def reduce_own(c):
        pair_copies[steps - 3 + c].wait_recv()
        q = 4 * a + c
        yz_sum[c] = part[slice_of(b, q)].astype(f32) + pair_in[q].astype(f32)

    def reduce_line(c):
        for i in range(m - 1):
            sources = [sorted(others(m, z), key=lambda s: (abs(s - z), s))[i] for z in range(m)]
            src = pick(a, sources)
            skip = pick(a, [int(joined(m, s, z)) for z, s in enumerate(sources)])

            @pl.when(skip == 0)
            def _():
                slot = 3 * src + c
                remote(pair_sum.at[slot], line_in.at[slot], line_s.at[0], line_r.at[slot], partner).wait_recv()
                yz_sum[c] = yz_sum[c] + line_in[slot].astype(f32)

    slab_cross = remote(slab_sum, pair_in.at[4 * a + 3], pair_s.at[1], pair_r.at[steps], partner)

    def reduce_slab():
        q = 4 * a + 3
        total = [part[slice_of(bb, q)].astype(f32) for bb in (1 - b, b)]
        sent(slab_in, 2 * (m - 1), slab_s, slab_r).wait_recv()
        for i in range(m - 1):
            src = pick(a, [others(m, z)[i] for z in range(m)])
            for side, bb in enumerate((1 - b, b)):
                slot = 2 * src + bb
                total[side] = total[side] + slab_in[slot].astype(f32)
        slab_sum[...] = total[0].astype(bf)
        slab_cross.start()
        yz_sum[3] = total[1]

    def reduce_slab_own():
        slab_cross.wait_recv()
        yz_sum[3] = yz_sum[3] + pair_in[4 * a + 3].astype(f32)

    for i in range(2):
        row_terms(i * share)
    tell_level(m)
    start_slabs(m - 1)
    for i in range(2, 2 * m):
        row_terms(i * share)
    rows_in[...] = row_sums[...].astype(bf)
    core = remote(rows_in.at[1 - g], row_other.at[...], core_s.at[0], core_r.at[0], me, 1 - g)
    core.start()
    flip_plane(2, 0)
    flip_plane(2, 1)

    first = 5
    for i in range(first):
        reduce_pair(i)
    merges = 3 * (m - 2)
    slab_at = steps - 3 - 1
    done = 0
    for i in range(first, steps - 3):
        if done < merges:
            reduce_joined(done)
            done += 1
        reduce_pair(i)
    reduce_slab()
    core.wait_recv()
    mid = rows_in[g].astype(f32) + row_other[...].astype(f32)
    row_slots[reach] = mid.astype(bf)
    row_copies = []
    for dx in range(-reach, reach + 1):
        if dx != 0:
            slot = reach - dx
            copy = remote(
                row_slots.at[reach], row_slots.at[slot], row_s.at[0], row_r.at[0], jnp.clip(me + dx, 0, n - 1)
            )
            row_copies.append((dx, copy))
            pl.when((me + dx >= 0) & (me + dx < n))(copy.start)
    while done < merges:
        reduce_joined(done)
        done += 1
    for layer in range(2):
        flip_plane(g, layer)
    wide[...] = flipped(expand[...]).astype(bf)

    edge = reach * chans
    halo = [
        (place > 0, place < last, remote(
            yz_plane.at[pl.ds(edge, edge)], yz_plane.at[pl.ds(edge + rows * chans, edge)],
            halo_s.at[0], halo_r.at[0], owner(before % n), before // n,
        )),
        (place < last, place > 0, remote(
            yz_plane.at[pl.ds(rows * chans, edge)], yz_plane.at[pl.ds(0, edge)],
            halo_s.at[1], halo_r.at[1], owner(after % n), after // n,
        )),
    ]

    @pl.when(place == 0)
    def _():
        yz_plane[pl.ds(0, edge), :] = jnp.zeros((edge, cols), bf)

    @pl.when(place == last)
    def _():
        yz_plane[pl.ds(edge + rows * chans, edge), :] = jnp.zeros((edge, cols), bf)

    def settle(c):
        for r in range(reach):
            at = (reach + offset(c) + r) * chans
            yz_plane[at : at + chans, :] = yz_sum[c, r].astype(bf)

    def inner_row(i, keep):
        inner = silu(conv_row(yz_plane[i * chans : (i + 3) * chans, :], weights[2, 0])) * keep
        yz_inner[i * chans : (i + 1) * chans, :] = inner.astype(bf)

    for c in range(2):
        reduce_own(c)
    for c in range(2):
        reduce_line(c)
        settle(c)
        pl.when(halo[c][0])(halo[c][2].start)
    reduce_own(2)
    reduce_slab_own()
    settle(3)
    for i in range(rows - reach, rows):
        inner_row(i, 1.0)
    reduce_line(2)
    settle(2)

    spread_copies = []
    own = piece(b, a)

    def cross_copy(bb, q, pair_at):
        at = slice_of(bb, q)
        return remote(yz_out.at[at], yz_out.at[at], cross_s.at[0], cross_r.at[pair_at], partner)

    def give_half(half):
        for c in half:
            for r in range(reach):
                at = (offset(c) + r) * chans
                done = conv_row(yz_inner[at : at + 3 * chans, :], weights[2, 1])
                yz_out[own * rows + c * reach + r] = done.astype(bf)
        for c in half:
            cross_copy(b, 4 * a + c, own_order.index(c) // 2).start()
        later = table(lambda z: [deferred(m, z, k) for k in give_order(m, z)])
        for turn, i, part_of in [(0, i, half) for i in range(1)] + [(1, i, halves[0]) for i in range(m - 1)] + [(2, i, half) for i in range(1, m - 1)]:
            first_half = half is halves[0]
            if turn == 1 and (first_half or not any(x[i] for x in later)):
                continue
            k = pick(a, [give_order(m, z)[i] for z in range(m)])
            go = [not passed(m, z, give_order(m, z)[i]) for z in range(m)]
            if turn == 1:
                go = [x and later[z][i] for z, x in enumerate(go)]
            elif first_half:
                go = [x and not later[z][i] for z, x in enumerate(go)]
            going = pick(a, [int(x) for x in go])
            for c in part_of:
                q = 4 * a + c
                at = slice_of(b, q)
                copy = remote(yz_out.at[at], yz_out.at[at], spread_s.at[0], spread_r.at[q - jnp.where(a > k, 4, 0)], k * 2 + b)
                pl.when(going == 1)(copy.start)
                spread_copies.append((going == 1, copy))

    for i in range(reach, rows - reach):
        inner_row(i, 1.0)
    give_half(halves[0])
    beside = jnp.minimum(me, reach) + jnp.minimum(n - 1 - me, reach)
    for size in range(1, 2 * reach + 1):
        pl.when(beside == size)(sent(row_slots, size, row_s, row_r).wait_recv)
    for s in range(2 * reach + 1):
        at = me + s - reach
        inside = (at >= 0) & (at < n)
        here = pl.ds(s * chans, chans)

        @pl.when(inside)
        def _():
            row_plane[here, :] = row_slots[s]

        @pl.when(jnp.logical_not(inside))
        def _():
            row_plane[here, :] = jnp.zeros((chans, cols), bf)

    for s in range(3):
        at = me + s - 1
        keep = ((at >= 0) & (at < n)).astype(f32)
        inner = silu(conv_row(row_plane[s * chans : (s + 3) * chans, :], weights[g, 0]))
        row_inner[s * chans : (s + 1) * chans, :] = (inner * keep).astype(bf)
    outs[g] = conv_row(row_inner[...], weights[g, 1]).astype(bf)
    share_out = remote(outs.at[g], outs.at[g], core_s.at[1], core_r.at[1], me, 1 - g)
    share_out.start()
    for _, receives, copy in halo:
        pl.when(receives)(copy.wait_recv)
    inner_row(rows, 1.0)
    inner_row(rows + 1, (place < last).astype(f32))
    inner_row(0, (place > 0).astype(f32))
    inner_row(1, 1.0)
    give_half(halves[1])
    remote(outs.at[1 - g], outs.at[1 - g], core_s.at[1], core_r.at[1], me, 1 - g).wait_recv()

    def finish(*chunks):
        xy_out = outs[0].astype(f32)
        xz_out = outs[1].astype(f32)
        at = []
        for bb, q in chunks:
            c = q % 4
            stored = piece(bb, q // 4) * rows + c * reach
            first = piece(bb, q // 4) * rows + offset(c)
            at += [(stored + r, first + r) for r in range(reach)]
        mixed = []
        for s, y in at:
            product = column(xy_out, g * count + y) * xz_out
            product = product * yz_out[s].astype(f32)
            mixed.append((product_scale * product).astype(bf))
        mixed = jnp.concatenate(mixed, axis=1)
        hidden = silu(jnp.dot(wide[...], mixed, preferred_element_type=f32)).astype(bf)
        branch = jnp.dot(shrink[...], hidden, preferred_element_type=f32)
        for k, (s, y) in enumerate(at):
            updated[y] = (feature_row(y) + branch[:, k * cols : (k + 1) * cols]).astype(bf)

    takes = [pick(a, [take_order(m, z)[i] for z in range(m)]) for i in range(4 * m - 4)]
    hands = a == m - 2
    handed = max(m - 3, 0)

    def hand_copy(q):
        at = slice_of(b, q)
        return remote(yz_out.at[at], yz_out.at[at], spread_s.at[0], spread_r.at[q], (m - 1) * 2 + b)

    def take(i):
        q = takes[i]
        at = slice_of(b, q)
        remote(yz_out.at[at], yz_out.at[at], spread_s.at[0], spread_r.at[q - jnp.where(q // 4 > a, 4, 0)], partner).wait_recv()
        kept = pick(a, [int(not diverted(z, take_order(m, z)[i])) for z in range(m)])
        spot = pick(a, [cross_order(m, z).index(take_order(m, z)[i]) // 2 for z in range(m)])
        pl.when(kept == 1)(cross_copy(b, q, spot).start)
        pl.when(hands & (q // 4 == handed))(hand_copy(q).start)
        return b, q

    crossed = [pick(a, [cross_order(m, z)[i] for z in range(m)]) for i in range(4 * m)]

    def divert_copy(c):
        at = slice_of(1 - b, 4 + c)
        return remote(yz_out.at[at], yz_out.at[at], divert_s.at[0], cross_r.at[cross_order(m, 0).index(4 + c) // 2], b)

    def take_crossed(i):
        q = crossed[i]
        if i % 2 == 0:
            at = pl.ds(0, 2 * reach)
            remote(yz_out.at[at], yz_out.at[at], cross_s.at[0], cross_r.at[i // 2], partner).wait_recv()
        if i < len(halves[0]):
            pl.when(a == 1)(divert_copy(halves[0][i]).start)
        return 1 - b, q

    finish(*[(b, 4 * a + c) for c in own_order])

    def drain():
        pair_all.wait_send()
        slab_cross.wait_send()
        line_all.wait_send()
        slab_all.wait_send()
        for sends, _, copy in halo:
            pl.when(sends)(copy.wait_send)
        core.wait_send()
        share_out.wait_send()
        for size in range(1, 2 * reach + 1):
            pl.when(beside == size)(sent(row_slots, size, row_s, row_r).wait_send)

    pair = 2
    lag = 2
    for i in range(0, len(takes), pair):
        ready = [take(j) for j in range(i, i + pair)]
        ready += [take_crossed(j) for j in range(i - lag * pair, i - lag * pair + pair) if j >= 0]
        finish(*ready)
        if i == 2 * pair:
            drain()
    at = len(takes) - lag * pair
    for size in (4, 2, 2):
        size = min(size, len(crossed) - at)
        if size > 0:
            finish(*[take_crossed(at + j) for j in range(size)])
            at += size
        if at == len(crossed) - 2:
            counts = [
                4 * (m - 1 - sum(passed(m, z, k) for k in others(m, z)) + sum(passed(m, k, m - 1) for k in [m - 3]) * (z == m - 2))
                for z in range(m)
            ]
            for size in sorted(set(counts)):
                amount = sent(yz_out, size * reach, spread_s, spread_r)
                pl.when(pick(a, [int(x == size) for x in counts]) == 1)(amount.wait_send)
    while at < len(crossed):
        finish(take_crossed(at))
        at += 1
    pl.when(a > 0)(cross_all.wait_send)
    pl.when(a == 0)(sent(yz_out, (4 * m - len(halves[0])) * reach, cross_s, cross_r).wait_send)
    pl.when(a == 1)(sent(yz_out, len(halves[0]) * reach, divert_s, cross_r).wait_send)


def fused(voxels, occupancy, row_weights, column_weights, depth_weights, plane_kernels, expand_weight, shrink_weight):
    n = lax.axis_size("gx")
    m = n // 2
    count, cols, chans = voxels.shape[1:]
    rows = count // n
    sets, layers = plane_kernels.shape[:2]
    planes = 2
    span = 2 * reach + 1
    bf = jnp.bfloat16
    f32 = jnp.float32
    dma = pltpu.SemaphoreType.DMA
    operands = (
        voxels[0].transpose(0, 2, 1),
        occupancy[0],
        row_weights,
        column_weights,
        depth_weights.T,
        plane_kernels,
        expand_weight,
        shrink_weight.T,
    )
    updated = pl.pallas_call(
        functools.partial(block_kernel, n),
        out_shape=pltpu.VMEM((count, chans, cols), bf),
        in_specs=[pl.BlockSpec(memory_space=pl.ANY) for _ in operands],
        out_specs=pl.BlockSpec(memory_space=pltpu.VMEM),
        scratch_shapes=[pltpu.VMEM(x.shape, x.dtype) for x in operands]
        + [
            dma((4,)),
            dma((5,)),
            pltpu.VMEM((count, chans, cols), bf),
            pltpu.VMEM((planes, chans, cols), bf),
            pltpu.VMEM((sets, layers, 3 * chans, 3 * chans), bf),
            pltpu.VMEM(expand_weight.shape[::-1], bf),
            pltpu.VMEM((count, chans, cols), bf),
            pltpu.VMEM((planes, chans, cols), f32),
            pltpu.VMEM((chans, count), f32),
            pltpu.VMEM((4 * m, reach, chans, cols), bf),
            pltpu.VMEM((4 * m, reach, chans, cols), bf),
            pltpu.VMEM((6 * m, reach, chans, cols), bf),
            pltpu.VMEM((2 * m, reach, chans, cols), bf),
            pltpu.VMEM((reach, chans, cols), bf),
            pltpu.VMEM((4, reach, chans, cols), f32),
            pltpu.VMEM(((rows + 4) * chans, cols), bf),
            pltpu.VMEM(((rows + 2) * chans, cols), bf),
            pltpu.VMEM((chans, cols), bf),
            pltpu.VMEM((span, chans, cols), bf),
            pltpu.VMEM((span * chans, cols), bf),
            pltpu.VMEM((3 * chans, cols), bf),
            pltpu.VMEM((planes, chans, cols), bf),
            dma((2,)), dma((3 * m + 1,)), dma((1,)), dma((6 * m - 6,)), dma((1,)), dma((1,)), dma((2,)), dma((2,)),
            dma((1,)), dma((1,)), dma((2,)), dma((2,)),
            dma((1,)), dma((4 * m - 4,)), dma((1,)), dma((2 * m,)), dma((1,)),
            pltpu.SemaphoreType.REGULAR((m - 2, 2)),
        ],
        compiler_params=pltpu.CompilerParams(collective_id=0, has_side_effects=True),
    )(*operands)
    return updated.transpose(0, 2, 1)[None]


def fits(voxels):
    n = lax.axis_size("gx")
    sides = lax.axis_size("gy")
    xs, ys, zs, _ = voxels.shape
    return xs == 1 and sides == 2 and n % 2 == 0 and n >= 8 and ys == n * 4 * reach and 2 * ys == zs


def plain_planes(features, row_weights, column_weights, depth_weights, plane_kernels):
    xy_plane = jnp.einsum(
        "xyzc,zc->xyc", features, depth_weights, preferred_element_type=jnp.float32
    ).astype(jnp.bfloat16)
    xz_part = jnp.einsum(
        "xyzc,yc->xzc", features, column_weights, preferred_element_type=jnp.float32
    )
    yz_part = jnp.einsum("xyzc,xc->yzc", features, row_weights, preferred_element_type=jnp.float32)
    xy_out = plane_block(xy_plane, plane_kernels[0], rim_xy)
    xz_plane = lax.psum(xz_part, "gy").astype(jnp.bfloat16)
    xz_out = plane_block(xz_plane, plane_kernels[1], rim_xz)
    yz_plane = lax.psum(yz_part, "gx").astype(jnp.bfloat16)
    yz_out = plane_block(yz_plane, plane_kernels[2], rim_yz)
    return xy_out, xz_out, yz_out


def shards(
    voxels,
    occupancy,
    row_weights,
    column_weights,
    depth_weights,
    plane_kernels,
    expand_weight,
    shrink_weight,
):
    if fits(voxels):
        return fused(
            voxels,
            occupancy,
            row_weights,
            column_weights,
            depth_weights,
            plane_kernels,
            expand_weight,
            shrink_weight,
        )
    features = voxels * occupancy.astype(jnp.bfloat16)[..., None]
    xy_out, xz_out, yz_out = plain_planes(features, row_weights, column_weights, depth_weights, plane_kernels)
    product = xy_out.astype(jnp.float32)[:, :, None, :] * xz_out.astype(jnp.float32)[:, None, :, :]
    product = product * yz_out.astype(jnp.float32)[None, :, :, :]
    mixed = (product_scale * product).astype(jnp.bfloat16)
    hidden = jax.nn.silu(
        jnp.einsum("xyzc,ch->xyzh", mixed, expand_weight, preferred_element_type=jnp.float32)
    ).astype(jnp.bfloat16)
    branch = jnp.einsum("xyzh,hc->xyzc", hidden, shrink_weight, preferred_element_type=jnp.float32)
    return (features.astype(jnp.float32) + branch).astype(jnp.bfloat16)


def solution(mesh):
    in_specs = (
        P(("groups", "gx"), "gy", None, None),
        P(("groups", "gx"), "gy", None),
        P("gx", None),
        P("gy", None),
        P(),
        P(),
        P(),
        P(),
    )
    out_specs = P(("groups", "gx"), "gy", None, None)
    return jax.shard_map(shards, mesh=mesh, in_specs=in_specs, out_specs=out_specs, check_vma=False)
```

```python
import functools

import jax
import jax.numpy as jnp
from jax import lax
from jax.experimental import pallas as pl
from jax.experimental.pallas import tpu as pltpu
from jax.sharding import PartitionSpec as P

MESH = pl.DeviceIdType.MESH
reach = 2

product_scale = 8.0


def with_halo(cells, sides, width):
    for axis, dim in sides:
        count = lax.axis_size(axis)
        ends = count - 1
        head = lax.slice_in_dim(cells, 0, width, axis=dim)
        tail = lax.slice_in_dim(cells, cells.shape[dim] - width, cells.shape[dim], axis=dim)
        cells = jnp.concatenate(
            [
                lax.ppermute(tail, axis, [(i, (i + 1) % count) for i in range(ends)]),
                cells,
                lax.ppermute(head, axis, [((i + 1) % count, i) for i in range(ends)]),
            ],
            axis=dim,
        )
    return cells


def conv_valid(padded, kernel):
    rows = padded.shape[0] - 2
    cols = padded.shape[1] - 2
    total = jnp.zeros((rows, cols, kernel.shape[-1]), jnp.float32)
    for row_off in range(3):
        for col_off in range(3):
            window = padded[row_off : row_off + rows, col_off : col_off + cols]
            total = total + jnp.einsum(
                "ijc,co->ijo", window, kernel[row_off, col_off], preferred_element_type=jnp.float32
            )
    return total


def plane_block(plane, kernels, extend):
    inner = jax.nn.silu(conv_valid(extend(plane), kernels[0])).astype(jnp.bfloat16)
    return conv_valid(extend(inner), kernels[1]).astype(jnp.bfloat16)


def rim_xy(plane):
    return with_halo(plane, (("gx", 0), ("gy", 1)), 1)


def rim_xz(plane):
    padded = with_halo(plane, (("gx", 0),), 1)
    return jnp.pad(padded, ((0, 0), (1, 1), (0, 0)))


def rim_yz(plane):
    padded = with_halo(plane, (("gy", 0),), 1)
    return jnp.pad(padded, ((0, 0), (1, 1), (0, 0)))


def conv_row(window, weight):
    taps = jnp.dot(weight, window, preferred_element_type=jnp.float32)
    chans = taps.shape[0] // 3
    cols = taps.shape[1]
    lane = lax.broadcasted_iota(jnp.int32, (chans, cols), 1)
    left = pltpu.roll(taps[:chans], 1, 1)
    right = pltpu.roll(taps[2 * chans :], cols - 1, 1)
    left = jnp.where(lane == 0, 0.0, left)
    right = jnp.where(lane == cols - 1, 0.0, right)
    return taps[chans : 2 * chans] + left + right


def silu(v):
    half = 0.5 * v
    return half + half * jnp.tanh(half)


def identity(size):
    row = lax.broadcasted_iota(jnp.int32, (size, size), 0)
    col = lax.broadcasted_iota(jnp.int32, (size, size), 1)
    return jnp.where(row == col, 1.0, 0.0)


def flipped(x):
    eye = identity(x.shape[1]).astype(x.dtype)
    return lax.dot_general(eye, x, (((1,), (1,)), ((), ())), preferred_element_type=jnp.float32)


def column(x, at):
    lane = lax.broadcasted_iota(jnp.int32, x.shape, 1)
    return jnp.sum(jnp.where(lane == at, x, 0.0), axis=1, keepdims=True)


halves = ((2, 3), (1, 0))
own_order = halves[0] + halves[1]


def pick(index, values):
    chosen = values[0]
    for i, value in enumerate(values):
        if i > 0 and value != values[0]:
            chosen = jnp.where(index == i, value, chosen)
    return chosen


def others(m, z):
    return [k for k in range(m) if k != z]


def joined(m, z, k):
    return z in (0, m - 1) and abs(k - z) > 1


def joins(m, z):
    if z == 1:
        return [(0, k) for k in range(m - 1, 1, -1)]
    if z == m - 2:
        return [(m - 1, k) for k in range(m - 2)]
    return []


def sum_order(m, z):
    far = sorted(others(m, z), key=lambda k: -abs(k - z))
    held = [k for _, k in joins(m, z)]
    first = [k for k in far if k in held or joined(m, z, k)]
    rest = [k for k in far if k not in first]
    ks = [(k, c) for c in range(3) for k in first] + [(k, c) for c in range(3) for k in rest + [z]]
    ks = [kc for kc in ks if kc[0] != z] + [kc for kc in ks if kc[0] == z]
    return [4 * k + c for k, c in ks]


def passed(m, z, k):
    return k == m - 1 and z == m - 3


def deferred(m, z, k):
    return (z == m - 1 and k == m - 2) or (z == m - 2 and k == m - 3)


def give_order(m, z):
    return sorted(others(m, z), key=lambda k: k - z if k > z else k)


def take_order(m, z):
    def rank(k):
        return z if k > z else z - k - 1, abs(k - z) > 1 and k < z, -k

    ks = sorted([k for k in others(m, z) if not passed(m, k, z) and not deferred(m, k, z)], key=rank)
    if m == 4 and z == 0:
        return [14, 15, 10, 11, 6, 7, 13, 5, 12, 4, 9, 8]
    if m == 4 and z == 1 and []:
        return []
    late = [k for k in others(m, z) if passed(m, k, z) or deferred(m, k, z)]
    return [4 * k + c for group in (ks, late) for half in halves for k in group for c in half]


def diverted(z, q):
    return z == 0 and q in [4 + c for c in halves[0]]


def cross_order(m, z):
    chunks = [4 * z + c for c in own_order] + take_order(m, z)
    late = [q for q in chunks if diverted(z, q)]
    chunks = [q for q in chunks if q not in late]
    if late:
        chunks[-4:-4] = late
    return chunks


def block_kernel(
    n, voxels_in, occupancy_in, row_weights_in, column_weights_in, depth_in, kernels_in, expand_in, shrink_in, updated,
    voxels, occupancy, row_weights, column_weights, depth_weights, plane_kernels, expand, shrink, load_s, fetch_s,
    part, rows_in, weights, wide, yz_out, row_sums, turned,
    pair_in, pair_sum, line_in, slab_in, slab_sum, yz_sum, yz_plane, yz_inner,
    row_other, row_slots, row_plane, row_inner, outs,
    pair_s, pair_r, line_s, line_r, slab_s, slab_r, halo_s, halo_r, row_s, row_r, core_s, core_r, spread_s, spread_r, cross_s, cross_r, divert_s, known,
):
    me = lax.axis_index("gx")
    g = lax.axis_index("gy")
    m = n // 2
    a = me // 2
    b = me % 2
    count, chans, cols = part.shape
    rows = count // n
    bf = jnp.bfloat16
    f32 = jnp.float32
    partner = a * 2 + 1 - b

    def table(make):
        return [make(z) for z in range(m)]

    def feature_row(y):
        return voxels[y].astype(f32) * occupancy[pl.ds(y, 1), :].astype(f32)

    def piece(bb, aa):
        return bb * m + aa + bb * (m - 1 - 2 * aa)

    def owner(j):
        bb = j // m
        aa = j % m
        return (aa + bb * (m - 1 - 2 * aa)) * 2 + bb

    def offset(c):
        starts = [0, rows - reach, reach, 2 * reach]
        return starts[c] if isinstance(c, int) else pick(c, starts)

    def slice_of(bb, q):
        return pl.ds(piece(bb, q // 4) * rows + (q % 4) * reach, reach)

    def remote(src, dst, send, recv, gx, gy=None):
        target = {"gx": gx} if gy is None else {"gx": gx, "gy": gy}
        return pltpu.make_async_remote_copy(
            src_ref=src, dst_ref=dst, send_sem=send, recv_sem=recv, device_id=target, device_id_type=MESH
        )

    place = g * n + piece(b, a)
    last = 2 * n - 1
    before = jnp.maximum(place - 1, 0)
    after = jnp.minimum(place + 1, last)

    barrier = pltpu.get_barrier_semaphore()

    def greet(gx, gy):
        pl.semaphore_signal(barrier, inc=1, device_id={"gx": gx, "gy": gy}, device_id_type=MESH)

    lower = a > 0
    upper = a < m - 1
    slant = jnp.where(b == 0, lower, upper)
    seam_low = place == n - 1
    seam_high = place == n
    greet(partner, g)
    greet(me, 1 - g)
    pl.when(lower)(lambda: greet(jnp.maximum(me - 2, 0), g))
    pl.when(upper)(lambda: greet(jnp.minimum(me + 2, n - 1), g))
    pl.when(slant)(lambda: greet(jnp.clip(me + 2 * b - 1, 0, n - 1), g))
    pl.when(seam_low)(lambda: greet(owner(0), 1 - g))
    pl.when(seam_high)(lambda: greet(owner(n - 1), 1 - g))
    greeters = (
        2 + lower.astype(jnp.int32) + upper.astype(jnp.int32) + slant.astype(jnp.int32)
        + seam_low.astype(jnp.int32) + seam_high.astype(jnp.int32)
    )

    order = table(lambda z: sum_order(m, z))
    steps = 3 * m
    turns = [pick(a, [o[i] for o in order]) for i in range(steps)]

    small = [
        pltpu.make_async_copy(row_weights_in, row_weights, load_s.at[0]),
        pltpu.make_async_copy(occupancy_in, occupancy, load_s.at[1]),
    ]
    large = []
    for bb in (1 - b, b):
        for k in range(m):
            at = pl.ds(piece(bb, k) * rows, rows)
            large.append(pltpu.make_async_copy(voxels_in.at[at], voxels.at[at], load_s.at[2 + len(large) // m]))
    fetches = [
        pltpu.make_async_copy(kernels_in, plane_kernels, fetch_s.at[0]),
        pltpu.make_async_copy(column_weights_in, column_weights, fetch_s.at[1]),
        pltpu.make_async_copy(depth_in, depth_weights, fetch_s.at[2]),
        pltpu.make_async_copy(expand_in, expand, fetch_s.at[3]),
        pltpu.make_async_copy(shrink_in, shrink, fetch_s.at[4]),
    ]
    for copy in small + large + fetches:
        copy.start()

    for copy in small:
        copy.wait()
    rw = jnp.broadcast_to(row_weights[...].astype(f32), (chans, chans))
    rw = jnp.sum(rw * identity(chans), axis=1, keepdims=True)

    def yz_terms(j):
        for c in range(4):
            for r in range(reach):
                part[j * rows + c * reach + r] = (feature_row(j * rows + offset(c) + r) * rw).astype(bf)

    pair_copies = []
    for i, q in enumerate(turns):
        pair_copies.append(remote(part.at[slice_of(1 - b, q)], pair_in.at[q], pair_s.at[0], pair_r.at[i], partner))

    def yz_pieces(bb):
        def some(k, carry):
            yz_terms(piece(bb, k))
            return carry

        lax.fori_loop(0, m, some, 0)

    def loaded(which):
        at = pl.ds(0, m * rows)
        pltpu.make_async_copy(voxels_in.at[at], voxels.at[at], load_s.at[2 + which]).wait()

    loaded(0)
    yz_pieces(1 - b)

    def sent(buffer, size, sem, recv):
        return remote(buffer.at[pl.ds(0, size)], buffer.at[pl.ds(0, size)], sem.at[0], recv.at[0], partner)

    pair_all = sent(part, steps * reach, pair_s, pair_r)
    line_all = sent(pair_sum, steps - 3, line_s, line_r)
    slab_all = sent(part, 2 * (m - 1) * reach, slab_s, slab_r)
    cross_all = sent(yz_out, 4 * m * reach, cross_s, cross_r)
    slab_copies = []
    for dist in range(1, m):
        for side in (-1, 1):
            k = jnp.clip(a + side * dist, 0, m - 1)
            there = (a + side * dist >= 0) & (a + side * dist < m)
            for bb in range(2):
                copy = remote(
                    part.at[slice_of(bb, 4 * k + 3)], slab_in.at[2 * a + bb], slab_s.at[0], slab_r.at[0], k * 2 + b
                )
                slab_copies.append((dist, there, copy))

    def start_slabs(dist):
        for d, there, copy in slab_copies:
            if d == dist:
                pl.when(there)(copy.start)

    pl.semaphore_wait(barrier, greeters)
    for copy in pair_copies:
        copy.start()
    loaded(1)
    yz_pieces(b)
    start_slabs(1)

    def tell(level, side):
        step = 2 if side == 0 else -2
        pl.semaphore_signal(
            known.at[level - 2, side], inc=1, device_id={"gx": jnp.clip(me - step, 0, n - 1), "gy": g}, device_id_type=MESH
        )

    def heard(level, side):
        return (a + level <= m - 1) if side == 0 else (a - level >= 0)

    def tells(level, side):
        return (lower if side == 0 else upper) & heard(level - 1, side)

    def tell_level(level):
        for side in range(2):
            if level > 2:
                pl.when(heard(level - 1, side))(lambda: pl.semaphore_wait(known.at[level - 3, side], 1))
            if level < m:
                pl.when(tells(level, side))(lambda: tell(level, side))

    tell_level(2)
    for level in range(3, m):
        tell_level(level)
        start_slabs(level - 1)

    for copy in fetches:
        copy.wait()
    turned[...] = flipped(column_weights[...])
    row_sums[...] = jnp.zeros(row_sums.shape, f32)
    lane = lax.broadcasted_iota(jnp.int32, (chans, cols), 1)

    group = 4
    share = count // (2 * m)

    def row_terms(first):
        depth = depth_weights[...].astype(f32)

        def some(step, carry):
            xy, xz = row_sums[0], row_sums[1]
            for k in range(group):
                y = first + step * group + k
                f = feature_row(y)
                xy = jnp.where(lane == g * count + y, jnp.sum(f * depth, axis=1, keepdims=True), xy)
                xz = xz + f * column(turned[...], y)
            row_sums[0] = xy
            row_sums[1] = xz
            return carry

        lax.fori_loop(0, share // group, some, 0)

    def flip_plane(p, layer):
        for off in range(3):
            taps = plane_kernels[p, layer, :, off].reshape(3 * chans, chans)
            weights[p, layer, off * chans : (off + 1) * chans, :] = flipped(taps).astype(bf)

    holds = table(lambda z: [k for _, k in joins(m, z)])
    holding = (a == 1) | (a == m - 2)

    def line_copy(i):
        gx, slot = [], []
        for z in range(m):
            k, c = order[z][i] // 4, order[z][i] % 4
            if k == z:
                gx.append(z)
                slot.append(0)
            elif joined(m, z, k):
                via = z + (1 if k > z else -1)
                gx.append(via)
                slot.append(3 * m + 3 * holds[via].index(k) + c)
            else:
                gx.append(k)
                slot.append(3 * z + c)
        to = pick(a, slot)
        q = turns[i]
        return remote(pair_sum.at[q], line_in.at[to], line_s.at[0], line_r.at[to], pick(a, gx) * 2 + b)

    line_copies = [line_copy(i) for i in range(steps - 3)]
    held = [pick(a, [int(order[z][i] // 4 in holds[z]) for z in range(m)]) for i in range(steps - 3)]

    def reduce_pair(i):
        q = turns[i]
        pair_copies[i].wait_recv()
        mine = part[slice_of(b, q)].astype(f32)
        pair_sum[q] = (mine + pair_in[q].astype(f32)).astype(bf)
        pl.when(held[i] == 0)(line_copies[i].start)

    def reduce_joined(i):
        @pl.when(holding)
        def _():
            q = turns[i]
            slot = 3 * m + pick(a, [3 * (holds[z].index(order[z][i] // 4) if holds[z] else 0) + order[z][i] % 4 for z in range(m)])
            remote(pair_sum.at[q], line_in.at[slot], line_s.at[0], line_r.at[slot], partner).wait_recv()
            pair_sum[q] = (pair_sum[q].astype(f32) + line_in[slot].astype(f32)).astype(bf)
            line_copies[i].start()

    def reduce_own(c):
        pair_copies[steps - 3 + c].wait_recv()
        q = 4 * a + c
        yz_sum[c] = part[slice_of(b, q)].astype(f32) + pair_in[q].astype(f32)

    def reduce_line(c):
        for i in range(m - 1):
            sources = [sorted(others(m, z), key=lambda s: (abs(s - z), s))[i] for z in range(m)]
            src = pick(a, sources)
            skip = pick(a, [int(joined(m, s, z)) for z, s in enumerate(sources)])

            @pl.when(skip == 0)
            def _():
                slot = 3 * src + c
                remote(pair_sum.at[slot], line_in.at[slot], line_s.at[0], line_r.at[slot], partner).wait_recv()
                yz_sum[c] = yz_sum[c] + line_in[slot].astype(f32)

    slab_cross = remote(slab_sum, pair_in.at[4 * a + 3], pair_s.at[1], pair_r.at[steps], partner)

    def reduce_slab():
        q = 4 * a + 3
        total = [part[slice_of(bb, q)].astype(f32) for bb in (1 - b, b)]
        sent(slab_in, 2 * (m - 1), slab_s, slab_r).wait_recv()
        for i in range(m - 1):
            src = pick(a, [others(m, z)[i] for z in range(m)])
            for side, bb in enumerate((1 - b, b)):
                slot = 2 * src + bb
                total[side] = total[side] + slab_in[slot].astype(f32)
        slab_sum[...] = total[0].astype(bf)
        slab_cross.start()
        yz_sum[3] = total[1]

    def reduce_slab_own():
        slab_cross.wait_recv()
        yz_sum[3] = yz_sum[3] + pair_in[4 * a + 3].astype(f32)

    for i in range(2):
        row_terms(i * share)
    tell_level(m)
    start_slabs(m - 1)
    for i in range(2, 2 * m):
        row_terms(i * share)
    rows_in[...] = row_sums[...].astype(bf)
    core = remote(rows_in.at[1 - g], row_other.at[...], core_s.at[0], core_r.at[0], me, 1 - g)
    core.start()
    flip_plane(2, 0)
    flip_plane(2, 1)

    first = 5
    for i in range(first):
        reduce_pair(i)
    merges = 3 * (m - 2)
    slab_at = steps - 3 - 1
    done = 0
    for i in range(first, steps - 3):
        if done < merges:
            reduce_joined(done)
            done += 1
        reduce_pair(i)
    reduce_slab()
    core.wait_recv()
    mid = rows_in[g].astype(f32) + row_other[...].astype(f32)
    row_slots[reach] = mid.astype(bf)
    row_copies = []
    for dx in range(-reach, reach + 1):
        if dx != 0:
            slot = reach - dx
            copy = remote(
                row_slots.at[reach], row_slots.at[slot], row_s.at[0], row_r.at[0], jnp.clip(me + dx, 0, n - 1)
            )
            row_copies.append((dx, copy))
            pl.when((me + dx >= 0) & (me + dx < n))(copy.start)
    while done < merges:
        reduce_joined(done)
        done += 1
    for layer in range(2):
        flip_plane(g, layer)
    wide[...] = flipped(expand[...]).astype(bf)

    edge = reach * chans
    halo = [
        (place > 0, place < last, remote(
            yz_plane.at[pl.ds(edge, edge)], yz_plane.at[pl.ds(edge + rows * chans, edge)],
            halo_s.at[0], halo_r.at[0], owner(before % n), before // n,
        )),
        (place < last, place > 0, remote(
            yz_plane.at[pl.ds(rows * chans, edge)], yz_plane.at[pl.ds(0, edge)],
            halo_s.at[1], halo_r.at[1], owner(after % n), after // n,
        )),
    ]

    @pl.when(place == 0)
    def _():
        yz_plane[pl.ds(0, edge), :] = jnp.zeros((edge, cols), bf)

    @pl.when(place == last)
    def _():
        yz_plane[pl.ds(edge + rows * chans, edge), :] = jnp.zeros((edge, cols), bf)

    def settle(c):
        for r in range(reach):
            at = (reach + offset(c) + r) * chans
            yz_plane[at : at + chans, :] = yz_sum[c, r].astype(bf)

    def inner_row(i, keep):
        inner = silu(conv_row(yz_plane[i * chans : (i + 3) * chans, :], weights[2, 0])) * keep
        yz_inner[i * chans : (i + 1) * chans, :] = inner.astype(bf)

    for c in range(2):
        reduce_own(c)
    for c in range(2):
        reduce_line(c)
        settle(c)
        pl.when(halo[c][0])(halo[c][2].start)
    reduce_own(2)
    reduce_slab_own()
    settle(3)
    for i in range(rows - reach, rows):
        inner_row(i, 1.0)
    reduce_line(2)
    settle(2)

    spread_copies = []
    own = piece(b, a)

    def cross_copy(bb, q, pair_at):
        at = slice_of(bb, q)
        return remote(yz_out.at[at], yz_out.at[at], cross_s.at[0], cross_r.at[pair_at], partner)

    def give_half(half):
        for c in half:
            for r in range(reach):
                at = (offset(c) + r) * chans
                done = conv_row(yz_inner[at : at + 3 * chans, :], weights[2, 1])
                yz_out[own * rows + c * reach + r] = done.astype(bf)
        for c in half:
            cross_copy(b, 4 * a + c, own_order.index(c) // 2).start()
        later = table(lambda z: [deferred(m, z, k) for k in give_order(m, z)])
        for turn, i, part_of in [(0, i, half) for i in range(1)] + [(1, i, halves[0]) for i in range(m - 1)] + [(2, i, half) for i in range(1, m - 1)]:
            first_half = half is halves[0]
            if turn == 1 and (first_half or not any(x[i] for x in later)):
                continue
            k = pick(a, [give_order(m, z)[i] for z in range(m)])
            go = [not passed(m, z, give_order(m, z)[i]) for z in range(m)]
            if turn == 1:
                go = [x and later[z][i] for z, x in enumerate(go)]
            elif first_half:
                go = [x and not later[z][i] for z, x in enumerate(go)]
            going = pick(a, [int(x) for x in go])
            for c in part_of:
                q = 4 * a + c
                at = slice_of(b, q)
                copy = remote(yz_out.at[at], yz_out.at[at], spread_s.at[0], spread_r.at[q - jnp.where(a > k, 4, 0)], k * 2 + b)
                pl.when(going == 1)(copy.start)
                spread_copies.append((going == 1, copy))

    for i in range(reach, rows - reach):
        inner_row(i, 1.0)
    give_half(halves[0])
    beside = jnp.minimum(me, reach) + jnp.minimum(n - 1 - me, reach)
    for size in range(1, 2 * reach + 1):
        pl.when(beside == size)(sent(row_slots, size, row_s, row_r).wait_recv)
    for s in range(2 * reach + 1):
        at = me + s - reach
        inside = (at >= 0) & (at < n)
        here = pl.ds(s * chans, chans)

        @pl.when(inside)
        def _():
            row_plane[here, :] = row_slots[s]

        @pl.when(jnp.logical_not(inside))
        def _():
            row_plane[here, :] = jnp.zeros((chans, cols), bf)

    for s in range(3):
        at = me + s - 1
        keep = ((at >= 0) & (at < n)).astype(f32)
        inner = silu(conv_row(row_plane[s * chans : (s + 3) * chans, :], weights[g, 0]))
        row_inner[s * chans : (s + 1) * chans, :] = (inner * keep).astype(bf)
    outs[g] = conv_row(row_inner[...], weights[g, 1]).astype(bf)
    share_out = remote(outs.at[g], outs.at[g], core_s.at[1], core_r.at[1], me, 1 - g)
    share_out.start()
    for _, receives, copy in halo:
        pl.when(receives)(copy.wait_recv)
    inner_row(rows, 1.0)
    inner_row(rows + 1, (place < last).astype(f32))
    inner_row(0, (place > 0).astype(f32))
    inner_row(1, 1.0)
    give_half(halves[1])
    remote(outs.at[1 - g], outs.at[1 - g], core_s.at[1], core_r.at[1], me, 1 - g).wait_recv()

    def finish(*chunks):
        xy_out = outs[0].astype(f32)
        xz_out = outs[1].astype(f32)
        at = []
        for bb, q in chunks:
            c = q % 4
            stored = piece(bb, q // 4) * rows + c * reach
            first = piece(bb, q // 4) * rows + offset(c)
            at += [(stored + r, first + r) for r in range(reach)]
        mixed = []
        for s, y in at:
            product = column(xy_out, g * count + y) * xz_out
            product = product * yz_out[s].astype(f32)
            mixed.append((product_scale * product).astype(bf))
        mixed = jnp.concatenate(mixed, axis=1)
        hidden = silu(jnp.dot(wide[...], mixed, preferred_element_type=f32)).astype(bf)
        branch = jnp.dot(shrink[...], hidden, preferred_element_type=f32)
        for k, (s, y) in enumerate(at):
            updated[y] = (feature_row(y) + branch[:, k * cols : (k + 1) * cols]).astype(bf)

    takes = [pick(a, [take_order(m, z)[i] for z in range(m)]) for i in range(4 * m - 4)]
    hands = a == m - 2
    handed = max(m - 3, 0)

    def hand_copy(q):
        at = slice_of(b, q)
        return remote(yz_out.at[at], yz_out.at[at], spread_s.at[0], spread_r.at[q], (m - 1) * 2 + b)

    def take(i):
        q = takes[i]
        at = slice_of(b, q)
        remote(yz_out.at[at], yz_out.at[at], spread_s.at[0], spread_r.at[q - jnp.where(q // 4 > a, 4, 0)], partner).wait_recv()
        kept = pick(a, [int(not diverted(z, take_order(m, z)[i])) for z in range(m)])
        spot = pick(a, [cross_order(m, z).index(take_order(m, z)[i]) // 2 for z in range(m)])
        pl.when(kept == 1)(cross_copy(b, q, spot).start)
        pl.when(hands & (q // 4 == handed))(hand_copy(q).start)
        return b, q

    crossed = [pick(a, [cross_order(m, z)[i] for z in range(m)]) for i in range(4 * m)]

    def divert_copy(c):
        at = slice_of(1 - b, 4 + c)
        return remote(yz_out.at[at], yz_out.at[at], divert_s.at[0], cross_r.at[cross_order(m, 0).index(4 + c) // 2], b)

    def take_crossed(i):
        q = crossed[i]
        if i % 2 == 0:
            at = pl.ds(0, 2 * reach)
            remote(yz_out.at[at], yz_out.at[at], cross_s.at[0], cross_r.at[i // 2], partner).wait_recv()
        if i < len(halves[0]):
            pl.when(a == 1)(divert_copy(halves[0][i]).start)
        return 1 - b, q

    finish(*[(b, 4 * a + c) for c in own_order])

    def drain():
        pair_all.wait_send()
        slab_cross.wait_send()
        line_all.wait_send()
        slab_all.wait_send()
        for sends, _, copy in halo:
            pl.when(sends)(copy.wait_send)
        core.wait_send()
        share_out.wait_send()
        for size in range(1, 2 * reach + 1):
            pl.when(beside == size)(sent(row_slots, size, row_s, row_r).wait_send)

    pair = 2
    lag = 3
    for i in range(0, len(takes), pair):
        ready = [take(j) for j in range(i, i + pair)]
        ready += [take_crossed(j) for j in range(i - lag * pair, i - lag * pair + pair) if j >= 0]
        finish(*ready)
        if i == 2 * pair:
            drain()
    at = len(takes) - lag * pair
    for size in (4, 4, 2, 2):
        size = min(size, len(crossed) - at)
        if size > 0:
            finish(*[take_crossed(at + j) for j in range(size)])
            at += size
        if at == len(crossed) - 2:
            counts = [
                4 * (m - 1 - sum(passed(m, z, k) for k in others(m, z)) + sum(passed(m, k, m - 1) for k in [m - 3]) * (z == m - 2))
                for z in range(m)
            ]
            for size in sorted(set(counts)):
                amount = sent(yz_out, size * reach, spread_s, spread_r)
                pl.when(pick(a, [int(x == size) for x in counts]) == 1)(amount.wait_send)
    while at < len(crossed):
        finish(take_crossed(at))
        at += 1
    pl.when(a > 0)(cross_all.wait_send)
    pl.when(a == 0)(sent(yz_out, (4 * m - len(halves[0])) * reach, cross_s, cross_r).wait_send)
    pl.when(a == 1)(sent(yz_out, len(halves[0]) * reach, divert_s, cross_r).wait_send)


def fused(voxels, occupancy, row_weights, column_weights, depth_weights, plane_kernels, expand_weight, shrink_weight):
    n = lax.axis_size("gx")
    m = n // 2
    count, cols, chans = voxels.shape[1:]
    rows = count // n
    sets, layers = plane_kernels.shape[:2]
    planes = 2
    span = 2 * reach + 1
    bf = jnp.bfloat16
    f32 = jnp.float32
    dma = pltpu.SemaphoreType.DMA
    operands = (
        voxels[0].transpose(0, 2, 1),
        occupancy[0],
        row_weights,
        column_weights,
        depth_weights.T,
        plane_kernels,
        expand_weight,
        shrink_weight.T,
    )
    updated = pl.pallas_call(
        functools.partial(block_kernel, n),
        out_shape=pltpu.VMEM((count, chans, cols), bf),
        in_specs=[pl.BlockSpec(memory_space=pl.ANY) for _ in operands],
        out_specs=pl.BlockSpec(memory_space=pltpu.VMEM),
        scratch_shapes=[pltpu.VMEM(x.shape, x.dtype) for x in operands]
        + [
            dma((4,)),
            dma((5,)),
            pltpu.VMEM((count, chans, cols), bf),
            pltpu.VMEM((planes, chans, cols), bf),
            pltpu.VMEM((sets, layers, 3 * chans, 3 * chans), bf),
            pltpu.VMEM(expand_weight.shape[::-1], bf),
            pltpu.VMEM((count, chans, cols), bf),
            pltpu.VMEM((planes, chans, cols), f32),
            pltpu.VMEM((chans, count), f32),
            pltpu.VMEM((4 * m, reach, chans, cols), bf),
            pltpu.VMEM((4 * m, reach, chans, cols), bf),
            pltpu.VMEM((6 * m, reach, chans, cols), bf),
            pltpu.VMEM((2 * m, reach, chans, cols), bf),
            pltpu.VMEM((reach, chans, cols), bf),
            pltpu.VMEM((4, reach, chans, cols), f32),
            pltpu.VMEM(((rows + 4) * chans, cols), bf),
            pltpu.VMEM(((rows + 2) * chans, cols), bf),
            pltpu.VMEM((chans, cols), bf),
            pltpu.VMEM((span, chans, cols), bf),
            pltpu.VMEM((span * chans, cols), bf),
            pltpu.VMEM((3 * chans, cols), bf),
            pltpu.VMEM((planes, chans, cols), bf),
            dma((2,)), dma((3 * m + 1,)), dma((1,)), dma((6 * m - 6,)), dma((1,)), dma((1,)), dma((2,)), dma((2,)),
            dma((1,)), dma((1,)), dma((2,)), dma((2,)),
            dma((1,)), dma((4 * m - 4,)), dma((1,)), dma((2 * m,)), dma((1,)),
            pltpu.SemaphoreType.REGULAR((m - 2, 2)),
        ],
        compiler_params=pltpu.CompilerParams(collective_id=0, has_side_effects=True),
    )(*operands)
    return updated.transpose(0, 2, 1)[None]


def fits(voxels):
    n = lax.axis_size("gx")
    sides = lax.axis_size("gy")
    xs, ys, zs, _ = voxels.shape
    return xs == 1 and sides == 2 and n % 2 == 0 and n >= 8 and ys == n * 4 * reach and 2 * ys == zs


def plain_planes(features, row_weights, column_weights, depth_weights, plane_kernels):
    xy_plane = jnp.einsum(
        "xyzc,zc->xyc", features, depth_weights, preferred_element_type=jnp.float32
    ).astype(jnp.bfloat16)
    xz_part = jnp.einsum(
        "xyzc,yc->xzc", features, column_weights, preferred_element_type=jnp.float32
    )
    yz_part = jnp.einsum("xyzc,xc->yzc", features, row_weights, preferred_element_type=jnp.float32)
    xy_out = plane_block(xy_plane, plane_kernels[0], rim_xy)
    xz_plane = lax.psum(xz_part, "gy").astype(jnp.bfloat16)
    xz_out = plane_block(xz_plane, plane_kernels[1], rim_xz)
    yz_plane = lax.psum(yz_part, "gx").astype(jnp.bfloat16)
    yz_out = plane_block(yz_plane, plane_kernels[2], rim_yz)
    return xy_out, xz_out, yz_out


def shards(
    voxels,
    occupancy,
    row_weights,
    column_weights,
    depth_weights,
    plane_kernels,
    expand_weight,
    shrink_weight,
):
    if fits(voxels):
        return fused(
            voxels,
            occupancy,
            row_weights,
            column_weights,
            depth_weights,
            plane_kernels,
            expand_weight,
            shrink_weight,
        )
    features = voxels * occupancy.astype(jnp.bfloat16)[..., None]
    xy_out, xz_out, yz_out = plain_planes(features, row_weights, column_weights, depth_weights, plane_kernels)
    product = xy_out.astype(jnp.float32)[:, :, None, :] * xz_out.astype(jnp.float32)[:, None, :, :]
    product = product * yz_out.astype(jnp.float32)[None, :, :, :]
    mixed = (product_scale * product).astype(jnp.bfloat16)
    hidden = jax.nn.silu(
        jnp.einsum("xyzc,ch->xyzh", mixed, expand_weight, preferred_element_type=jnp.float32)
    ).astype(jnp.bfloat16)
    branch = jnp.einsum("xyzh,hc->xyzc", hidden, shrink_weight, preferred_element_type=jnp.float32)
    return (features.astype(jnp.float32) + branch).astype(jnp.bfloat16)


def solution(mesh):
    in_specs = (
        P(("groups", "gx"), "gy", None, None),
        P(("groups", "gx"), "gy", None),
        P("gx", None),
        P("gy", None),
        P(),
        P(),
        P(),
        P(),
    )
    out_specs = P(("groups", "gx"), "gy", None, None)
    return jax.shard_map(shards, mesh=mesh, in_specs=in_specs, out_specs=out_specs, check_vma=False)
```

```python
import functools

import jax
import jax.numpy as jnp
from jax import lax
from jax.experimental import pallas as pl
from jax.experimental.pallas import tpu as pltpu
from jax.sharding import PartitionSpec as P

MESH = pl.DeviceIdType.MESH
reach = 2

product_scale = 8.0


def with_halo(cells, sides, width):
    for axis, dim in sides:
        count = lax.axis_size(axis)
        ends = count - 1
        head = lax.slice_in_dim(cells, 0, width, axis=dim)
        tail = lax.slice_in_dim(cells, cells.shape[dim] - width, cells.shape[dim], axis=dim)
        cells = jnp.concatenate(
            [
                lax.ppermute(tail, axis, [(i, (i + 1) % count) for i in range(ends)]),
                cells,
                lax.ppermute(head, axis, [((i + 1) % count, i) for i in range(ends)]),
            ],
            axis=dim,
        )
    return cells


def conv_valid(padded, kernel):
    rows = padded.shape[0] - 2
    cols = padded.shape[1] - 2
    total = jnp.zeros((rows, cols, kernel.shape[-1]), jnp.float32)
    for row_off in range(3):
        for col_off in range(3):
            window = padded[row_off : row_off + rows, col_off : col_off + cols]
            total = total + jnp.einsum(
                "ijc,co->ijo", window, kernel[row_off, col_off], preferred_element_type=jnp.float32
            )
    return total


def plane_block(plane, kernels, extend):
    inner = jax.nn.silu(conv_valid(extend(plane), kernels[0])).astype(jnp.bfloat16)
    return conv_valid(extend(inner), kernels[1]).astype(jnp.bfloat16)


def rim_xy(plane):
    return with_halo(plane, (("gx", 0), ("gy", 1)), 1)


def rim_xz(plane):
    padded = with_halo(plane, (("gx", 0),), 1)
    return jnp.pad(padded, ((0, 0), (1, 1), (0, 0)))


def rim_yz(plane):
    padded = with_halo(plane, (("gy", 0),), 1)
    return jnp.pad(padded, ((0, 0), (1, 1), (0, 0)))


def conv_row(window, weight):
    taps = jnp.dot(weight, window, preferred_element_type=jnp.float32)
    chans = taps.shape[0] // 3
    cols = taps.shape[1]
    lane = lax.broadcasted_iota(jnp.int32, (chans, cols), 1)
    left = pltpu.roll(taps[:chans], 1, 1)
    right = pltpu.roll(taps[2 * chans :], cols - 1, 1)
    left = jnp.where(lane == 0, 0.0, left)
    right = jnp.where(lane == cols - 1, 0.0, right)
    return taps[chans : 2 * chans] + left + right


def silu(v):
    half = 0.5 * v
    return half + half * jnp.tanh(half)


def identity(size):
    row = lax.broadcasted_iota(jnp.int32, (size, size), 0)
    col = lax.broadcasted_iota(jnp.int32, (size, size), 1)
    return jnp.where(row == col, 1.0, 0.0)


def flipped(x):
    eye = identity(x.shape[1]).astype(x.dtype)
    return lax.dot_general(eye, x, (((1,), (1,)), ((), ())), preferred_element_type=jnp.float32)


def column(x, at):
    lane = lax.broadcasted_iota(jnp.int32, x.shape, 1)
    return jnp.sum(jnp.where(lane == at, x, 0.0), axis=1, keepdims=True)


halves = ((2, 3), (1, 0))
own_order = halves[0] + halves[1]


def pick(index, values):
    chosen = values[0]
    for i, value in enumerate(values):
        if i > 0 and value != values[0]:
            chosen = jnp.where(index == i, value, chosen)
    return chosen


def others(m, z):
    return [k for k in range(m) if k != z]


def joined(m, z, k):
    return z in (0, m - 1) and abs(k - z) > 1


def joins(m, z):
    if z == 1:
        return [(0, k) for k in range(m - 1, 1, -1)]
    if z == m - 2:
        return [(m - 1, k) for k in range(m - 2)]
    return []


def sum_order(m, z):
    far = sorted(others(m, z), key=lambda k: -abs(k - z))
    held = [k for _, k in joins(m, z)]
    first = [k for k in far if k in held or joined(m, z, k)]
    rest = [k for k in far if k not in first]
    ks = [(k, c) for c in range(3) for k in first] + [(k, c) for c in range(3) for k in rest + [z]]
    ks = [kc for kc in ks if kc[0] != z] + [kc for kc in ks if kc[0] == z]
    return [4 * k + c for k, c in ks]


def passed(m, z, k):
    return k == m - 1 and z == m - 3


def deferred(m, z, k):
    return (z == m - 1 and k == m - 2) or (z == m - 2 and k == m - 3)


def give_order(m, z):
    return sorted(others(m, z), key=lambda k: k - z if k > z else k)


def take_order(m, z):
    def rank(k):
        return z if k > z else z - k - 1, abs(k - z) > 1 and k < z, -k

    ks = sorted([k for k in others(m, z) if not passed(m, k, z) and not deferred(m, k, z)], key=rank)
    if m == 4 and z == 0:
        return [14, 15, 10, 11, 6, 7, 13, 5, 12, 4, 9, 8]
    if m == 4 and z == 1 and []:
        return []
    late = [k for k in others(m, z) if passed(m, k, z) or deferred(m, k, z)]
    return [4 * k + c for group in (ks, late) for half in halves for k in group for c in half]


def diverted(z, q):
    return z == 0 and q in [4 + c for c in halves[0]]


def cross_order(m, z):
    chunks = [4 * z + c for c in own_order] + take_order(m, z)
    late = [q for q in chunks if diverted(z, q)]
    chunks = [q for q in chunks if q not in late]
    if late:
        chunks[-4:-4] = late
    return chunks


def block_kernel(
    n, voxels_in, occupancy_in, row_weights_in, column_weights_in, depth_in, kernels_in, expand_in, shrink_in, updated,
    voxels, occupancy, row_weights, column_weights, depth_weights, plane_kernels, expand, shrink, load_s, fetch_s,
    part, rows_in, weights, wide, yz_out, row_sums, turned,
    pair_in, pair_sum, line_in, slab_in, slab_sum, yz_sum, yz_plane, yz_inner,
    row_other, row_slots, row_plane, row_inner, outs,
    pair_s, pair_r, line_s, line_r, slab_s, slab_r, halo_s, halo_r, row_s, row_r, core_s, core_r, spread_s, spread_r, cross_s, cross_r, divert_s, known,
):
    me = lax.axis_index("gx")
    g = lax.axis_index("gy")
    m = n // 2
    a = me // 2
    b = me % 2
    count, chans, cols = part.shape
    rows = count // n
    bf = jnp.bfloat16
    f32 = jnp.float32
    partner = a * 2 + 1 - b

    def table(make):
        return [make(z) for z in range(m)]

    def feature_row(y):
        return voxels[y].astype(f32) * occupancy[pl.ds(y, 1), :].astype(f32)

    def piece(bb, aa):
        return bb * m + aa + bb * (m - 1 - 2 * aa)

    def owner(j):
        bb = j // m
        aa = j % m
        return (aa + bb * (m - 1 - 2 * aa)) * 2 + bb

    def offset(c):
        starts = [0, rows - reach, reach, 2 * reach]
        return starts[c] if isinstance(c, int) else pick(c, starts)

    def slice_of(bb, q):
        return pl.ds(piece(bb, q // 4) * rows + (q % 4) * reach, reach)

    def remote(src, dst, send, recv, gx, gy=None):
        target = {"gx": gx} if gy is None else {"gx": gx, "gy": gy}
        return pltpu.make_async_remote_copy(
            src_ref=src, dst_ref=dst, send_sem=send, recv_sem=recv, device_id=target, device_id_type=MESH
        )

    place = g * n + piece(b, a)
    last = 2 * n - 1
    before = jnp.maximum(place - 1, 0)
    after = jnp.minimum(place + 1, last)

    barrier = pltpu.get_barrier_semaphore()

    def greet(gx, gy):
        pl.semaphore_signal(barrier, inc=1, device_id={"gx": gx, "gy": gy}, device_id_type=MESH)

    lower = a > 0
    upper = a < m - 1
    slant = jnp.where(b == 0, lower, upper)
    seam_low = place == n - 1
    seam_high = place == n
    greet(partner, g)
    greet(me, 1 - g)
    pl.when(lower)(lambda: greet(jnp.maximum(me - 2, 0), g))
    pl.when(upper)(lambda: greet(jnp.minimum(me + 2, n - 1), g))
    pl.when(slant)(lambda: greet(jnp.clip(me + 2 * b - 1, 0, n - 1), g))
    pl.when(seam_low)(lambda: greet(owner(0), 1 - g))
    pl.when(seam_high)(lambda: greet(owner(n - 1), 1 - g))
    greeters = (
        2 + lower.astype(jnp.int32) + upper.astype(jnp.int32) + slant.astype(jnp.int32)
        + seam_low.astype(jnp.int32) + seam_high.astype(jnp.int32)
    )

    order = table(lambda z: sum_order(m, z))
    steps = 3 * m
    turns = [pick(a, [o[i] for o in order]) for i in range(steps)]

    small = [
        pltpu.make_async_copy(row_weights_in, row_weights, load_s.at[0]),
        pltpu.make_async_copy(occupancy_in, occupancy, load_s.at[1]),
    ]
    large = []
    for bb in (1 - b, b):
        for k in range(m):
            at = pl.ds(piece(bb, k) * rows, rows)
            large.append(pltpu.make_async_copy(voxels_in.at[at], voxels.at[at], load_s.at[2 + len(large) // m]))
    fetches = [
        pltpu.make_async_copy(kernels_in, plane_kernels, fetch_s.at[0]),
        pltpu.make_async_copy(column_weights_in, column_weights, fetch_s.at[1]),
        pltpu.make_async_copy(depth_in, depth_weights, fetch_s.at[2]),
        pltpu.make_async_copy(expand_in, expand, fetch_s.at[3]),
        pltpu.make_async_copy(shrink_in, shrink, fetch_s.at[4]),
    ]
    for copy in small + large + fetches:
        copy.start()

    for copy in small:
        copy.wait()
    rw = jnp.broadcast_to(row_weights[...].astype(f32), (chans, chans))
    rw = jnp.sum(rw * identity(chans), axis=1, keepdims=True)

    def yz_terms(j):
        for c in range(4):
            for r in range(reach):
                part[j * rows + c * reach + r] = (feature_row(j * rows + offset(c) + r) * rw).astype(bf)

    pair_copies = []
    for i, q in enumerate(turns):
        pair_copies.append(remote(part.at[slice_of(1 - b, q)], pair_in.at[q], pair_s.at[0], pair_r.at[min(i, steps - 3)], partner))

    def yz_pieces(bb):
        def some(k, carry):
            yz_terms(piece(bb, k))
            return carry

        lax.fori_loop(0, m, some, 0)

    def loaded(which):
        at = pl.ds(0, m * rows)
        pltpu.make_async_copy(voxels_in.at[at], voxels.at[at], load_s.at[2 + which]).wait()

    loaded(0)
    yz_pieces(1 - b)

    def sent(buffer, size, sem, recv):
        return remote(buffer.at[pl.ds(0, size)], buffer.at[pl.ds(0, size)], sem.at[0], recv.at[0], partner)

    pair_all = sent(part, steps * reach, pair_s, pair_r)
    line_all = sent(pair_sum, steps - 3, line_s, line_r)
    slab_all = sent(part, 2 * (m - 1) * reach, slab_s, slab_r)
    cross_all = sent(yz_out, 4 * m * reach, cross_s, cross_r)
    slab_copies = []
    for dist in range(1, m):
        for side in (-1, 1):
            k = jnp.clip(a + side * dist, 0, m - 1)
            there = (a + side * dist >= 0) & (a + side * dist < m)
            for bb in range(2):
                copy = remote(
                    part.at[slice_of(bb, 4 * k + 3)], slab_in.at[2 * a + bb], slab_s.at[0], slab_r.at[0], k * 2 + b
                )
                slab_copies.append((dist, there, copy))

    def start_slabs(dist):
        for d, there, copy in slab_copies:
            if d == dist:
                pl.when(there)(copy.start)

    pl.semaphore_wait(barrier, greeters)
    for copy in pair_copies:
        copy.start()
    loaded(1)
    yz_pieces(b)
    start_slabs(1)

    def tell(level, side):
        step = 2 if side == 0 else -2
        pl.semaphore_signal(
            known.at[level - 2, side], inc=1, device_id={"gx": jnp.clip(me - step, 0, n - 1), "gy": g}, device_id_type=MESH
        )

    def heard(level, side):
        return (a + level <= m - 1) if side == 0 else (a - level >= 0)

    def tells(level, side):
        return (lower if side == 0 else upper) & heard(level - 1, side)

    def tell_level(level):
        for side in range(2):
            if level > 2:
                pl.when(heard(level - 1, side))(lambda: pl.semaphore_wait(known.at[level - 3, side], 1))
            if level < m:
                pl.when(tells(level, side))(lambda: tell(level, side))

    tell_level(2)
    for level in range(3, m):
        tell_level(level)
        start_slabs(level - 1)

    for copy in fetches:
        copy.wait()
    turned[...] = flipped(column_weights[...])
    row_sums[...] = jnp.zeros(row_sums.shape, f32)
    lane = lax.broadcasted_iota(jnp.int32, (chans, cols), 1)

    group = 4
    share = count // (2 * m)

    def row_terms(first):
        depth = depth_weights[...].astype(f32)

        def some(step, carry):
            xy, xz = row_sums[0], row_sums[1]
            for k in range(group):
                y = first + step * group + k
                f = feature_row(y)
                xy = jnp.where(lane == g * count + y, jnp.sum(f * depth, axis=1, keepdims=True), xy)
                xz = xz + f * column(turned[...], y)
            row_sums[0] = xy
            row_sums[1] = xz
            return carry

        lax.fori_loop(0, share // group, some, 0)

    def flip_plane(p, layer):
        for off in range(3):
            taps = plane_kernels[p, layer, :, off].reshape(3 * chans, chans)
            weights[p, layer, off * chans : (off + 1) * chans, :] = flipped(taps).astype(bf)

    holds = table(lambda z: [k for _, k in joins(m, z)])
    holding = (a == 1) | (a == m - 2)

    def line_copy(i):
        gx, slot = [], []
        for z in range(m):
            k, c = order[z][i] // 4, order[z][i] % 4
            if k == z:
                gx.append(z)
                slot.append(0)
            elif joined(m, z, k):
                via = z + (1 if k > z else -1)
                gx.append(via)
                slot.append(3 * (m - 1) + 3 * holds[via].index(k) + c)
            else:
                gx.append(k)
                slot.append(3 * (z - (z > k)) + c)
        to = pick(a, slot)
        q = turns[i]
        return remote(pair_sum.at[q], line_in.at[to], line_s.at[0], line_r.at[to], pick(a, gx) * 2 + b)

    line_copies = [line_copy(i) for i in range(steps - 3)]
    held = [pick(a, [int(order[z][i] // 4 in holds[z]) for z in range(m)]) for i in range(steps - 3)]

    def reduce_pair(i):
        q = turns[i]
        pair_copies[i].wait_recv()
        mine = part[slice_of(b, q)].astype(f32)
        pair_sum[q] = (mine + pair_in[q].astype(f32)).astype(bf)
        pl.when(held[i] == 0)(line_copies[i].start)

    def reduce_joined(i):
        @pl.when(holding)
        def _():
            q = turns[i]
            slot = 3 * (m - 1) + pick(a, [3 * (holds[z].index(order[z][i] // 4) if holds[z] else 0) + order[z][i] % 4 for z in range(m)])
            remote(pair_sum.at[q], line_in.at[slot], line_s.at[0], line_r.at[slot], partner).wait_recv()
            pair_sum[q] = (pair_sum[q].astype(f32) + line_in[slot].astype(f32)).astype(bf)
            line_copies[i].start()

    def reduce_own(c):
        if c == 0:
            remote(pair_in.at[pl.ds(0, 3)], pair_in.at[pl.ds(0, 3)], pair_s.at[0], pair_r.at[steps - 3], partner).wait_recv()
        q = 4 * a + c
        yz_sum[c] = part[slice_of(b, q)].astype(f32) + pair_in[q].astype(f32)

    def reduce_line(c):
        for i in range(m - 1):
            sources = [sorted(others(m, z), key=lambda s: (abs(s - z), s))[i] for z in range(m)]
            src = pick(a, sources)
            skip = pick(a, [int(joined(m, s, z)) for z, s in enumerate(sources)])

            @pl.when(skip == 0)
            def _():
                slot = 3 * (src - jnp.where(src > a, 1, 0)) + c
                remote(pair_sum.at[slot], line_in.at[slot], line_s.at[0], line_r.at[slot], partner).wait_recv()
                yz_sum[c] = yz_sum[c] + line_in[slot].astype(f32)

    slab_cross = remote(slab_sum, pair_in.at[4 * a + 3], pair_s.at[1], pair_r.at[steps - 2], partner)

    def reduce_slab():
        q = 4 * a + 3
        total = [part[slice_of(bb, q)].astype(f32) for bb in (1 - b, b)]
        sent(slab_in, 2 * (m - 1), slab_s, slab_r).wait_recv()
        for i in range(m - 1):
            src = pick(a, [others(m, z)[i] for z in range(m)])
            for side, bb in enumerate((1 - b, b)):
                slot = 2 * src + bb
                total[side] = total[side] + slab_in[slot].astype(f32)
        slab_sum[...] = total[0].astype(bf)
        slab_cross.start()
        yz_sum[3] = total[1]

    def reduce_slab_own():
        slab_cross.wait_recv()
        yz_sum[3] = yz_sum[3] + pair_in[4 * a + 3].astype(f32)

    for i in range(2):
        row_terms(i * share)
    tell_level(m)
    start_slabs(m - 1)
    for i in range(2, 2 * m):
        row_terms(i * share)
    rows_in[...] = row_sums[...].astype(bf)
    core = remote(rows_in.at[1 - g], row_other.at[...], core_s.at[0], core_r.at[0], me, 1 - g)
    core.start()
    flip_plane(2, 0)
    flip_plane(2, 1)

    first = 5
    for i in range(first):
        reduce_pair(i)
    merges = 3 * (m - 2)
    slab_at = steps - 3 - 1
    done = 0
    for i in range(first, steps - 3):
        if done < merges:
            reduce_joined(done)
            done += 1
        reduce_pair(i)
    reduce_slab()
    core.wait_recv()
    mid = rows_in[g].astype(f32) + row_other[...].astype(f32)
    row_slots[reach] = mid.astype(bf)
    row_copies = []
    for dx in range(-reach, reach + 1):
        if dx != 0:
            slot = reach - dx
            copy = remote(
                row_slots.at[reach], row_slots.at[slot], row_s.at[0], row_r.at[0], jnp.clip(me + dx, 0, n - 1)
            )
            row_copies.append((dx, copy))
            pl.when((me + dx >= 0) & (me + dx < n))(copy.start)
    while done < merges:
        reduce_joined(done)
        done += 1
    for layer in range(2):
        flip_plane(g, layer)
    wide[...] = flipped(expand[...]).astype(bf)

    edge = reach * chans
    halo = [
        (place > 0, place < last, remote(
            yz_plane.at[pl.ds(edge, edge)], yz_plane.at[pl.ds(edge + rows * chans, edge)],
            halo_s.at[0], halo_r.at[0], owner(before % n), before // n,
        )),
        (place < last, place > 0, remote(
            yz_plane.at[pl.ds(rows * chans, edge)], yz_plane.at[pl.ds(0, edge)],
            halo_s.at[1], halo_r.at[1], owner(after % n), after // n,
        )),
    ]

    @pl.when(place == 0)
    def _():
        yz_plane[pl.ds(0, edge), :] = jnp.zeros((edge, cols), bf)

    @pl.when(place == last)
    def _():
        yz_plane[pl.ds(edge + rows * chans, edge), :] = jnp.zeros((edge, cols), bf)

    def settle(c):
        for r in range(reach):
            at = (reach + offset(c) + r) * chans
            yz_plane[at : at + chans, :] = yz_sum[c, r].astype(bf)

    def inner_row(i, keep):
        inner = silu(conv_row(yz_plane[i * chans : (i + 3) * chans, :], weights[2, 0])) * keep
        yz_inner[i * chans : (i + 1) * chans, :] = inner.astype(bf)

    for c in range(2):
        reduce_own(c)
    for c in range(2):
        reduce_line(c)
        settle(c)
        pl.when(halo[c][0])(halo[c][2].start)
    reduce_own(2)
    reduce_slab_own()
    settle(3)
    for i in range(rows - reach, rows):
        inner_row(i, 1.0)
    reduce_line(2)
    settle(2)

    spread_copies = []
    own = piece(b, a)

    def cross_copy(bb, q, pair_at):
        at = slice_of(bb, q)
        return remote(yz_out.at[at], yz_out.at[at], cross_s.at[0], cross_r.at[pair_at], partner)

    def give_half(half):
        for c in half:
            for r in range(reach):
                at = (offset(c) + r) * chans
                done = conv_row(yz_inner[at : at + 3 * chans, :], weights[2, 1])
                yz_out[own * rows + c * reach + r] = done.astype(bf)
        for c in half:
            cross_copy(b, 4 * a + c, own_order.index(c) // 2).start()
        later = table(lambda z: [deferred(m, z, k) for k in give_order(m, z)])
        for turn, i, part_of in [(0, i, half) for i in range(1)] + [(1, i, halves[0]) for i in range(m - 1)] + [(2, i, half) for i in range(1, m - 1)]:
            first_half = half is halves[0]
            if turn == 1 and (first_half or not any(x[i] for x in later)):
                continue
            k = pick(a, [give_order(m, z)[i] for z in range(m)])
            go = [not passed(m, z, give_order(m, z)[i]) for z in range(m)]
            if turn == 1:
                go = [x and later[z][i] for z, x in enumerate(go)]
            elif first_half:
                go = [x and not later[z][i] for z, x in enumerate(go)]
            going = pick(a, [int(x) for x in go])
            for c in part_of:
                q = 4 * a + c
                at = slice_of(b, q)
                copy = remote(yz_out.at[at], yz_out.at[at], spread_s.at[0], spread_r.at[q - jnp.where(a > k, 4, 0)], k * 2 + b)
                pl.when(going == 1)(copy.start)
                spread_copies.append((going == 1, copy))

    for i in range(reach, rows - reach):
        inner_row(i, 1.0)
    give_half(halves[0])
    beside = jnp.minimum(me, reach) + jnp.minimum(n - 1 - me, reach)
    for size in range(1, 2 * reach + 1):
        pl.when(beside == size)(sent(row_slots, size, row_s, row_r).wait_recv)
    for s in range(2 * reach + 1):
        at = me + s - reach
        inside = (at >= 0) & (at < n)
        here = pl.ds(s * chans, chans)

        @pl.when(inside)
        def _():
            row_plane[here, :] = row_slots[s]

        @pl.when(jnp.logical_not(inside))
        def _():
            row_plane[here, :] = jnp.zeros((chans, cols), bf)

    for s in range(3):
        at = me + s - 1
        keep = ((at >= 0) & (at < n)).astype(f32)
        inner = silu(conv_row(row_plane[s * chans : (s + 3) * chans, :], weights[g, 0]))
        row_inner[s * chans : (s + 1) * chans, :] = (inner * keep).astype(bf)
    outs[g] = conv_row(row_inner[...], weights[g, 1]).astype(bf)
    share_out = remote(outs.at[g], outs.at[g], core_s.at[1], core_r.at[1], me, 1 - g)
    share_out.start()
    for _, receives, copy in halo:
        pl.when(receives)(copy.wait_recv)
    inner_row(rows, 1.0)
    inner_row(rows + 1, (place < last).astype(f32))
    inner_row(0, (place > 0).astype(f32))
    inner_row(1, 1.0)
    give_half(halves[1])
    remote(outs.at[1 - g], outs.at[1 - g], core_s.at[1], core_r.at[1], me, 1 - g).wait_recv()

    def finish(*chunks):
        xy_out = outs[0].astype(f32)
        xz_out = outs[1].astype(f32)
        at = []
        for bb, q in chunks:
            c = q % 4
            stored = piece(bb, q // 4) * rows + c * reach
            first = piece(bb, q // 4) * rows + offset(c)
            at += [(stored + r, first + r) for r in range(reach)]
        mixed = []
        for s, y in at:
            product = column(xy_out, g * count + y) * xz_out
            product = product * yz_out[s].astype(f32)
            mixed.append((product_scale * product).astype(bf))
        mixed = jnp.concatenate(mixed, axis=1)
        hidden = silu(jnp.dot(wide[...], mixed, preferred_element_type=f32)).astype(bf)
        branch = jnp.dot(shrink[...], hidden, preferred_element_type=f32)
        for k, (s, y) in enumerate(at):
            updated[y] = (feature_row(y) + branch[:, k * cols : (k + 1) * cols]).astype(bf)

    takes = [pick(a, [take_order(m, z)[i] for z in range(m)]) for i in range(4 * m - 4)]
    hands = a == m - 2
    handed = max(m - 3, 0)

    def hand_copy(q):
        at = slice_of(b, q)
        return remote(yz_out.at[at], yz_out.at[at], spread_s.at[0], spread_r.at[q], (m - 1) * 2 + b)

    def take(i):
        q = takes[i]
        at = slice_of(b, q)
        remote(yz_out.at[at], yz_out.at[at], spread_s.at[0], spread_r.at[q - jnp.where(q // 4 > a, 4, 0)], partner).wait_recv()
        kept = pick(a, [int(not diverted(z, take_order(m, z)[i])) for z in range(m)])
        spot = pick(a, [cross_order(m, z).index(take_order(m, z)[i]) // 2 for z in range(m)])
        pl.when(kept == 1)(cross_copy(b, q, spot).start)
        pl.when(hands & (q // 4 == handed))(hand_copy(q).start)
        return b, q

    crossed = [pick(a, [cross_order(m, z)[i] for z in range(m)]) for i in range(4 * m)]

    def divert_copy(c):
        at = slice_of(1 - b, 4 + c)
        return remote(yz_out.at[at], yz_out.at[at], divert_s.at[0], cross_r.at[cross_order(m, 0).index(4 + c) // 2], b)

    def take_crossed(i):
        q = crossed[i]
        if i % 2 == 0:
            at = pl.ds(0, 2 * reach)
            remote(yz_out.at[at], yz_out.at[at], cross_s.at[0], cross_r.at[i // 2], partner).wait_recv()
        if i < len(halves[0]):
            pl.when(a == 1)(divert_copy(halves[0][i]).start)
        return 1 - b, q

    finish(*[(b, 4 * a + c) for c in own_order])

    def drain():
        pair_all.wait_send()
        slab_cross.wait_send()
        line_all.wait_send()
        slab_all.wait_send()
        for sends, _, copy in halo:
            pl.when(sends)(copy.wait_send)
        core.wait_send()
        share_out.wait_send()
        for size in range(1, 2 * reach + 1):
            pl.when(beside == size)(sent(row_slots, size, row_s, row_r).wait_send)

    pair = 2
    lag = 3
    for i in range(0, len(takes), pair):
        ready = [take(j) for j in range(i, i + pair)]
        ready += [take_crossed(j) for j in range(i - lag * pair, i - lag * pair + pair) if j >= 0]
        finish(*ready)
        if i == 2 * pair:
            drain()
    at = len(takes) - lag * pair
    for size in (4, 4, 2, 2):
        size = min(size, len(crossed) - at)
        if size > 0:
            finish(*[take_crossed(at + j) for j in range(size)])
            at += size
        if at == len(crossed) - 2:
            counts = [
                4 * (m - 1 - sum(passed(m, z, k) for k in others(m, z)) + sum(passed(m, k, m - 1) for k in [m - 3]) * (z == m - 2))
                for z in range(m)
            ]
            for size in sorted(set(counts)):
                amount = sent(yz_out, size * reach, spread_s, spread_r)
                pl.when(pick(a, [int(x == size) for x in counts]) == 1)(amount.wait_send)
    while at < len(crossed):
        finish(take_crossed(at))
        at += 1
    pl.when(a > 0)(cross_all.wait_send)
    pl.when(a == 0)(sent(yz_out, (4 * m - len(halves[0])) * reach, cross_s, cross_r).wait_send)
    pl.when(a == 1)(sent(yz_out, len(halves[0]) * reach, divert_s, cross_r).wait_send)


def fused(voxels, occupancy, row_weights, column_weights, depth_weights, plane_kernels, expand_weight, shrink_weight):
    n = lax.axis_size("gx")
    m = n // 2
    count, cols, chans = voxels.shape[1:]
    rows = count // n
    sets, layers = plane_kernels.shape[:2]
    planes = 2
    span = 2 * reach + 1
    bf = jnp.bfloat16
    f32 = jnp.float32
    dma = pltpu.SemaphoreType.DMA
    operands = (
        voxels[0].transpose(0, 2, 1),
        occupancy[0],
        row_weights,
        column_weights,
        depth_weights.T,
        plane_kernels,
        expand_weight,
        shrink_weight.T,
    )
    updated = pl.pallas_call(
        functools.partial(block_kernel, n),
        out_shape=pltpu.VMEM((count, chans, cols), bf),
        in_specs=[pl.BlockSpec(memory_space=pl.ANY) for _ in operands],
        out_specs=pl.BlockSpec(memory_space=pltpu.VMEM),
        scratch_shapes=[pltpu.VMEM(x.shape, x.dtype) for x in operands]
        + [
            dma((4,)),
            dma((5,)),
            pltpu.VMEM((count, chans, cols), bf),
            pltpu.VMEM((planes, chans, cols), bf),
            pltpu.VMEM((sets, layers, 3 * chans, 3 * chans), bf),
            pltpu.VMEM(expand_weight.shape[::-1], bf),
            pltpu.VMEM((count, chans, cols), bf),
            pltpu.VMEM((planes, chans, cols), f32),
            pltpu.VMEM((chans, count), f32),
            pltpu.VMEM((4 * m, reach, chans, cols), bf),
            pltpu.VMEM((4 * m, reach, chans, cols), bf),
            pltpu.VMEM((6 * m, reach, chans, cols), bf),
            pltpu.VMEM((2 * m, reach, chans, cols), bf),
            pltpu.VMEM((reach, chans, cols), bf),
            pltpu.VMEM((4, reach, chans, cols), f32),
            pltpu.VMEM(((rows + 4) * chans, cols), bf),
            pltpu.VMEM(((rows + 2) * chans, cols), bf),
            pltpu.VMEM((chans, cols), bf),
            pltpu.VMEM((span, chans, cols), bf),
            pltpu.VMEM((span * chans, cols), bf),
            pltpu.VMEM((3 * chans, cols), bf),
            pltpu.VMEM((planes, chans, cols), bf),
            dma((2,)), dma((3 * m - 1,)), dma((1,)), dma((6 * m - 9,)), dma((1,)), dma((1,)), dma((2,)), dma((2,)),
            dma((1,)), dma((1,)), dma((2,)), dma((2,)),
            dma((1,)), dma((4 * m - 4,)), dma((1,)), dma((2 * m,)), dma((1,)),
            pltpu.SemaphoreType.REGULAR((m - 2, 2)),
        ],
        compiler_params=pltpu.CompilerParams(collective_id=0, has_side_effects=True),
    )(*operands)
    return updated.transpose(0, 2, 1)[None]


def fits(voxels):
    n = lax.axis_size("gx")
    sides = lax.axis_size("gy")
    xs, ys, zs, _ = voxels.shape
    return xs == 1 and sides == 2 and n % 2 == 0 and n >= 8 and ys == n * 4 * reach and 2 * ys == zs


def plain_planes(features, row_weights, column_weights, depth_weights, plane_kernels):
    xy_plane = jnp.einsum(
        "xyzc,zc->xyc", features, depth_weights, preferred_element_type=jnp.float32
    ).astype(jnp.bfloat16)
    xz_part = jnp.einsum(
        "xyzc,yc->xzc", features, column_weights, preferred_element_type=jnp.float32
    )
    yz_part = jnp.einsum("xyzc,xc->yzc", features, row_weights, preferred_element_type=jnp.float32)
    xy_out = plane_block(xy_plane, plane_kernels[0], rim_xy)
    xz_plane = lax.psum(xz_part, "gy").astype(jnp.bfloat16)
    xz_out = plane_block(xz_plane, plane_kernels[1], rim_xz)
    yz_plane = lax.psum(yz_part, "gx").astype(jnp.bfloat16)
    yz_out = plane_block(yz_plane, plane_kernels[2], rim_yz)
    return xy_out, xz_out, yz_out


def shards(
    voxels,
    occupancy,
    row_weights,
    column_weights,
    depth_weights,
    plane_kernels,
    expand_weight,
    shrink_weight,
):
    if fits(voxels):
        return fused(
            voxels,
            occupancy,
            row_weights,
            column_weights,
            depth_weights,
            plane_kernels,
            expand_weight,
            shrink_weight,
        )
    features = voxels * occupancy.astype(jnp.bfloat16)[..., None]
    xy_out, xz_out, yz_out = plain_planes(features, row_weights, column_weights, depth_weights, plane_kernels)
    product = xy_out.astype(jnp.float32)[:, :, None, :] * xz_out.astype(jnp.float32)[:, None, :, :]
    product = product * yz_out.astype(jnp.float32)[None, :, :, :]
    mixed = (product_scale * product).astype(jnp.bfloat16)
    hidden = jax.nn.silu(
        jnp.einsum("xyzc,ch->xyzh", mixed, expand_weight, preferred_element_type=jnp.float32)
    ).astype(jnp.bfloat16)
    branch = jnp.einsum("xyzh,hc->xyzc", hidden, shrink_weight, preferred_element_type=jnp.float32)
    return (features.astype(jnp.float32) + branch).astype(jnp.bfloat16)


def solution(mesh):
    in_specs = (
        P(("groups", "gx"), "gy", None, None),
        P(("groups", "gx"), "gy", None),
        P("gx", None),
        P("gy", None),
        P(),
        P(),
        P(),
        P(),
    )
    out_specs = P(("groups", "gx"), "gy", None, None)
    return jax.shard_map(shards, mesh=mesh, in_specs=in_specs, out_specs=out_specs, check_vma=False)
```

```python
import functools

import jax
import jax.numpy as jnp
from jax import lax
from jax.experimental import pallas as pl
from jax.experimental.pallas import tpu as pltpu
from jax.sharding import PartitionSpec as P

MESH = pl.DeviceIdType.MESH
reach = 2

product_scale = 8.0


def with_halo(cells, sides, width):
    for axis, dim in sides:
        count = lax.axis_size(axis)
        ends = count - 1
        head = lax.slice_in_dim(cells, 0, width, axis=dim)
        tail = lax.slice_in_dim(cells, cells.shape[dim] - width, cells.shape[dim], axis=dim)
        cells = jnp.concatenate(
            [
                lax.ppermute(tail, axis, [(i, (i + 1) % count) for i in range(ends)]),
                cells,
                lax.ppermute(head, axis, [((i + 1) % count, i) for i in range(ends)]),
            ],
            axis=dim,
        )
    return cells


def conv_valid(padded, kernel):
    rows = padded.shape[0] - 2
    cols = padded.shape[1] - 2
    total = jnp.zeros((rows, cols, kernel.shape[-1]), jnp.float32)
    for row_off in range(3):
        for col_off in range(3):
            window = padded[row_off : row_off + rows, col_off : col_off + cols]
            total = total + jnp.einsum(
                "ijc,co->ijo", window, kernel[row_off, col_off], preferred_element_type=jnp.float32
            )
    return total


def plane_block(plane, kernels, extend):
    inner = jax.nn.silu(conv_valid(extend(plane), kernels[0])).astype(jnp.bfloat16)
    return conv_valid(extend(inner), kernels[1]).astype(jnp.bfloat16)


def rim_xy(plane):
    return with_halo(plane, (("gx", 0), ("gy", 1)), 1)


def rim_xz(plane):
    padded = with_halo(plane, (("gx", 0),), 1)
    return jnp.pad(padded, ((0, 0), (1, 1), (0, 0)))


def rim_yz(plane):
    padded = with_halo(plane, (("gy", 0),), 1)
    return jnp.pad(padded, ((0, 0), (1, 1), (0, 0)))


def conv_row(window, weight):
    taps = jnp.dot(weight, window, preferred_element_type=jnp.float32)
    chans = taps.shape[0] // 3
    cols = taps.shape[1]
    lane = lax.broadcasted_iota(jnp.int32, (chans, cols), 1)
    left = pltpu.roll(taps[:chans], 1, 1)
    right = pltpu.roll(taps[2 * chans :], cols - 1, 1)
    left = jnp.where(lane == 0, 0.0, left)
    right = jnp.where(lane == cols - 1, 0.0, right)
    return taps[chans : 2 * chans] + left + right


def silu(v):
    half = 0.5 * v
    return half + half * jnp.tanh(half)


def identity(size):
    row = lax.broadcasted_iota(jnp.int32, (size, size), 0)
    col = lax.broadcasted_iota(jnp.int32, (size, size), 1)
    return jnp.where(row == col, 1.0, 0.0)


def flipped(x):
    eye = identity(x.shape[1]).astype(x.dtype)
    return lax.dot_general(eye, x, (((1,), (1,)), ((), ())), preferred_element_type=jnp.float32)


def column(x, at):
    lane = lax.broadcasted_iota(jnp.int32, x.shape, 1)
    return jnp.sum(jnp.where(lane == at, x, 0.0), axis=1, keepdims=True)


halves = ((2, 3), (1, 0))
own_order = halves[0] + halves[1]


def pick(index, values):
    chosen = values[0]
    for i, value in enumerate(values):
        if i > 0 and value != values[0]:
            chosen = jnp.where(index == i, value, chosen)
    return chosen


def others(m, z):
    return [k for k in range(m) if k != z]


def joined(m, z, k):
    return z in (0, m - 1) and abs(k - z) > 1


def joins(m, z):
    if z == 1:
        return [(0, k) for k in range(m - 1, 1, -1)]
    if z == m - 2:
        return [(m - 1, k) for k in range(m - 2)]
    return []


def sum_order(m, z):
    far = sorted(others(m, z), key=lambda k: -abs(k - z))
    held = [k for _, k in joins(m, z)]
    first = [k for k in far if k in held or joined(m, z, k)]
    rest = [k for k in far if k not in first]
    ks = [(k, c) for c in range(3) for k in first] + [(k, c) for c in range(3) for k in rest + [z]]
    ks = [kc for kc in ks if kc[0] != z] + [kc for kc in ks if kc[0] == z]
    return [4 * k + c for k, c in ks]


def passed(m, z, k):
    return k == m - 1 and z == m - 3


def deferred(m, z, k):
    return (z == m - 1 and k == m - 2) or (z == m - 2 and k == m - 3)


def give_order(m, z):
    return sorted(others(m, z), key=lambda k: k - z if k > z else k)


def take_order(m, z):
    def rank(k):
        return z if k > z else z - k - 1, abs(k - z) > 1 and k < z, -k

    ks = sorted([k for k in others(m, z) if not passed(m, k, z) and not deferred(m, k, z)], key=rank)
    if m == 4 and z == 0:
        return [14, 15, 10, 11, 13, 12, 6, 7, 9, 8, 5, 4]
    if m == 4 and z == 1 and []:
        return []
    late = [k for k in others(m, z) if passed(m, k, z) or deferred(m, k, z)]
    return [4 * k + c for group in (ks, late) for half in halves for k in group for c in half]


def diverted(z, q):
    return z == 0 and q in [4 + c for c in halves[0]]


def cross_order(m, z):
    chunks = [4 * z + c for c in own_order] + take_order(m, z)
    late = [q for q in chunks if diverted(z, q)]
    chunks = [q for q in chunks if q not in late]
    if late:
        chunks[-4:-4] = late
    return chunks


def block_kernel(
    n, voxels_in, occupancy_in, row_weights_in, column_weights_in, depth_in, kernels_in, expand_in, shrink_in, updated,
    voxels, occupancy, row_weights, column_weights, depth_weights, plane_kernels, expand, shrink, load_s, fetch_s,
    part, rows_in, weights, wide, yz_out, row_sums, turned,
    pair_in, pair_sum, line_in, slab_in, slab_sum, yz_sum, yz_plane, yz_inner,
    row_other, row_slots, row_plane, row_inner, outs,
    pair_s, pair_r, line_s, line_r, slab_s, slab_r, halo_s, halo_r, row_s, row_r, core_s, core_r, spread_s, spread_r, cross_s, cross_r, divert_s, known,
):
    me = lax.axis_index("gx")
    g = lax.axis_index("gy")
    m = n // 2
    a = me // 2
    b = me % 2
    count, chans, cols = part.shape
    rows = count // n
    bf = jnp.bfloat16
    f32 = jnp.float32
    partner = a * 2 + 1 - b

    def table(make):
        return [make(z) for z in range(m)]

    def feature_row(y):
        return voxels[y].astype(f32) * occupancy[pl.ds(y, 1), :].astype(f32)

    def piece(bb, aa):
        return bb * m + aa + bb * (m - 1 - 2 * aa)

    def owner(j):
        bb = j // m
        aa = j % m
        return (aa + bb * (m - 1 - 2 * aa)) * 2 + bb

    def offset(c):
        starts = [0, rows - reach, reach, 2 * reach]
        return starts[c] if isinstance(c, int) else pick(c, starts)

    def slice_of(bb, q):
        return pl.ds(piece(bb, q // 4) * rows + (q % 4) * reach, reach)

    def remote(src, dst, send, recv, gx, gy=None):
        target = {"gx": gx} if gy is None else {"gx": gx, "gy": gy}
        return pltpu.make_async_remote_copy(
            src_ref=src, dst_ref=dst, send_sem=send, recv_sem=recv, device_id=target, device_id_type=MESH
        )

    place = g * n + piece(b, a)
    last = 2 * n - 1
    before = jnp.maximum(place - 1, 0)
    after = jnp.minimum(place + 1, last)

    barrier = pltpu.get_barrier_semaphore()

    def greet(gx, gy):
        pl.semaphore_signal(barrier, inc=1, device_id={"gx": gx, "gy": gy}, device_id_type=MESH)

    lower = a > 0
    upper = a < m - 1
    slant = jnp.where(b == 0, lower, upper)
    seam_low = place == n - 1
    seam_high = place == n
    greet(partner, g)
    greet(me, 1 - g)
    pl.when(lower)(lambda: greet(jnp.maximum(me - 2, 0), g))
    pl.when(upper)(lambda: greet(jnp.minimum(me + 2, n - 1), g))
    pl.when(slant)(lambda: greet(jnp.clip(me + 2 * b - 1, 0, n - 1), g))
    pl.when(seam_low)(lambda: greet(owner(0), 1 - g))
    pl.when(seam_high)(lambda: greet(owner(n - 1), 1 - g))
    greeters = (
        2 + lower.astype(jnp.int32) + upper.astype(jnp.int32) + slant.astype(jnp.int32)
        + seam_low.astype(jnp.int32) + seam_high.astype(jnp.int32)
    )

    order = table(lambda z: sum_order(m, z))
    steps = 3 * m
    turns = [pick(a, [o[i] for o in order]) for i in range(steps)]

    small = [
        pltpu.make_async_copy(row_weights_in, row_weights, load_s.at[0]),
        pltpu.make_async_copy(occupancy_in, occupancy, load_s.at[1]),
    ]
    large = []
    for bb in (1 - b, b):
        for k in range(m):
            at = pl.ds(piece(bb, k) * rows, rows)
            large.append(pltpu.make_async_copy(voxels_in.at[at], voxels.at[at], load_s.at[2 + len(large) // m]))
    fetches = [
        pltpu.make_async_copy(kernels_in, plane_kernels, fetch_s.at[0]),
        pltpu.make_async_copy(column_weights_in, column_weights, fetch_s.at[1]),
        pltpu.make_async_copy(depth_in, depth_weights, fetch_s.at[2]),
        pltpu.make_async_copy(expand_in, expand, fetch_s.at[3]),
        pltpu.make_async_copy(shrink_in, shrink, fetch_s.at[4]),
    ]
    for copy in small + large + fetches:
        copy.start()

    for copy in small:
        copy.wait()
    rw = jnp.broadcast_to(row_weights[...].astype(f32), (chans, chans))
    rw = jnp.sum(rw * identity(chans), axis=1, keepdims=True)

    def yz_terms(j):
        for c in range(4):
            for r in range(reach):
                part[j * rows + c * reach + r] = (feature_row(j * rows + offset(c) + r) * rw).astype(bf)

    pair_copies = []
    for i, q in enumerate(turns):
        pair_copies.append(remote(part.at[slice_of(1 - b, q)], pair_in.at[q], pair_s.at[0], pair_r.at[min(i, steps - 3)], partner))

    def yz_pieces(bb):
        def some(k, carry):
            yz_terms(piece(bb, k))
            return carry

        lax.fori_loop(0, m, some, 0)

    def loaded(which):
        at = pl.ds(0, m * rows)
        pltpu.make_async_copy(voxels_in.at[at], voxels.at[at], load_s.at[2 + which]).wait()

    loaded(0)
    yz_pieces(1 - b)

    def sent(buffer, size, sem, recv):
        return remote(buffer.at[pl.ds(0, size)], buffer.at[pl.ds(0, size)], sem.at[0], recv.at[0], partner)

    pair_all = sent(part, steps * reach, pair_s, pair_r)
    line_all = sent(pair_sum, steps - 3, line_s, line_r)
    slab_all = sent(part, 2 * (m - 1) * reach, slab_s, slab_r)
    cross_all = sent(yz_out, 4 * m * reach, cross_s, cross_r)
    slab_copies = []
    for dist in range(1, m):
        for side in (-1, 1):
            k = jnp.clip(a + side * dist, 0, m - 1)
            there = (a + side * dist >= 0) & (a + side * dist < m)
            for bb in range(2):
                copy = remote(
                    part.at[slice_of(bb, 4 * k + 3)], slab_in.at[2 * a + bb], slab_s.at[0], slab_r.at[0], k * 2 + b
                )
                slab_copies.append((dist, there, copy))

    def start_slabs(dist):
        for d, there, copy in slab_copies:
            if d == dist:
                pl.when(there)(copy.start)

    pl.semaphore_wait(barrier, greeters)
    for copy in pair_copies:
        copy.start()
    loaded(1)
    yz_pieces(b)
    start_slabs(1)

    def tell(level, side):
        step = 2 if side == 0 else -2
        pl.semaphore_signal(
            known.at[level - 2, side], inc=1, device_id={"gx": jnp.clip(me - step, 0, n - 1), "gy": g}, device_id_type=MESH
        )

    def heard(level, side):
        return (a + level <= m - 1) if side == 0 else (a - level >= 0)

    def tells(level, side):
        return (lower if side == 0 else upper) & heard(level - 1, side)

    def tell_level(level):
        for side in range(2):
            if level > 2:
                pl.when(heard(level - 1, side))(lambda: pl.semaphore_wait(known.at[level - 3, side], 1))
            if level < m:
                pl.when(tells(level, side))(lambda: tell(level, side))

    tell_level(2)
    for level in range(3, m):
        tell_level(level)
        start_slabs(level - 1)

    for copy in fetches:
        copy.wait()
    turned[...] = flipped(column_weights[...])
    row_sums[...] = jnp.zeros(row_sums.shape, f32)
    lane = lax.broadcasted_iota(jnp.int32, (chans, cols), 1)

    group = 4
    share = count // (2 * m)

    def row_terms(first):
        depth = depth_weights[...].astype(f32)

        def some(step, carry):
            xy, xz = row_sums[0], row_sums[1]
            for k in range(group):
                y = first + step * group + k
                f = feature_row(y)
                xy = jnp.where(lane == g * count + y, jnp.sum(f * depth, axis=1, keepdims=True), xy)
                xz = xz + f * column(turned[...], y)
            row_sums[0] = xy
            row_sums[1] = xz
            return carry

        lax.fori_loop(0, share // group, some, 0)

    def flip_plane(p, layer):
        for off in range(3):
            taps = plane_kernels[p, layer, :, off].reshape(3 * chans, chans)
            weights[p, layer, off * chans : (off + 1) * chans, :] = flipped(taps).astype(bf)

    holds = table(lambda z: [k for _, k in joins(m, z)])
    holding = (a == 1) | (a == m - 2)

    def line_copy(i):
        gx, slot = [], []
        for z in range(m):
            k, c = order[z][i] // 4, order[z][i] % 4
            if k == z:
                gx.append(z)
                slot.append(0)
            elif joined(m, z, k):
                via = z + (1 if k > z else -1)
                gx.append(via)
                slot.append(3 * (m - 1) + 3 * holds[via].index(k) + c)
            else:
                gx.append(k)
                slot.append(3 * (z - (z > k)) + c)
        to = pick(a, slot)
        q = turns[i]
        return remote(pair_sum.at[q], line_in.at[to], line_s.at[0], line_r.at[to], pick(a, gx) * 2 + b)

    line_copies = [line_copy(i) for i in range(steps - 3)]
    held = [pick(a, [int(order[z][i] // 4 in holds[z]) for z in range(m)]) for i in range(steps - 3)]

    def reduce_pair(i):
        q = turns[i]
        pair_copies[i].wait_recv()
        mine = part[slice_of(b, q)].astype(f32)
        pair_sum[q] = (mine + pair_in[q].astype(f32)).astype(bf)
        pl.when(held[i] == 0)(line_copies[i].start)

    def reduce_joined(i):
        @pl.when(holding)
        def _():
            q = turns[i]
            slot = 3 * (m - 1) + pick(a, [3 * (holds[z].index(order[z][i] // 4) if holds[z] else 0) + order[z][i] % 4 for z in range(m)])
            remote(pair_sum.at[q], line_in.at[slot], line_s.at[0], line_r.at[slot], partner).wait_recv()
            pair_sum[q] = (pair_sum[q].astype(f32) + line_in[slot].astype(f32)).astype(bf)
            line_copies[i].start()

    def reduce_own(c):
        if c == 0:
            remote(pair_in.at[pl.ds(0, 3)], pair_in.at[pl.ds(0, 3)], pair_s.at[0], pair_r.at[steps - 3], partner).wait_recv()
        q = 4 * a + c
        yz_sum[c] = part[slice_of(b, q)].astype(f32) + pair_in[q].astype(f32)

    def reduce_line(c):
        for i in range(m - 1):
            sources = [sorted(others(m, z), key=lambda s: (abs(s - z), s))[i] for z in range(m)]
            src = pick(a, sources)
            skip = pick(a, [int(joined(m, s, z)) for z, s in enumerate(sources)])

            @pl.when(skip == 0)
            def _():
                slot = 3 * (src - jnp.where(src > a, 1, 0)) + c
                remote(pair_sum.at[slot], line_in.at[slot], line_s.at[0], line_r.at[slot], partner).wait_recv()
                yz_sum[c] = yz_sum[c] + line_in[slot].astype(f32)

    slab_cross = remote(slab_sum, pair_in.at[4 * a + 3], pair_s.at[1], pair_r.at[steps - 2], partner)

    def reduce_slab():
        q = 4 * a + 3
        total = [part[slice_of(bb, q)].astype(f32) for bb in (1 - b, b)]
        sent(slab_in, 2 * (m - 1), slab_s, slab_r).wait_recv()
        for i in range(m - 1):
            src = pick(a, [others(m, z)[i] for z in range(m)])
            for side, bb in enumerate((1 - b, b)):
                slot = 2 * src + bb
                total[side] = total[side] + slab_in[slot].astype(f32)
        slab_sum[...] = total[0].astype(bf)
        slab_cross.start()
        yz_sum[3] = total[1]

    def reduce_slab_own():
        slab_cross.wait_recv()
        yz_sum[3] = yz_sum[3] + pair_in[4 * a + 3].astype(f32)

    for i in range(2):
        row_terms(i * share)
    tell_level(m)
    start_slabs(m - 1)
    for i in range(2, 2 * m):
        row_terms(i * share)
    rows_in[...] = row_sums[...].astype(bf)
    core = remote(rows_in.at[1 - g], row_other.at[...], core_s.at[0], core_r.at[0], me, 1 - g)
    core.start()
    flip_plane(2, 0)
    flip_plane(2, 1)

    first = 5
    for i in range(first):
        reduce_pair(i)
    merges = 3 * (m - 2)
    slab_at = steps - 3 - 1
    done = 0
    for i in range(first, steps - 3):
        if done < merges:
            reduce_joined(done)
            done += 1
        reduce_pair(i)
    reduce_slab()
    core.wait_recv()
    mid = rows_in[g].astype(f32) + row_other[...].astype(f32)
    row_slots[reach] = mid.astype(bf)
    row_copies = []
    for dx in range(-reach, reach + 1):
        if dx != 0:
            slot = reach - dx
            copy = remote(
                row_slots.at[reach], row_slots.at[slot], row_s.at[0], row_r.at[0], jnp.clip(me + dx, 0, n - 1)
            )
            row_copies.append((dx, copy))
            pl.when((me + dx >= 0) & (me + dx < n))(copy.start)
    while done < merges:
        reduce_joined(done)
        done += 1
    for layer in range(2):
        flip_plane(g, layer)
    wide[...] = flipped(expand[...]).astype(bf)

    edge = reach * chans
    halo = [
        (place > 0, place < last, remote(
            yz_plane.at[pl.ds(edge, edge)], yz_plane.at[pl.ds(edge + rows * chans, edge)],
            halo_s.at[0], halo_r.at[0], owner(before % n), before // n,
        )),
        (place < last, place > 0, remote(
            yz_plane.at[pl.ds(rows * chans, edge)], yz_plane.at[pl.ds(0, edge)],
            halo_s.at[1], halo_r.at[1], owner(after % n), after // n,
        )),
    ]

    @pl.when(place == 0)
    def _():
        yz_plane[pl.ds(0, edge), :] = jnp.zeros((edge, cols), bf)

    @pl.when(place == last)
    def _():
        yz_plane[pl.ds(edge + rows * chans, edge), :] = jnp.zeros((edge, cols), bf)

    def settle(c):
        for r in range(reach):
            at = (reach + offset(c) + r) * chans
            yz_plane[at : at + chans, :] = yz_sum[c, r].astype(bf)

    def inner_row(i, keep):
        inner = silu(conv_row(yz_plane[i * chans : (i + 3) * chans, :], weights[2, 0])) * keep
        yz_inner[i * chans : (i + 1) * chans, :] = inner.astype(bf)

    for c in range(2):
        reduce_own(c)
    for c in range(2):
        reduce_line(c)
        settle(c)
        pl.when(halo[c][0])(halo[c][2].start)
    reduce_own(2)
    reduce_slab_own()
    settle(3)
    for i in range(rows - reach, rows):
        inner_row(i, 1.0)
    reduce_line(2)
    settle(2)

    spread_copies = []
    own = piece(b, a)

    def cross_copy(bb, q, pair_at):
        at = slice_of(bb, q)
        return remote(yz_out.at[at], yz_out.at[at], cross_s.at[0], cross_r.at[pair_at], partner)

    def give_half(half):
        for c in half:
            for r in range(reach):
                at = (offset(c) + r) * chans
                done = conv_row(yz_inner[at : at + 3 * chans, :], weights[2, 1])
                yz_out[own * rows + c * reach + r] = done.astype(bf)
        for c in half:
            cross_copy(b, 4 * a + c, own_order.index(c) // 2).start()
        later = table(lambda z: [deferred(m, z, k) for k in give_order(m, z)])
        for turn, i, part_of in [(0, i, half) for i in range(1)] + [(1, i, halves[0]) for i in range(m - 1)] + [(2, i, half) for i in range(1, m - 1)]:
            first_half = half is halves[0]
            if turn == 1 and (first_half or not any(x[i] for x in later)):
                continue
            k = pick(a, [give_order(m, z)[i] for z in range(m)])
            go = [not passed(m, z, give_order(m, z)[i]) for z in range(m)]
            if turn == 1:
                go = [x and later[z][i] for z, x in enumerate(go)]
            elif first_half:
                go = [x and not later[z][i] for z, x in enumerate(go)]
            going = pick(a, [int(x) for x in go])
            for c in part_of:
                q = 4 * a + c
                at = slice_of(b, q)
                copy = remote(yz_out.at[at], yz_out.at[at], spread_s.at[0], spread_r.at[q - jnp.where(a > k, 4, 0)], k * 2 + b)
                pl.when(going == 1)(copy.start)
                spread_copies.append((going == 1, copy))

    for i in range(reach, rows - reach):
        inner_row(i, 1.0)
    give_half(halves[0])
    beside = jnp.minimum(me, reach) + jnp.minimum(n - 1 - me, reach)
    for size in range(1, 2 * reach + 1):
        pl.when(beside == size)(sent(row_slots, size, row_s, row_r).wait_recv)
    for s in range(2 * reach + 1):
        at = me + s - reach
        inside = (at >= 0) & (at < n)
        here = pl.ds(s * chans, chans)

        @pl.when(inside)
        def _():
            row_plane[here, :] = row_slots[s]

        @pl.when(jnp.logical_not(inside))
        def _():
            row_plane[here, :] = jnp.zeros((chans, cols), bf)

    for s in range(3):
        at = me + s - 1
        keep = ((at >= 0) & (at < n)).astype(f32)
        inner = silu(conv_row(row_plane[s * chans : (s + 3) * chans, :], weights[g, 0]))
        row_inner[s * chans : (s + 1) * chans, :] = (inner * keep).astype(bf)
    outs[g] = conv_row(row_inner[...], weights[g, 1]).astype(bf)
    share_out = remote(outs.at[g], outs.at[g], core_s.at[1], core_r.at[1], me, 1 - g)
    share_out.start()
    for _, receives, copy in halo:
        pl.when(receives)(copy.wait_recv)
    inner_row(rows, 1.0)
    inner_row(rows + 1, (place < last).astype(f32))
    inner_row(0, (place > 0).astype(f32))
    inner_row(1, 1.0)
    give_half(halves[1])
    remote(outs.at[1 - g], outs.at[1 - g], core_s.at[1], core_r.at[1], me, 1 - g).wait_recv()

    def finish(*chunks):
        xy_out = outs[0].astype(f32)
        xz_out = outs[1].astype(f32)
        at = []
        for bb, q in chunks:
            c = q % 4
            stored = piece(bb, q // 4) * rows + c * reach
            first = piece(bb, q // 4) * rows + offset(c)
            at += [(stored + r, first + r) for r in range(reach)]
        mixed = []
        for s, y in at:
            product = column(xy_out, g * count + y) * xz_out
            product = product * yz_out[s].astype(f32)
            mixed.append((product_scale * product).astype(bf))
        mixed = jnp.concatenate(mixed, axis=1)
        hidden = silu(jnp.dot(wide[...], mixed, preferred_element_type=f32)).astype(bf)
        branch = jnp.dot(shrink[...], hidden, preferred_element_type=f32)
        for k, (s, y) in enumerate(at):
            updated[y] = (feature_row(y) + branch[:, k * cols : (k + 1) * cols]).astype(bf)

    takes = [pick(a, [take_order(m, z)[i] for z in range(m)]) for i in range(4 * m - 4)]
    hands = a == m - 2
    handed = max(m - 3, 0)

    def hand_copy(q):
        at = slice_of(b, q)
        return remote(yz_out.at[at], yz_out.at[at], spread_s.at[0], spread_r.at[q], (m - 1) * 2 + b)

    def take(i):
        q = takes[i]
        at = slice_of(b, q)
        remote(yz_out.at[at], yz_out.at[at], spread_s.at[0], spread_r.at[q - jnp.where(q // 4 > a, 4, 0)], partner).wait_recv()
        kept = pick(a, [int(not diverted(z, take_order(m, z)[i])) for z in range(m)])
        spot = pick(a, [cross_order(m, z).index(take_order(m, z)[i]) // 2 for z in range(m)])
        pl.when(kept == 1)(cross_copy(b, q, spot).start)
        pl.when(hands & (q // 4 == handed))(hand_copy(q).start)
        return b, q

    crossed = [pick(a, [cross_order(m, z)[i] for z in range(m)]) for i in range(4 * m)]

    def divert_copy(c):
        at = slice_of(1 - b, 4 + c)
        return remote(yz_out.at[at], yz_out.at[at], divert_s.at[0], cross_r.at[cross_order(m, 0).index(4 + c) // 2], b)

    def take_crossed(i):
        q = crossed[i]
        if i % 2 == 0:
            at = pl.ds(0, 2 * reach)
            remote(yz_out.at[at], yz_out.at[at], cross_s.at[0], cross_r.at[i // 2], partner).wait_recv()
        if i < len(halves[0]):
            pl.when(a == 1)(divert_copy(halves[0][i]).start)
        return 1 - b, q

    finish(*[(b, 4 * a + c) for c in own_order])

    def drain():
        pair_all.wait_send()
        slab_cross.wait_send()
        line_all.wait_send()
        slab_all.wait_send()
        for sends, _, copy in halo:
            pl.when(sends)(copy.wait_send)
        core.wait_send()
        share_out.wait_send()
        for size in range(1, 2 * reach + 1):
            pl.when(beside == size)(sent(row_slots, size, row_s, row_r).wait_send)

    pair = 2
    lag = 3
    for i in range(0, len(takes), pair):
        ready = [take(j) for j in range(i, i + pair)]
        ready += [take_crossed(j) for j in range(i - lag * pair, i - lag * pair + pair) if j >= 0]
        finish(*ready)
        if i == 2 * pair:
            drain()
    at = len(takes) - lag * pair
    for size in (4, 4, 2, 2):
        size = min(size, len(crossed) - at)
        if size > 0:
            finish(*[take_crossed(at + j) for j in range(size)])
            at += size
        if at == len(crossed) - 2:
            counts = [
                4 * (m - 1 - sum(passed(m, z, k) for k in others(m, z)) + sum(passed(m, k, m - 1) for k in [m - 3]) * (z == m - 2))
                for z in range(m)
            ]
            for size in sorted(set(counts)):
                amount = sent(yz_out, size * reach, spread_s, spread_r)
                pl.when(pick(a, [int(x == size) for x in counts]) == 1)(amount.wait_send)
    while at < len(crossed):
        finish(take_crossed(at))
        at += 1
    pl.when(a > 0)(cross_all.wait_send)
    pl.when(a == 0)(sent(yz_out, (4 * m - len(halves[0])) * reach, cross_s, cross_r).wait_send)
    pl.when(a == 1)(sent(yz_out, len(halves[0]) * reach, divert_s, cross_r).wait_send)


def fused(voxels, occupancy, row_weights, column_weights, depth_weights, plane_kernels, expand_weight, shrink_weight):
    n = lax.axis_size("gx")
    m = n // 2
    count, cols, chans = voxels.shape[1:]
    rows = count // n
    sets, layers = plane_kernels.shape[:2]
    planes = 2
    span = 2 * reach + 1
    bf = jnp.bfloat16
    f32 = jnp.float32
    dma = pltpu.SemaphoreType.DMA
    operands = (
        voxels[0].transpose(0, 2, 1),
        occupancy[0],
        row_weights,
        column_weights,
        depth_weights.T,
        plane_kernels,
        expand_weight,
        shrink_weight.T,
    )
    updated = pl.pallas_call(
        functools.partial(block_kernel, n),
        out_shape=pltpu.VMEM((count, chans, cols), bf),
        in_specs=[pl.BlockSpec(memory_space=pl.ANY) for _ in operands],
        out_specs=pl.BlockSpec(memory_space=pltpu.VMEM),
        scratch_shapes=[pltpu.VMEM(x.shape, x.dtype) for x in operands]
        + [
            dma((4,)),
            dma((5,)),
            pltpu.VMEM((count, chans, cols), bf),
            pltpu.VMEM((planes, chans, cols), bf),
            pltpu.VMEM((sets, layers, 3 * chans, 3 * chans), bf),
            pltpu.VMEM(expand_weight.shape[::-1], bf),
            pltpu.VMEM((count, chans, cols), bf),
            pltpu.VMEM((planes, chans, cols), f32),
            pltpu.VMEM((chans, count), f32),
            pltpu.VMEM((4 * m, reach, chans, cols), bf),
            pltpu.VMEM((4 * m, reach, chans, cols), bf),
            pltpu.VMEM((6 * m, reach, chans, cols), bf),
            pltpu.VMEM((2 * m, reach, chans, cols), bf),
            pltpu.VMEM((reach, chans, cols), bf),
            pltpu.VMEM((4, reach, chans, cols), f32),
            pltpu.VMEM(((rows + 4) * chans, cols), bf),
            pltpu.VMEM(((rows + 2) * chans, cols), bf),
            pltpu.VMEM((chans, cols), bf),
            pltpu.VMEM((span, chans, cols), bf),
            pltpu.VMEM((span * chans, cols), bf),
            pltpu.VMEM((3 * chans, cols), bf),
            pltpu.VMEM((planes, chans, cols), bf),
            dma((2,)), dma((3 * m - 1,)), dma((1,)), dma((6 * m - 9,)), dma((1,)), dma((1,)), dma((2,)), dma((2,)),
            dma((1,)), dma((1,)), dma((2,)), dma((2,)),
            dma((1,)), dma((4 * m - 4,)), dma((1,)), dma((2 * m,)), dma((1,)),
            pltpu.SemaphoreType.REGULAR((m - 2, 2)),
        ],
        compiler_params=pltpu.CompilerParams(collective_id=0, has_side_effects=True),
    )(*operands)
    return updated.transpose(0, 2, 1)[None]


def fits(voxels):
    n = lax.axis_size("gx")
    sides = lax.axis_size("gy")
    xs, ys, zs, _ = voxels.shape
    return xs == 1 and sides == 2 and n % 2 == 0 and n >= 8 and ys == n * 4 * reach and 2 * ys == zs


def plain_planes(features, row_weights, column_weights, depth_weights, plane_kernels):
    xy_plane = jnp.einsum(
        "xyzc,zc->xyc", features, depth_weights, preferred_element_type=jnp.float32
    ).astype(jnp.bfloat16)
    xz_part = jnp.einsum(
        "xyzc,yc->xzc", features, column_weights, preferred_element_type=jnp.float32
    )
    yz_part = jnp.einsum("xyzc,xc->yzc", features, row_weights, preferred_element_type=jnp.float32)
    xy_out = plane_block(xy_plane, plane_kernels[0], rim_xy)
    xz_plane = lax.psum(xz_part, "gy").astype(jnp.bfloat16)
    xz_out = plane_block(xz_plane, plane_kernels[1], rim_xz)
    yz_plane = lax.psum(yz_part, "gx").astype(jnp.bfloat16)
    yz_out = plane_block(yz_plane, plane_kernels[2], rim_yz)
    return xy_out, xz_out, yz_out


def shards(
    voxels,
    occupancy,
    row_weights,
    column_weights,
    depth_weights,
    plane_kernels,
    expand_weight,
    shrink_weight,
):
    if fits(voxels):
        return fused(
            voxels,
            occupancy,
            row_weights,
            column_weights,
            depth_weights,
            plane_kernels,
            expand_weight,
            shrink_weight,
        )
    features = voxels * occupancy.astype(jnp.bfloat16)[..., None]
    xy_out, xz_out, yz_out = plain_planes(features, row_weights, column_weights, depth_weights, plane_kernels)
    product = xy_out.astype(jnp.float32)[:, :, None, :] * xz_out.astype(jnp.float32)[:, None, :, :]
    product = product * yz_out.astype(jnp.float32)[None, :, :, :]
    mixed = (product_scale * product).astype(jnp.bfloat16)
    hidden = jax.nn.silu(
        jnp.einsum("xyzc,ch->xyzh", mixed, expand_weight, preferred_element_type=jnp.float32)
    ).astype(jnp.bfloat16)
    branch = jnp.einsum("xyzh,hc->xyzc", hidden, shrink_weight, preferred_element_type=jnp.float32)
    return (features.astype(jnp.float32) + branch).astype(jnp.bfloat16)


def solution(mesh):
    in_specs = (
        P(("groups", "gx"), "gy", None, None),
        P(("groups", "gx"), "gy", None),
        P("gx", None),
        P("gy", None),
        P(),
        P(),
        P(),
        P(),
    )
    out_specs = P(("groups", "gx"), "gy", None, None)
    return jax.shard_map(shards, mesh=mesh, in_specs=in_specs, out_specs=out_specs, check_vma=False)
```
